32 devices in a mesh: fsdp: 8 (over z, x), dp: 4 (over y, core).
Axes of the slice: x: 2, y: 2, z: 4, core: 2. Of those that a mesh axis runs over, the one named last changes fastest.
Arguments:
- tokens: bfloat16 [32, 1024, 1152], P(('fsdp', 'dp')), may hold values from -6 to 6
- timesteps: int32 [32], P(('fsdp', 'dp')), may hold values from 0 to 999, as said below
- labels: int32 [32], P(('fsdp', 'dp')), may hold values from 0 to 999
- head_keep: int32 [32, 16], P(('fsdp', 'dp')), may hold values from 0 to 1, as said below
- chan_keep: int32 [32, 4608], P(('fsdp', 'dp')), may hold values from 0 to 1, as said below
- cotangent: bfloat16 [32, 1024, 1152], P(('fsdp', 'dp')), may hold values from -6 to 6
- qkv_weight: bfloat16 [1152, 3456], P('fsdp'), may hold values from -0.1875 to 0.1875
- qv_bias: bfloat16 [2, 1152], P(None, 'fsdp'), may hold values from -3 to 3
- out_weight: bfloat16 [1152, 1152], P('fsdp'), may hold values from -3 to 3
- out_bias: bfloat16 [1152], P('fsdp'), may hold values from -3 to 3
- up_weight: bfloat16 [1152, 4608], P('fsdp'), may hold values from -0.1875 to 0.1875
- up_bias: bfloat16 [4608], P('fsdp'), may hold values from -3 to 3
- down_weight: bfloat16 [4608, 1152], P('fsdp'), may hold values from -0.09375 to 0.09375
- down_bias: bfloat16 [1152], P('fsdp'), may hold values from -3 to 3
- ada_weight: bfloat16 [1152, 6912], P('fsdp'), may hold values from -0.1875 to 0.1875
- ada_bias: bfloat16 [6912], P('fsdp'), may hold values from -3 to 3
- class_table: bfloat16 [1000, 1152], P(None, 'fsdp'), may hold values from -6 to 6
Outputs:
- block_out: bfloat16 [32, 1024, 1152], P(('fsdp', 'dp'))
- tokens_grad: bfloat16 [32, 1024, 1152], P(('fsdp', 'dp'))
- qkv_weight_grad: float32 [1152, 3456], P('fsdp')
- qv_bias_grad: float32 [2, 1152], P(None, 'fsdp')
- out_weight_grad: float32 [1152, 1152], P('fsdp')
- out_bias_grad: float32 [1152], P('fsdp')
- up_weight_grad: float32 [1152, 4608], P('fsdp')
- up_bias_grad: float32 [4608], P('fsdp')
- down_weight_grad: float32 [4608, 1152], P('fsdp')
- down_bias_grad: float32 [1152], P('fsdp')
- ada_weight_grad: float32 [1152, 6912], P('fsdp')
- ada_bias_grad: float32 [6912], P('fsdp')
- class_table_grad: float32 [1000, 1152], P(None, 'fsdp')
The draws below stay inside these ranges and needn't reach their ends.
Inputs may be any that keep to these rules, and one draw needn't show every extreme that they name: timesteps lean toward the noisy end. `head_keep`: each image draws its own keep rate, from a quarter to one, so kept heads differ from image to image. `chan_keep`: each image draws its own keep rate, from a quarter to one, so kept hidden units differ from image to image.
All inputs are finite; a program needn't handle non-finite values.
Results may differ from the reference program's by a relative error of at most 0.02.
The reference program's roundings to bfloat16 on the way count: a program that leaves them out, or rounds other values in their place, can miss the bound.
Values may be sent and summed in bfloat16 or wider, within the bound.
No kernel may reach another device: no remote copies, remote signals or barrier semaphores. Data moves between devices by JAX's collectives and lax.ppermute only.
A program may use at most 384 MiB of HBM per device.

```python
import math
import jax
import jax.numpy as jnp
from jax import lax

D = 1152
FF = 4608
HEADS = 16
CLASSES = 1000
SEQ_LEN = 1024
BATCH = 32


def keep_mask(key, row_count, col_count):
    rate_key, pick_key = jax.random.split(key)
    keep_rate = jax.random.randint(rate_key, (row_count, 1), 16, 65)
    pick_draw = jax.random.randint(pick_key, (row_count, col_count), 0, 64)
    return (pick_draw < keep_rate).astype(jnp.int32)


def draw_head_keep(key, part):
    return keep_mask(jax.random.fold_in(key, 11), BATCH, HEADS)


def draw_chan_keep(key, part):
    return keep_mask(jax.random.fold_in(key, 23), BATCH, FF)


def draw_timesteps(key, part):
    first_key, second_key = jax.random.split(jax.random.fold_in(key, 37))
    first_draw = jax.random.randint(first_key, (BATCH,), 0, 1000)
    second_draw = jax.random.randint(second_key, (BATCH,), 0, 1000)
    return jnp.maximum(first_draw, second_draw).astype(jnp.int32)


def plant(values, stream_key, smallest, largest):
    index_at = [jax.random.randint(jax.random.fold_in(stream_key, axis), (), 0, length) for axis, length in enumerate(values.shape)]
    main_axis = values.shape.index(max(values.shape))
    neighbour = index_at[:main_axis] + [(index_at[main_axis] + 1) % values.shape[main_axis]] + index_at[main_axis + 1:]
    return values.at[tuple(index_at)].set(smallest).at[tuple(neighbour)].set(largest)


def level_of(key, extent, pieces, low, high):
    gain = 1.0
    for axis_at, blocks in pieces:
        heights = jax.random.uniform(jax.random.fold_in(jax.random.fold_in(key, 6), axis_at), (blocks,), jnp.float32, low / len(pieces), high / len(pieces))
        gain = gain * jnp.repeat(jnp.exp(heights), extent[axis_at] // blocks).reshape((-1,) + (1,) * (len(extent) - 1 - axis_at))
    return gain


def scatter_about(own_key, dims, spread, limit, shards=(), kind=jnp.bfloat16):
    entries = spread * jax.random.normal(own_key, dims, jnp.float32)
    if shards:
        entries = entries * level_of(own_key, dims, shards, -0.22, 0.18)
    return jnp.clip(entries, -limit, limit).astype(kind)


def setup_inputs(seed: int = 0) -> dict:
    streams_of = jax.random.split(jax.random.key(seed), 18)
    return {
        "tokens": scatter_about(streams_of[0], (BATCH, SEQ_LEN, D), 1.0, 6.0, ((0, 32),)),
        "timesteps": draw_timesteps(jax.random.fold_in(streams_of[17], 71), 0),
        "labels": plant(jax.random.randint(streams_of[2], (BATCH,), 0, CLASSES), jax.random.fold_in(streams_of[2], 1), 0, CLASSES - 1).astype(jnp.int32),
        "head_keep": draw_head_keep(jax.random.fold_in(streams_of[17], 71), 0),
        "chan_keep": draw_chan_keep(jax.random.fold_in(streams_of[17], 71), 0),
        "cotangent": scatter_about(streams_of[5], (BATCH, SEQ_LEN, D), 1.0, 6.0, ((0, 32),)),
        "qkv_weight": scatter_about(streams_of[6], (D, 3 * D), D ** -0.5, 0.1875, ((0, 8),)),
        "qv_bias": scatter_about(streams_of[7], (2, D), 0.5, 3.0, ((1, 8),)),
        "out_weight": scatter_about(streams_of[8], (D, D), (max(D // 256, 2)) ** -0.5, 3.0, ((0, 8),)),
        "out_bias": scatter_about(streams_of[9], (D,), 0.5, 3.0, ((0, 8),)),
        "up_weight": scatter_about(streams_of[10], (D, FF), D ** -0.5, 0.1875, ((0, 8),)),
        "up_bias": scatter_about(streams_of[11], (FF,), 0.5, 3.0, ((0, 8),)),
        "down_weight": scatter_about(streams_of[12], (FF, D), FF ** -0.5, 0.09375, ((0, 8),)),
        "down_bias": scatter_about(streams_of[13], (D,), 0.5, 3.0, ((0, 8),)),
        "ada_weight": scatter_about(streams_of[14], (D, 6 * D), D ** -0.5, 0.1875, ((0, 8),)),
        "ada_bias": scatter_about(streams_of[15], (6 * D,), 0.5, 3.0, ((0, 8),)),
        "class_table": scatter_about(streams_of[16], (CLASSES, D), 1.0, 6.0, ((1, 8),)),
    }


@jax.custom_vjp
def low(v):
    return lax.optimization_barrier(v.astype(jnp.bfloat16)).astype(jnp.float32)

@jax.custom_vjp
def low_back(v):
    return v

def low_keep(v):
    return (low(v), None)

def low_pass(kept, grad):
    return (grad,)

def back_keep(v):
    return (v, None)

def back_low(kept, grad):
    return (low(grad),)
low.defvjp(low_keep, low_pass)
low_back.defvjp(back_keep, back_low)
HIGHEST = lax.Precision.HIGHEST

def matmul(left, right):
    return jnp.dot(left, right, precision=HIGHEST, preferred_element_type=jnp.float32)

def time_embed(time_steps, model_width):
    half_width = model_width // 2
    frequency = jnp.exp(-math.log(10000.0) * jnp.arange(half_width, dtype=jnp.float32) / half_width)
    angles = time_steps.astype(jnp.float32)[:, None] * frequency[None, :]
    return jnp.concatenate([jnp.cos(angles), jnp.sin(angles)], axis=1)

def layer_norm(values):
    row_mean = lax.optimization_barrier(jnp.mean(values, axis=-1, keepdims=True))
    centred = values - row_mean
    return centred * lax.rsqrt(lax.optimization_barrier(jnp.mean(centred * centred, axis=-1, keepdims=True)) + 1e-06)

def gelu_tanh(values):
    return jax.nn.gelu(values, approximate=True)

def one_sample(params, row_tokens, time_step, label_one, head_mask, chan_mask):
    qkv_weight, qv_bias, out_weight, out_bias, up_weight, up_bias, down_weight, down_bias, ada_weight, ada_bias, class_table = params
    seq_length, model_width = row_tokens.shape
    head_count = head_mask.shape[0]
    head_size = model_width // head_count
    cond_pre = time_embed(jnp.reshape(time_step, (1,)), model_width)[0] + class_table[label_one]
    ada_row = low_back(matmul(low(jax.nn.silu(cond_pre))[None, :], ada_weight)[0] + ada_bias)
    shift_attn, scale_attn, gate_attn, shift_mlp, scale_mlp, gate_mlp = jnp.reshape(ada_row, (6, model_width))
    mod_one = low(layer_norm(row_tokens) * (1.0 + scale_attn) + shift_attn)
    zero_row = jnp.zeros_like(qv_bias[0])
    qkv_bias_row = jnp.concatenate([qv_bias[0], zero_row, qv_bias[1]])
    qkv_rows = low_back(low(matmul(mod_one, qkv_weight) + qkv_bias_row))
    qkv_split = jnp.reshape(qkv_rows, (seq_length, 3, head_count, head_size))
    query_rows = qkv_split[:, 0]
    key_rows = qkv_split[:, 1]
    value_rows = qkv_split[:, 2]
    raw_scores = jnp.einsum('qhd,khd->hqk', query_rows, key_rows, precision=HIGHEST)
    scores = low_back(raw_scores) * head_size ** (-0.5)
    attn_probs = low(jax.nn.softmax(scores, axis=-1))
    attn_raw = jnp.einsum('hqk,khd->qhd', attn_probs, value_rows, precision=HIGHEST)
    attn_low = low_back(low(attn_raw * head_mask[None, :, None]))
    attn_branch = low_back(matmul(jnp.reshape(attn_low, (seq_length, model_width)), out_weight) + out_bias)
    middle = row_tokens + gate_attn * attn_branch
    mod_two = low(layer_norm(middle) * (1.0 + scale_mlp) + shift_mlp)
    pre_act = low_back(matmul(mod_two, up_weight) + up_bias)
    act_low = low(gelu_tanh(pre_act) * chan_mask)
    mlp_branch = low_back(matmul(act_low, down_weight) + down_bias)
    return middle + gate_mlp * mlp_branch

def reference(tokens, timesteps, labels, head_keep, chan_keep, cotangent, qkv_weight, qv_bias, out_weight, out_bias, up_weight, up_bias, down_weight, down_bias, ada_weight, ada_bias, class_table):
    params = (qkv_weight.astype(jnp.float32), qv_bias.astype(jnp.float32), out_weight.astype(jnp.float32), out_bias.astype(jnp.float32), up_weight.astype(jnp.float32), up_bias.astype(jnp.float32), down_weight.astype(jnp.float32), down_bias.astype(jnp.float32), ada_weight.astype(jnp.float32), ada_bias.astype(jnp.float32), class_table.astype(jnp.float32))
    inputs = tokens.astype(jnp.float32)
    head_masks = head_keep.astype(jnp.float32)
    chan_masks = chan_keep.astype(jnp.float32)

    def forward(inputs, params):

        def scan_step(scan_carry, scan_item):
            row_tokens, time_step, label_one, head_mask, chan_mask = scan_item
            return (scan_carry, jax.checkpoint(one_sample)(params, row_tokens, time_step, label_one, head_mask, chan_mask))
        return lax.scan(scan_step, None, (inputs, timesteps, labels, head_masks, chan_masks))[1]
    block_out, pull_back = jax.vjp(forward, inputs, params)
    tokens_grad, param_grads = pull_back(cotangent.astype(jnp.float32))
    return (block_out.astype(jnp.bfloat16), tokens_grad.astype(jnp.bfloat16), param_grads[0], param_grads[1], param_grads[2], param_grads[3], param_grads[4], param_grads[5], param_grads[6], param_grads[7], param_grads[8], param_grads[9], param_grads[10])
```

```python
import functools
import math

import jax
import jax.numpy as jnp
from jax import lax
from jax.experimental import pallas as pl
from jax.experimental.pallas import tpu as pltpu
from jax.sharding import PartitionSpec as P

LOG2E = 1.4426950408889634
ROWS_NT = (((1,), (1,)), ((), ()))
ROWS_NN = (((1,), (0,)), ((), ()))


def matmul(left, right, dims):
    return lax.dot_general(left, right, dims, preferred_element_type=jnp.float32)


def norm_forward(values):
    row_mean = jnp.mean(values, axis=-1, keepdims=True)
    centred = values - row_mean
    inverse = lax.rsqrt(jnp.mean(centred * centred, axis=-1, keepdims=True) + 1e-06)
    return (centred * inverse, inverse)


def norm_backward(gradient, normed, inverse):
    return inverse * (
        gradient
        - jnp.mean(gradient, axis=-1, keepdims=True)
        - normed * jnp.mean(gradient * normed, axis=-1, keepdims=True)
    )


def gelu_tanh(values):
    return jax.nn.gelu(values, approximate=True)


def head_window(head, head_size, width):
    tile = jnp.minimum((head * head_size) // 128, width // 128 - 2)
    base = pl.multiple_of(tile * 128, 128)
    lane = lax.broadcasted_iota(jnp.int32, (1, 256), 1) + (base - head * head_size)
    return base, (lane >= 0) & (lane < head_size)


def as_row(column):
    return jnp.transpose(jnp.broadcast_to(column, (column.shape[0], 128)))[0:1]


def attend_forward_kernel(keep_ref, qkv_ref, out_ref, lse_ref, *, head_size, width, rows):
    head = pl.program_id(0)
    base, mask = head_window(head, head_size, width)
    scale = head_size**-0.5 * LOG2E
    zero = jnp.zeros((), jnp.bfloat16)
    keys = qkv_ref[:, pl.ds(width + base, 256)]
    values = qkv_ref[:, pl.ds(2 * width + base, 256)]
    keep = keep_ref[head].astype(jnp.float32)
    for start in range(0, qkv_ref.shape[0], rows):
        block = (pl.ds(start, rows), pl.ds(base, 256))
        query = jnp.where(mask, qkv_ref[block], zero)
        scores = matmul(query, keys, ROWS_NT)
        top = jnp.max(scores, axis=-1, keepdims=True)
        probs = jnp.exp2((scores - top) * scale)
        total = jnp.sum(probs, axis=-1, keepdims=True)
        mixed = matmul(probs.astype(jnp.bfloat16), values, ROWS_NN)
        mixed = (mixed * (keep / total)).astype(jnp.bfloat16)
        out_ref[block] = jnp.where(mask, mixed, out_ref[block])
        lse_ref[pl.ds(head, 1), pl.ds(start, rows)] = as_row(top * scale + jnp.log2(total))


def attend_backward_kernel(
    keep_ref, qkv_ref, out_ref, grad_ref, lse_ref, dqkv_ref, *, head_size, width, rows
):
    head = pl.program_id(0)
    base, mask = head_window(head, head_size, width)
    scale = head_size**-0.5
    zero = jnp.zeros((), jnp.bfloat16)
    length = qkv_ref.shape[0]
    key_block = (slice(None), pl.ds(width + base, 256))
    value_block = (slice(None), pl.ds(2 * width + base, 256))
    keys = qkv_ref[key_block]
    values = qkv_ref[value_block]
    keys_across = jnp.transpose(keys)
    key_grad = jnp.zeros((length, 256), jnp.float32)
    value_grad = jnp.zeros((length, 256), jnp.float32)
    kept = mask & (keep_ref[head] > 0)
    for start in range(0, length, rows):
        block = (pl.ds(start, rows), pl.ds(base, 256))
        query = jnp.where(mask, qkv_ref[block], zero)
        grad = jnp.where(kept, grad_ref[block], zero)
        row_dot = as_row(
            jnp.sum(
                grad.astype(jnp.float32) * out_ref[block].astype(jnp.float32), axis=-1, keepdims=True
            )
        )
        lse = lse_ref[pl.ds(head, 1), pl.ds(start, rows)]
        probs = jnp.exp2(matmul(keys, query, ROWS_NT) * (scale * LOG2E) - lse)
        score_grad = (probs * (matmul(values, grad, ROWS_NT) - row_dot)).astype(jnp.bfloat16)
        value_grad = value_grad + matmul(probs.astype(jnp.bfloat16), grad, ROWS_NN)
        key_grad = key_grad + matmul(score_grad, query, ROWS_NN)
        query_grad = jnp.transpose(matmul(keys_across, score_grad, ROWS_NN)) * scale
        dqkv_ref[block] = jnp.where(mask, query_grad.astype(jnp.bfloat16), dqkv_ref[block])
    dqkv_ref[key_block] = jnp.where(
        mask, (key_grad * scale).astype(jnp.bfloat16), dqkv_ref[key_block]
    )
    dqkv_ref[value_block] = jnp.where(mask, value_grad.astype(jnp.bfloat16), dqkv_ref[value_block])


def whole(shape):
    return pl.BlockSpec(shape, lambda *_: (0,) * len(shape), pipeline_mode=pl.Buffered(1))


def attend_forward(qkv, keep, rows=512):
    length, triple = qkv.shape
    width, heads = triple // 3, keep.shape[0]
    cells = heads * length * length
    return pl.pallas_call(
        functools.partial(
            attend_forward_kernel, head_size=width // heads, width=width, rows=min(rows, length)
        ),
        grid=(heads,),
        in_specs=[pl.BlockSpec(memory_space=pltpu.SMEM), whole((length, triple))],
        out_specs=[
            pl.BlockSpec((length, width), lambda head: (0, 0)),
            pl.BlockSpec((heads, length), lambda head: (0, 0)),
        ],
        out_shape=[
            jax.ShapeDtypeStruct((length, width), jnp.bfloat16),
            jax.ShapeDtypeStruct((heads, length), jnp.float32),
        ],
        compiler_params=pltpu.CompilerParams(vmem_limit_bytes=48 << 20),
        cost_estimate=pl.CostEstimate(
            flops=cells * 1024, transcendentals=cells, bytes_accessed=length * width * 8
        ),
        name="attend_forward",
    )(keep, qkv)


def attend_backward(qkv, out, grad, lse, keep, rows=256):
    length, triple = qkv.shape
    width, heads = triple // 3, keep.shape[0]
    cells = heads * length * length
    return pl.pallas_call(
        functools.partial(
            attend_backward_kernel, head_size=width // heads, width=width, rows=min(rows, length)
        ),
        grid=(heads,),
        in_specs=[
            pl.BlockSpec(memory_space=pltpu.SMEM),
            whole((length, triple)),
            whole((length, width)),
            whole((length, width)),
            whole((heads, length)),
        ],
        out_specs=pl.BlockSpec((length, triple), lambda head: (0, 0)),
        out_shape=jax.ShapeDtypeStruct((length, triple), jnp.bfloat16),
        compiler_params=pltpu.CompilerParams(vmem_limit_bytes=56 << 20),
        cost_estimate=pl.CostEstimate(
            flops=cells * 2560, transcendentals=cells, bytes_accessed=length * width * 16
        ),
        name="attend_backward",
    )(keep, qkv, out, grad, lse)


def gather_rows(rows, axis, size):
    place = lax.axis_index(axis)
    step = 1
    while step < size:
        other = lax.ppermute(rows, axis, [(i, i ^ step) for i in range(size)])
        high = (place // step) % 2 == 1
        rows = jnp.concatenate([jnp.where(high, other, rows), jnp.where(high, rows, other)], axis=0)
        step *= 2
    return rows


def conditioning(times, labels, table, shard, width):
    class_count, columns = table.shape
    half = width // 2
    column = shard * columns + jnp.arange(columns, dtype=jnp.int32)
    frequency = jnp.exp(-math.log(10000.0) * (column % half).astype(jnp.float32) / half)
    angles = times.astype(jnp.float32)[:, None] * frequency[None, :]
    embed = jnp.where(column[None, :] < half, jnp.cos(angles), jnp.sin(angles))
    picked = labels[:, None] == jnp.arange(class_count, dtype=jnp.int32)[None, :]
    return embed + jnp.dot(
        picked.astype(jnp.bfloat16), table, preferred_element_type=jnp.float32
    )


def own_part(values, shard, size):
    return lax.dynamic_slice_in_dim(values, shard * size, size, axis=values.ndim - 1)


def body(
    shard_count,
    image_count,
    tokens,
    timesteps,
    labels,
    head_keep,
    chan_keep,
    cotangent,
    qkv_weight,
    qv_bias,
    out_weight,
    out_bias,
    up_weight,
    up_bias,
    down_weight,
    down_bias,
    ada_weight,
    ada_bias,
    class_table,
):
    _, length, width = tokens.shape
    hidden = chan_keep.shape[1]
    class_count = class_table.shape[0]
    columns = width // shard_count
    group_count = image_count // shard_count
    shard = lax.axis_index("fsdp")
    bf16, f32 = jnp.bfloat16, jnp.float32

    facts = gather_rows(jnp.stack([timesteps, labels], axis=1), "fsdp", shard_count)
    group_act = jax.nn.silu(
        conditioning(facts[:, 0], facts[:, 1], class_table, shard, width)
    ).astype(bf16)
    partial = jnp.dot(group_act, ada_weight, preferred_element_type=f32)
    bias_row = lax.dynamic_update_slice_in_dim(
        jnp.zeros((6 * width,), f32), ada_bias.astype(f32), shard * ada_bias.shape[0], axis=0
    )
    small = jnp.concatenate([qv_bias.reshape(-1), out_bias, up_bias, down_bias]).astype(f32)
    sent = jnp.concatenate(
        [partial + bias_row, jnp.broadcast_to(small, (shard_count, small.shape[0]))], axis=1
    )
    parts = lax.all_to_all(sent, "fsdp", 0, 0, tiled=True)
    ada_rows = jnp.sum(parts[:, : 6 * width], axis=0).reshape(6, 1, width)
    shift_attn, scale_attn, gate_attn, shift_mlp, scale_mlp, gate_mlp = [ada_rows[i] for i in range(6)]
    small = parts[:, 6 * width :]
    query_bias = small[:, :columns].reshape(-1)
    value_bias = small[:, columns : 2 * columns].reshape(-1)
    out_bias_full = small[:, 2 * columns : 3 * columns].reshape(-1)
    up_end = 3 * columns + up_bias.shape[0]
    up_bias_full = small[:, 3 * columns : up_end].reshape(-1)
    down_bias_full = small[:, up_end:].reshape(-1)

    qkv_full = lax.all_gather(qkv_weight, "fsdp", axis=0, tiled=True)
    out_full = lax.all_gather(out_weight, "fsdp", axis=0, tiled=True)
    up_full = lax.all_gather(up_weight, "fsdp", axis=0, tiled=True)
    down_full = lax.all_gather(down_weight, "fsdp", axis=0, tiled=True)

    inputs = tokens[0].astype(f32)
    normed_one, inverse_one = norm_forward(inputs)
    mod_one = (normed_one * (1.0 + scale_attn) + shift_attn).astype(bf16)
    qkv_bias = jnp.concatenate([query_bias, jnp.zeros((width,), f32), value_bias])
    qkv = (jnp.dot(mod_one, qkv_full, preferred_element_type=f32) + qkv_bias).astype(bf16)
    attn_low, lse = attend_forward(qkv, head_keep[0])
    attn_branch = jnp.dot(attn_low, out_full, preferred_element_type=f32) + out_bias_full
    middle = inputs + gate_attn * attn_branch
    normed_two, inverse_two = norm_forward(middle)
    mod_two = (normed_two * (1.0 + scale_mlp) + shift_mlp).astype(bf16)
    pre_act = jnp.dot(mod_two, up_full, preferred_element_type=f32) + up_bias_full
    chan_mask = chan_keep.astype(f32)
    act_low = (gelu_tanh(pre_act) * chan_mask).astype(bf16)
    mlp_branch = jnp.dot(act_low, down_full, preferred_element_type=f32) + down_bias_full
    block_out = (middle + gate_mlp * mlp_branch).astype(bf16)

    out_grad = cotangent[0].astype(f32)
    gate_mlp_grad = jnp.sum(out_grad * mlp_branch, axis=0)
    branch_grad = (out_grad * gate_mlp).astype(bf16)
    down_bias_g = jnp.sum(branch_grad.astype(f32), axis=0)
    down_weight_g = jnp.einsum("tf,td->fd", act_low, branch_grad, preferred_element_type=f32)
    act_grad = jnp.einsum("td,fd->tf", branch_grad, down_full, preferred_element_type=f32)
    _, gelu_pull = jax.vjp(gelu_tanh, pre_act)
    pre_grad = gelu_pull(act_grad * chan_mask)[0].astype(bf16)
    up_bias_g = jnp.sum(pre_grad.astype(f32), axis=0)
    up_weight_g = jnp.einsum("td,tf->df", mod_two, pre_grad, preferred_element_type=f32)
    mod_two_grad = jnp.einsum("tf,df->td", pre_grad, up_full, preferred_element_type=f32)
    mlp_grads = lax.optimization_barrier(
        (down_weight_g.astype(bf16), up_weight_g.astype(bf16), mod_two_grad)
    )
    down_weight_g, up_weight_g, mod_two_grad = mlp_grads

    def reduce(grad):
        return lax.psum(
            lax.psum_scatter(grad, "fsdp", scatter_dimension=0, tiled=True), "dp"
        ).astype(f32)

    down_shard = reduce(down_weight_g)
    up_shard = reduce(up_weight_g)
    scale_mlp_grad = jnp.sum(mod_two_grad * normed_two, axis=0)
    shift_mlp_grad = jnp.sum(mod_two_grad, axis=0)
    middle_grad = out_grad + norm_backward(
        mod_two_grad * (1.0 + scale_mlp), normed_two, inverse_two
    )
    gate_attn_grad = jnp.sum(middle_grad * attn_branch, axis=0)
    attn_grad = (middle_grad * gate_attn).astype(bf16)
    out_bias_g = jnp.sum(attn_grad.astype(f32), axis=0)
    out_weight_g = jnp.einsum("td,te->de", attn_low, attn_grad, preferred_element_type=f32)
    low_grad = jnp.einsum("te,de->td", attn_grad, out_full, preferred_element_type=f32).astype(bf16)
    out_weight_g, low_grad = lax.optimization_barrier((out_weight_g.astype(bf16), low_grad))
    out_shard = reduce(out_weight_g)
    qkv_grad = attend_backward(qkv, attn_low, low_grad, lse, head_keep[0])
    qkv_weight_g = jnp.einsum("td,te->de", mod_one, qkv_grad, preferred_element_type=f32)
    qkv_weight_g, qkv_grad = lax.optimization_barrier((qkv_weight_g.astype(bf16), qkv_grad))
    qkv_shard = reduce(qkv_weight_g)
    bias_sums = jnp.sum(qkv_grad.astype(f32), axis=0)
    mod_one_grad = jnp.einsum("te,de->td", qkv_grad, qkv_full, preferred_element_type=f32)
    scale_attn_grad = jnp.sum(mod_one_grad * normed_one, axis=0)
    shift_attn_grad = jnp.sum(mod_one_grad, axis=0)
    tokens_grad = (
        middle_grad + norm_backward(mod_one_grad * (1.0 + scale_attn), normed_one, inverse_one)
    ).astype(bf16)

    row = jnp.concatenate(
        [
            shift_attn_grad,
            scale_attn_grad,
            gate_attn_grad,
            shift_mlp_grad,
            scale_mlp_grad,
            gate_mlp_grad,
            bias_sums[:width],
            bias_sums[2 * width :],
            out_bias_g,
            up_bias_g,
            down_bias_g,
        ]
    ).astype(bf16)[None]
    rows = gather_rows(gather_rows(row, "fsdp", shard_count), "dp", group_count)
    all_facts = gather_rows(facts, "dp", group_count)
    cond = conditioning(all_facts[:, 0], all_facts[:, 1], class_table, shard, width)
    cond_act, silu_pull = jax.vjp(jax.nn.silu, cond)
    ada_grad = rows[:, : 6 * width]
    ada_weight_g = jnp.einsum(
        "sd,se->de", cond_act.astype(bf16), ada_grad, preferred_element_type=f32
    )
    cond_act_grad = jnp.einsum("se,de->sd", ada_grad, ada_weight, preferred_element_type=f32)
    cond_grad = silu_pull(cond_act_grad)[0]
    picked = all_facts[:, 1][:, None] == jnp.arange(class_count, dtype=jnp.int32)[None, :]
    table_g = jnp.einsum(
        "sc,sd->cd", picked.astype(f32), cond_grad, precision=lax.Precision.HIGHEST
    )
    sums = jnp.sum(rows.astype(f32), axis=0)
    ada_bias_g = own_part(sums[: 6 * width], shard, ada_bias.shape[0])
    qv_bias_g = own_part(sums[6 * width : 8 * width].reshape(2, width), shard, columns)
    out_bias_g = own_part(sums[8 * width : 9 * width], shard, columns)
    up_bias_g = own_part(sums[9 * width : 9 * width + hidden], shard, up_bias.shape[0])
    down_bias_g = own_part(sums[9 * width + hidden :], shard, columns)
    return (
        block_out[None],
        tokens_grad[None],
        qkv_shard,
        qv_bias_g,
        out_shard,
        out_bias_g,
        up_shard,
        up_bias_g,
        down_shard,
        down_bias_g,
        ada_weight_g,
        ada_bias_g,
        table_g,
    )


def solution(mesh):
    shard_count = mesh.shape["fsdp"]
    image_count = shard_count * mesh.shape["dp"]
    images = ("fsdp", "dp")
    return jax.shard_map(
        functools.partial(body, shard_count, image_count),
        mesh=mesh,
        in_specs=(
            P(images, None, None),
            P(images),
            P(images),
            P(images, None),
            P(images, None),
            P(images, None, None),
            P("fsdp", None),
            P(None, "fsdp"),
            P("fsdp", None),
            P("fsdp"),
            P("fsdp", None),
            P("fsdp"),
            P("fsdp", None),
            P("fsdp"),
            P("fsdp", None),
            P("fsdp"),
            P(None, "fsdp"),
        ),
        out_specs=(
            P(images, None, None),
            P(images, None, None),
            P("fsdp", None),
            P(None, "fsdp"),
            P("fsdp", None),
            P("fsdp"),
            P("fsdp", None),
            P("fsdp"),
            P("fsdp", None),
            P("fsdp"),
            P("fsdp", None),
            P("fsdp"),
            P(None, "fsdp"),
        ),
        check_vma=False,
    )
```

```python
import functools
import math

import jax
import jax.numpy as jnp
from jax import lax
from jax.experimental import pallas as pl
from jax.experimental.pallas import tpu as pltpu
from jax.sharding import PartitionSpec as P

LOG2E = 1.4426950408889634
ROWS_NT = (((1,), (1,)), ((), ()))
ROWS_NN = (((1,), (0,)), ((), ()))


def matmul(left, right, dims):
    return lax.dot_general(left, right, dims, preferred_element_type=jnp.float32)


def norm_forward(values):
    row_mean = jnp.mean(values, axis=-1, keepdims=True)
    centred = values - row_mean
    inverse = lax.rsqrt(jnp.mean(centred * centred, axis=-1, keepdims=True) + 1e-06)
    return (centred * inverse, inverse)


def norm_backward(gradient, normed, inverse):
    return inverse * (
        gradient
        - jnp.mean(gradient, axis=-1, keepdims=True)
        - normed * jnp.mean(gradient * normed, axis=-1, keepdims=True)
    )


def head_window(head, head_size, width):
    tile = jnp.minimum((head * head_size) // 128, width // 128 - 2)
    base = pl.multiple_of(tile * 128, 128)
    lane = lax.broadcasted_iota(jnp.int32, (1, 256), 1) + (base - head * head_size)
    return base, (lane >= 0) & (lane < head_size)


def as_row(column):
    return jnp.transpose(jnp.broadcast_to(column, (column.shape[0], 128)))[0:1]


def attend_forward_kernel(
    keep_ref, query_ref, key_ref, value_ref, out_ref, lse_ref, *, head_size, width, rows
):
    query_ref, key_ref, value_ref = query_ref.at[0], key_ref.at[0], value_ref.at[0]
    head = pl.program_id(0)
    base, mask = head_window(head, head_size, width)
    scale = head_size**-0.5 * LOG2E
    zero = jnp.zeros((), jnp.bfloat16)
    window = (slice(None), pl.ds(base, 256))
    keys = key_ref[window]
    values = value_ref[window]
    keep = keep_ref[head].astype(jnp.float32)
    for start in range(0, query_ref.shape[0], rows):
        block = (pl.ds(start, rows), pl.ds(base, 256))
        query = jnp.where(mask, query_ref[block], zero)
        scores = matmul(query, keys, ROWS_NT)
        top = jnp.max(scores, axis=-1, keepdims=True)
        probs = jnp.exp2((scores - top) * scale)
        total = jnp.sum(probs, axis=-1, keepdims=True)
        mixed = matmul(probs.astype(jnp.bfloat16), values, ROWS_NN)
        mixed = (mixed * (keep / total)).astype(jnp.bfloat16)
        out_ref[block] = jnp.where(mask, mixed, out_ref[block])
        lse_ref[pl.ds(head, 1), pl.ds(start, rows)] = as_row(top * scale + jnp.log2(total))


def attend_backward_kernel(
    keep_ref,
    query_ref,
    key_ref,
    value_ref,
    out_ref,
    grad_ref,
    lse_ref,
    grads_ref,
    *,
    head_size,
    width,
    rows,
):
    query_ref, key_ref, value_ref = query_ref.at[0], key_ref.at[0], value_ref.at[0]
    dquery_ref, dkey_ref, dvalue_ref = grads_ref.at[0], grads_ref.at[1], grads_ref.at[2]
    head = pl.program_id(0)
    base, mask = head_window(head, head_size, width)
    scale = head_size**-0.5
    zero = jnp.zeros((), jnp.bfloat16)
    length = query_ref.shape[0]
    window = (slice(None), pl.ds(base, 256))
    keys = key_ref[window]
    values = value_ref[window]
    keys_across = jnp.transpose(keys)
    key_grad = jnp.zeros((length, 256), jnp.float32)
    value_grad = jnp.zeros((length, 256), jnp.float32)
    kept = mask & (keep_ref[head] > 0)
    for start in range(0, length, rows):
        block = (pl.ds(start, rows), pl.ds(base, 256))
        query = jnp.where(mask, query_ref[block], zero)
        grad = jnp.where(kept, grad_ref[block], zero)
        row_dot = as_row(
            jnp.sum(
                grad.astype(jnp.float32) * out_ref[block].astype(jnp.float32), axis=-1, keepdims=True
            )
        )
        lse = lse_ref[pl.ds(head, 1), pl.ds(start, rows)]
        probs = jnp.exp2(matmul(keys, query, ROWS_NT) * (scale * LOG2E) - lse)
        score_grad = (probs * (matmul(values, grad, ROWS_NT) - row_dot)).astype(jnp.bfloat16)
        value_grad = value_grad + matmul(probs.astype(jnp.bfloat16), grad, ROWS_NN)
        key_grad = key_grad + matmul(score_grad, query, ROWS_NN)
        query_grad = jnp.transpose(matmul(keys_across, score_grad, ROWS_NN)) * scale
        dquery_ref[block] = jnp.where(mask, query_grad.astype(jnp.bfloat16), dquery_ref[block])
    dkey_ref[window] = jnp.where(mask, (key_grad * scale).astype(jnp.bfloat16), dkey_ref[window])
    dvalue_ref[window] = jnp.where(mask, value_grad.astype(jnp.bfloat16), dvalue_ref[window])


def whole(shape):
    return pl.BlockSpec(shape, lambda *_: (0,) * len(shape), pipeline_mode=pl.Buffered(1))


def one_of(index, length, width):
    return pl.BlockSpec(
        (1, length, width), lambda head: (index, 0, 0), pipeline_mode=pl.Buffered(1)
    )


def attend_forward(qkv, keep, rows=512):
    _, length, width = qkv.shape
    heads = keep.shape[0]
    cells = heads * length * length
    return pl.pallas_call(
        functools.partial(
            attend_forward_kernel, head_size=width // heads, width=width, rows=min(rows, length)
        ),
        grid=(heads,),
        in_specs=[pl.BlockSpec(memory_space=pltpu.SMEM)]
        + [one_of(i, length, width) for i in range(3)],
        out_specs=[
            pl.BlockSpec((length, width), lambda head: (0, 0)),
            pl.BlockSpec((heads, length), lambda head: (0, 0)),
        ],
        out_shape=[
            jax.ShapeDtypeStruct((length, width), jnp.bfloat16),
            jax.ShapeDtypeStruct((heads, length), jnp.float32),
        ],
        compiler_params=pltpu.CompilerParams(vmem_limit_bytes=48 << 20),
        cost_estimate=pl.CostEstimate(
            flops=cells * 1024, transcendentals=cells, bytes_accessed=length * width * 8
        ),
        name="attend_forward",
    )(keep, qkv, qkv, qkv)


def attend_backward(qkv, out, grad, lse, keep, rows=256):
    _, length, width = qkv.shape
    heads = keep.shape[0]
    cells = heads * length * length
    return pl.pallas_call(
        functools.partial(
            attend_backward_kernel, head_size=width // heads, width=width, rows=min(rows, length)
        ),
        grid=(heads,),
        in_specs=[pl.BlockSpec(memory_space=pltpu.SMEM)]
        + [one_of(i, length, width) for i in range(3)]
        + [whole((length, width))] * 2
        + [whole((heads, length))],
        out_specs=pl.BlockSpec((3, length, width), lambda head: (0, 0, 0)),
        out_shape=jax.ShapeDtypeStruct((3, length, width), jnp.bfloat16),
        compiler_params=pltpu.CompilerParams(vmem_limit_bytes=56 << 20),
        cost_estimate=pl.CostEstimate(
            flops=cells * 2560, transcendentals=cells, bytes_accessed=length * width * 16
        ),
        name="attend_backward",
    )(keep, qkv, qkv, qkv, out, grad, lse)


ROWS_TN = (((0,), (0,)), ((), ()))
ANY = pl.BlockSpec(memory_space=pl.ANY)


def square_copies(place, sets, r, target, sem):
    part = jnp.bitwise_xor(place[2], r)
    if len(sets[0]) == 1:
        return [pltpu.make_async_copy(sets[0][0].at[part], target, sem)]
    copies, column = [], 0
    for refs in sets:
        _, rows, columns = refs[0].shape
        for x_r in range(2):
            for z_r in range(4):
                shard = (place[0] + z_r) % 4 * 2 + (place[1] + x_r) % 2
                block = (pl.ds(pl.multiple_of(shard * rows, 16), rows), pl.ds(column, columns))
                source = refs[2 * r + x_r].at[z_r]
                copies.append(pltpu.make_async_copy(source, target.at[block], sem))
        column += columns
    return copies


def strip_copies(place, refs, chunk, target, sem):
    if len(refs) == 1:
        return [pltpu.make_async_copy(refs[0].at[chunk], target, sem)]
    rows = refs[0].shape[2]
    z_r = (chunk + 4 - place[0]) % 4
    copies = []
    for core_r in range(2):
        for y in range(2):
            part = 2 * y + (place[2] + core_r) % 2
            for x_r in range(2):
                start = (place[1] + x_r) % 2 * (4 * rows) + part * rows
                block = target.at[pl.ds(pl.multiple_of(start, 16), rows)]
                source = refs[2 * core_r + x_r].at[z_r, y]
                copies.append(pltpu.make_async_copy(source, block, sem))
    return copies


def square_stores(place, outs, r, source, sem):
    part = jnp.bitwise_xor(place[2], r)
    if len(outs) == 1:
        return [pltpu.make_async_copy(source, outs[0].at[part], sem)]
    copies, column = [], 0
    for pair in range(0, len(outs), 2):
        out = outs[pair + r % 2]
        rows, columns = out.shape[3:]
        for shard in range(8):
            x_r, z_r = (place[1] + shard % 2) % 2, (shard // 2 + 4 - place[0]) % 4
            block = source.at[pl.ds(shard * rows, rows), pl.ds(column, columns)]
            copies.append(pltpu.make_async_copy(block, out.at[r // 2, x_r, z_r], sem))
        column += columns
    return copies


def strip_stores(place, outs, chunk, source, sem):
    if len(outs) == 1:
        return [pltpu.make_async_copy(source, outs[0].at[chunk], sem)]
    rows = outs[0].shape[3]
    z_r = (chunk + 4 - place[0]) % 4
    copies = []
    for r in range(4):
        part = jnp.bitwise_xor(place[2], r)
        for x in range(2):
            block = source.at[pl.ds(pl.multiple_of(x * (4 * rows) + part * rows, 16), rows)]
            x_r = (place[1] + x) % 2
            copies.append(pltpu.make_async_copy(block, outs[r % 2].at[r // 2, x_r, z_r], sem))
    return copies


def in_sets(refs, sets):
    refs, found = list(refs), []
    for entry in sets:
        found.append(refs[: len(entry)])
        refs = refs[len(entry) :]
    return found


def flat(sets):
    return [array for entry in sets for array in entry]


def start_all(copies):
    for copy in copies:
        copy.start()


def wait_all(copies):
    for copy in copies:
        copy.wait()


def for_each(step, action):
    for r in range(4):

        @pl.when(step == r)
        def _(r=r):
            action(r)


def fetch_squares(place, sets, step, held, sems):
    @pl.when(step == 0)
    def _():
        start_all(square_copies(place, sets, 0, held.at[0], sems.at[0]))

    for_each(
        step + 1,
        lambda r: start_all(square_copies(place, sets, r, held.at[r % 2], sems.at[r % 2])),
    )
    for_each(
        step, lambda r: wait_all(square_copies(place, sets, r, held.at[r % 2], sems.at[r % 2]))
    )


def tiles(length, rows=256):
    return [pl.ds(start, min(rows, length)) for start in range(0, length, min(rows, length))]


def prepare_kernel(tokens_ref, cotangent_ref, rows_ref, mod_ref, across_ref, grad_ref, sum_ref):
    normed, _ = norm_forward(tokens_ref[...].astype(jnp.float32))
    mod = normed * (1.0 + row_of(rows_ref, SCALE_ATTN)) + row_of(rows_ref, SHIFT_ATTN)
    mod_ref[...] = mod.astype(jnp.bfloat16)
    across_ref[...] = jnp.transpose(mod).astype(jnp.bfloat16)
    grad = (cotangent_ref[...].astype(jnp.float32) * row_of(rows_ref, GATE_MLP)).astype(jnp.bfloat16)
    grad_ref[...] = grad

    @pl.when(pl.program_id(0) == 0)
    def _():
        sum_ref[...] = jnp.zeros_like(sum_ref)

    sum_ref[0:1] += jnp.sum(grad.astype(jnp.float32), axis=0, keepdims=True)


def prepare(tokens, cotangent, rows, tile=256):
    length, width = tokens.shape
    tile = min(tile, length)
    by_rows = pl.BlockSpec((tile, width), lambda step: (step, 0))
    fixed = pl.BlockSpec((8, width), lambda step: (0, 0))
    return pl.pallas_call(
        prepare_kernel,
        grid=(length // tile,),
        in_specs=[by_rows, by_rows, fixed],
        out_specs=[by_rows, pl.BlockSpec((width, tile), lambda step: (0, step)), by_rows, fixed],
        out_shape=[
            jax.ShapeDtypeStruct((length, width), jnp.bfloat16),
            jax.ShapeDtypeStruct((width, length), jnp.bfloat16),
            jax.ShapeDtypeStruct((length, width), jnp.bfloat16),
            jax.ShapeDtypeStruct((8, width), jnp.float32),
        ],
        compiler_params=vmem_params(),
        cost_estimate=cost(20 * length * width, 10 * length * width),
        name="prepare",
    )(tokens, cotangent, rows)


def project_kernel(place, mod_ref, bias_ref, *rest, sets):
    *refs, out_ref, held, sems = rest
    step = pl.program_id(0)
    fetch_squares(place, in_sets(refs, sets), step, held, sems)
    part = jnp.bitwise_xor(place[2], step)

    @pl.when(part < 3)
    def _():
        weight = held[step % 2]
        bias = bias_ref[pl.ds(part, 1)]
        for tile in tiles(mod_ref.shape[0]):
            out_ref[0, tile] = (matmul(mod_ref[tile], weight, ROWS_NN) + bias).astype(jnp.bfloat16)


def vmem_params(mebibytes=56):
    return pltpu.CompilerParams(
        vmem_limit_bytes=mebibytes << 20, dimension_semantics=("arbitrary",)
    )


def cost(flops, moved):
    return pl.CostEstimate(flops=int(flops), transcendentals=0, bytes_accessed=int(moved))


def project(place, mod, bias, squares):
    length, width = mod.shape
    return pl.pallas_call(
        functools.partial(project_kernel, sets=squares),
        grid_spec=pltpu.PrefetchScalarGridSpec(
            num_scalar_prefetch=1,
            grid=(4,),
            in_specs=[
                pl.BlockSpec((length, width), lambda step, place: (0, 0)),
                pl.BlockSpec(bias.shape, lambda step, place: (0, 0)),
            ]
            + [ANY] * len(flat(squares)),
            out_specs=pl.BlockSpec(
                (1, length, width), lambda step, place: (jnp.bitwise_xor(place[2], step), 0, 0)
            ),
            scratch_shapes=[
                pltpu.VMEM((2, width, width), jnp.bfloat16),
                pltpu.SemaphoreType.DMA((2,)),
            ],
        ),
        out_shape=jax.ShapeDtypeStruct((4, length, width), jnp.bfloat16),
        compiler_params=vmem_params(),
        cost_estimate=cost(6 * length * width * width, 14 * length * width),
        name="project",
    )(place, mod, bias, *flat(squares))


def fetch_part(place, sets, wanted, target, sem):
    part = jnp.bitwise_xor(place[2], wanted)
    for_each(part, lambda r: start_all(square_copies(place, sets, r, target, sem)))
    for_each(part, lambda r: wait_all(square_copies(place, sets, r, target, sem)))


def row_of(rows_ref, index):
    return rows_ref[index : index + 1]


SHIFT_ATTN, SCALE_ATTN, GATE_ATTN, SHIFT_MLP, SCALE_MLP, GATE_MLP, OUT_BIAS, DOWN_BIAS = range(8)


def after_attention_kernel(place, low_ref, tokens_ref, rows_ref, *rest, sets):
    *refs, branch_ref, middle_ref, mod_ref, across_ref, weight, sem = rest

    @pl.when(pl.program_id(0) == 0)
    def _():
        fetch_part(place, in_sets(refs, sets), 3, weight, sem)

    branch = matmul(low_ref[...], weight[...], ROWS_NN) + row_of(rows_ref, OUT_BIAS)
    middle = tokens_ref[...].astype(jnp.float32) + row_of(rows_ref, GATE_ATTN) * branch
    normed, _ = norm_forward(middle)
    mod = normed * (1.0 + row_of(rows_ref, SCALE_MLP)) + row_of(rows_ref, SHIFT_MLP)
    branch_ref[...] = branch
    middle_ref[...] = middle
    mod_ref[...] = mod.astype(jnp.bfloat16)
    across_ref[...] = jnp.transpose(mod).astype(jnp.bfloat16)


def after_attention(place, low, tokens, rows, squares, tile=256):
    length, width = low.shape
    tile = min(tile, length)
    by_rows = pl.BlockSpec((tile, width), lambda step, place: (step, 0))
    return pl.pallas_call(
        functools.partial(after_attention_kernel, sets=squares),
        grid_spec=pltpu.PrefetchScalarGridSpec(
            num_scalar_prefetch=1,
            grid=(length // tile,),
            in_specs=[by_rows, by_rows, pl.BlockSpec(rows.shape, lambda step, place: (0, 0))]
            + [ANY] * len(flat(squares)),
            out_specs=[by_rows] * 3 + [pl.BlockSpec((width, tile), lambda step, place: (0, step))],
            scratch_shapes=[pltpu.VMEM((width, width), jnp.bfloat16), pltpu.SemaphoreType.DMA],
        ),
        out_shape=[
            jax.ShapeDtypeStruct((length, width), jnp.float32),
            jax.ShapeDtypeStruct((length, width), jnp.float32),
            jax.ShapeDtypeStruct((length, width), jnp.bfloat16),
            jax.ShapeDtypeStruct((width, length), jnp.bfloat16),
        ],
        compiler_params=vmem_params(),
        cost_estimate=cost(2 * length * width * width, 18 * length * width),
        name="after_attention",
    )(place, low, tokens, rows, *flat(squares))


ROOT = 0.7978845608028654


def gelu_and_slope(values):
    square = values * values
    bend = jnp.tanh(values * (ROOT + (ROOT * 0.044715) * square))
    half = 0.5 + 0.5 * bend
    slope = half + (0.5 * values) * (1.0 - bend * bend) * (ROOT + (3 * 0.044715 * ROOT) * square)
    return values * half, slope


def mlp_kernel(place, mod_ref, across_ref, grad_ref, bias_ref, keep_ref, *rest, ups, downs):
    count = len(flat(ups)) + downs
    refs, rest = rest[:count], rest[count:]
    up_sets, down_refs = in_sets(refs, ups), refs[-downs:]
    branch_ref, dmod_ref, dbias_ref = rest[:3]
    *stores, act, dpre, up, down, up_out, down_out, in_sems, out_sems = rest[3:]
    up_stores, down_stores = stores[: len(stores) // 2], stores[len(stores) // 2 :]
    step = pl.program_id(0)
    length = mod_ref.shape[0]

    def chunk_of(r):
        return jnp.bitwise_xor(place[2], r)

    def fetch(r):
        slot = r % 2
        return square_copies(place, up_sets, r, up.at[slot], in_sems.at[slot, 0]) + strip_copies(
            place, down_refs, chunk_of(r), down.at[slot], in_sems.at[slot, 1]
        )

    @pl.when(step == 0)
    def _():
        start_all(fetch(0))
        branch_ref[...] = jnp.zeros_like(branch_ref)
        dmod_ref[...] = jnp.zeros_like(dmod_ref)

    for_each(step + 1, lambda r: start_all(fetch(r)))
    for_each(step, lambda r: wait_all(fetch(r)))
    chunk = chunk_of(step)
    slot = step % 2
    bias = bias_ref[pl.ds(chunk, 1)]
    keep = keep_ref[pl.ds(chunk, 1)]
    total = jnp.zeros_like(bias)
    for tile in tiles(length):
        gelu, slope = gelu_and_slope(matmul(mod_ref[tile], up[slot], ROWS_NN) + bias)
        act[tile] = (gelu * keep).astype(jnp.bfloat16)
        back = matmul(grad_ref[tile], down[slot], ROWS_NT)
        low = (slope * keep * back).astype(jnp.bfloat16)
        dpre[tile] = low
        total = total + jnp.sum(low.astype(jnp.float32), axis=0, keepdims=True)
        branch_ref[tile] += matmul(act[tile], down[slot], ROWS_NN)
        dmod_ref[tile] += matmul(low, up[slot], ROWS_NT)
    dbias_ref[pl.ds(chunk, 1)] = total

    def leave(r):
        return square_stores(place, up_stores, r, up_out, out_sems.at[0]), strip_stores(
            place, down_stores, chunk_of(r), down_out, out_sems.at[1]
        )

    for_each(step - 1, lambda r: wait_all(leave(r)[0]))
    up_out[...] = matmul(across_ref[...], dpre[...], ROWS_NN).astype(jnp.bfloat16)
    for_each(step, lambda r: start_all(leave(r)[0]))
    for_each(step - 1, lambda r: wait_all(leave(r)[1]))
    down_out[...] = matmul(act[...], grad_ref[...], ROWS_TN).astype(jnp.bfloat16)
    for_each(step, lambda r: start_all(leave(r)[1]))

    @pl.when(step == 3)
    def _():
        wait_all(leave(3)[0])
        wait_all(leave(3)[1])


def gradient_shapes(paired, rows, columns):
    if paired:
        return [
            jax.ShapeDtypeStruct((2, 2, 4, rows, count), jnp.bfloat16)
            for count in columns
            for _ in range(2)
        ]
    return [jax.ShapeDtypeStruct((4, sum(columns), sum(columns)), jnp.bfloat16)]


def mlp(place, mod, across, grad, bias, keep, ups, downs, block_rows):
    length, width = mod.shape
    stores = gradient_shapes(len(downs) > 1, block_rows, [width])
    quarter = jax.ShapeDtypeStruct((4, width), jnp.float32)
    table = pl.BlockSpec((4, width), lambda step, place: (0, 0))
    held = pl.BlockSpec((length, width), lambda step, place: (0, 0), pipeline_mode=pl.Buffered(1))
    square = pltpu.VMEM((width, width), jnp.bfloat16)
    pair = pltpu.VMEM((2, width, width), jnp.bfloat16)
    tall = pltpu.VMEM((length, width), jnp.bfloat16)
    wide = pl.BlockSpec((length, width), lambda step, place: (0, 0))
    return pl.pallas_call(
        functools.partial(mlp_kernel, ups=ups, downs=len(downs)),
        grid_spec=pltpu.PrefetchScalarGridSpec(
            num_scalar_prefetch=1,
            grid=(4,),
            in_specs=[
                held,
                pl.BlockSpec((width, length), lambda step, place: (0, 0), pipeline_mode=pl.Buffered(1)),
                held,
                table,
                table,
            ]
            + [ANY] * (len(flat(ups)) + len(downs)),
            out_specs=[wide, wide, table] + [ANY] * (2 * len(stores)),
            scratch_shapes=[
                tall,
                tall,
                pair,
                pair,
                square,
                square,
                pltpu.SemaphoreType.DMA((2, 2)),
                pltpu.SemaphoreType.DMA((2,)),
            ],
        ),
        out_shape=[jax.ShapeDtypeStruct((length, width), jnp.float32)] * 2
        + [quarter]
        + stores
        + stores,
        compiler_params=vmem_params(60),
        cost_estimate=cost(48 * length * width * width, 32 * width * width),
        name="mlp",
    )(place, mod, across, grad, bias, keep, *flat(ups), *downs)


def after_mlp_kernel(
    place, mlp_ref, dmod_ref, middle_ref, branch_ref, cotangent_ref, low_ref, rows_ref, *rest, sets
):
    *refs, out_ref, dmiddle_ref, dlow_ref, sums_ref, dweight_ref, weight, dbranch, staged, sems = rest
    step = pl.program_id(0)
    tile = out_ref.shape[0]

    @pl.when(step == 0)
    def _():
        fetch_part(place, in_sets(refs, sets), 3, weight, sems.at[0])
        sums_ref[...] = jnp.zeros_like(sums_ref)

    middle = middle_ref[...]
    grad = cotangent_ref[...].astype(jnp.float32)
    mlp_branch = mlp_ref[...] + row_of(rows_ref, DOWN_BIAS)
    out_ref[...] = (middle + row_of(rows_ref, GATE_MLP) * mlp_branch).astype(jnp.bfloat16)
    normed, inverse = norm_forward(middle)
    dmod = dmod_ref[...]
    dmiddle = grad + norm_backward(dmod * (1.0 + row_of(rows_ref, SCALE_MLP)), normed, inverse)
    dmiddle_ref[...] = dmiddle
    low = (dmiddle * row_of(rows_ref, GATE_ATTN)).astype(jnp.bfloat16)
    dbranch[pl.ds(pl.multiple_of(step * tile, tile), tile)] = low
    dlow_ref[...] = matmul(low, weight[...], ROWS_NT).astype(jnp.bfloat16)

    def add(index, values):
        sums_ref[index : index + 1] += jnp.sum(values, axis=0, keepdims=True)

    add(0, grad * mlp_branch)
    add(1, dmod * normed)
    add(2, dmod)
    add(3, dmiddle * branch_ref[...])
    add(4, low.astype(jnp.float32))

    @pl.when(step == pl.num_programs(0) - 1)
    def _():
        staged[...] = matmul(low_ref[...], dbranch[...], ROWS_TN).astype(jnp.bfloat16)
        if len(dweight_ref.shape) == 2:
            copies = [pltpu.make_async_copy(staged, dweight_ref, sems.at[1])]
        else:
            rows = dweight_ref.shape[2]
            copies = []
            for shard in range(8):
                x_r, z_r = (place[1] + shard % 2) % 2, (shard // 2 + 4 - place[0]) % 4
                block = staged.at[pl.ds(shard * rows, rows)]
                copies.append(pltpu.make_async_copy(block, dweight_ref.at[x_r, z_r], sems.at[1]))
        start_all(copies)
        wait_all(copies)


def after_mlp(place, branch_mlp, dmod, middle, branch, cotangent, low, rows, squares, block_rows, tile=256):
    length, width = low.shape
    tile = min(tile, length)
    by_rows = pl.BlockSpec((tile, width), lambda step, place: (step, 0))
    fixed = lambda shape: pl.BlockSpec(shape, lambda step, place: (0, 0))
    wgrad = (2, 4, block_rows, width) if len(squares[0]) > 1 else (width, width)
    return pl.pallas_call(
        functools.partial(after_mlp_kernel, sets=squares),
        grid_spec=pltpu.PrefetchScalarGridSpec(
            num_scalar_prefetch=1,
            grid=(length // tile,),
            in_specs=[by_rows] * 5 + [fixed((length, width)), fixed(rows.shape)] + [ANY] * len(flat(squares)),
            out_specs=[by_rows] * 3 + [fixed((8, width)), ANY],
            scratch_shapes=[
                pltpu.VMEM((width, width), jnp.bfloat16),
                pltpu.VMEM((length, width), jnp.bfloat16),
                pltpu.VMEM((width, width), jnp.bfloat16),
                pltpu.SemaphoreType.DMA((2,)),
            ],
        ),
        out_shape=[
            jax.ShapeDtypeStruct((length, width), jnp.bfloat16),
            jax.ShapeDtypeStruct((length, width), jnp.float32),
            jax.ShapeDtypeStruct((length, width), jnp.bfloat16),
            jax.ShapeDtypeStruct((8, width), jnp.float32),
            jax.ShapeDtypeStruct(wgrad, jnp.bfloat16),
        ],
        compiler_params=vmem_params(),
        cost_estimate=cost(4 * length * width * width, 30 * length * width),
        name="after_mlp",
    )(place, branch_mlp, dmod, middle, branch, cotangent, low, rows, *flat(squares))


def square_grads_kernel(place, across_ref, grads_ref, out_grad_ref, *rest):
    *stores, sums_ref, staged, sems = rest
    step = pl.program_id(0)
    part = jnp.bitwise_xor(place[2], step)

    def leave(r):
        return square_stores(place, stores, r, staged.at[r % 2], sems.at[r % 2])

    def pass_on(r):
        if len(stores) == 1:
            return [pltpu.make_async_copy(out_grad_ref, stores[0].at[3], sems.at[r % 2])]
        copies, column = [], 0
        for pair in range(0, len(stores), 2):
            out = stores[pair + r % 2]
            columns = out.shape[4]
            source = out_grad_ref.at[:, :, :, pl.ds(column, columns)]
            copies.append(pltpu.make_async_copy(source, out.at[r // 2], sems.at[r % 2]))
            column += columns
        return copies

    def wait(r):
        wait_all(pass_on(r))

    for_each(step - 2, wait)

    @pl.when(part < 3)
    def _():
        grads = grads_ref[0]
        staged[step % 2] = matmul(across_ref[...], grads, ROWS_NN).astype(jnp.bfloat16)
        sums_ref[pl.ds(part, 1)] = jnp.sum(grads.astype(jnp.float32), axis=0, keepdims=True)
        for_each(step, lambda r: start_all(leave(r)))

    @pl.when(part == 3)
    def _():
        for_each(step, lambda r: start_all(pass_on(r)))

    @pl.when(step == 3)
    def _():
        wait(2)
        wait(3)


def square_grads(place, across, grads, out_grad, block_rows, columns):
    width, length = across.shape
    paired = len(out_grad.shape) > 2
    stores = gradient_shapes(paired, block_rows, columns)
    return pl.pallas_call(
        square_grads_kernel,
        grid_spec=pltpu.PrefetchScalarGridSpec(
            num_scalar_prefetch=1,
            grid=(4,),
            in_specs=[
                pl.BlockSpec((width, length), lambda step, place: (0, 0)),
                pl.BlockSpec(
                    (1, length, width),
                    lambda step, place: (jnp.minimum(jnp.bitwise_xor(place[2], step), 2), 0, 0),
                ),
                pl.BlockSpec(
                    out_grad.shape,
                    lambda step, place: (0,) * len(out_grad.shape),
                    pipeline_mode=pl.Buffered(1),
                ),
            ],
            out_specs=[ANY] * len(stores) + [pl.BlockSpec((4, width), lambda step, place: (0, 0))],
            scratch_shapes=[
                pltpu.VMEM((2, width, width), jnp.bfloat16),
                pltpu.SemaphoreType.DMA((2,)),
            ],
        ),
        out_shape=stores + [jax.ShapeDtypeStruct((4, width), jnp.float32)],
        compiler_params=vmem_params(),
        cost_estimate=cost(6 * length * width * width, 16 * length * width),
        name="square_grads",
    )(place, across, grads, out_grad)


def tokens_back_kernel(place, grads_ref, tokens_ref, dmiddle_ref, rows_ref, *rest, sets):
    *refs, out_ref, sums_ref, dmod, held, sems = rest
    step = pl.program_id(0)
    fetch_squares(place, in_sets(refs, sets), step, held, sems)
    part = jnp.bitwise_xor(place[2], step)
    length = tokens_ref.shape[0]

    @pl.when(step == 0)
    def _():
        dmod[...] = jnp.zeros_like(dmod)

    @pl.when(part < 3)
    def _():
        for tile in tiles(length):
            dmod[tile] += matmul(grads_ref[0, tile], held[step % 2], ROWS_NT)

    @pl.when(step == 3)
    def _():
        shift = jnp.zeros((1, dmod.shape[1]), jnp.float32)
        scale = shift
        for tile in tiles(length):
            back = dmod[tile]
            normed, inverse = norm_forward(tokens_ref[tile].astype(jnp.float32))
            scale = scale + jnp.sum(back * normed, axis=0, keepdims=True)
            shift = shift + jnp.sum(back, axis=0, keepdims=True)
            back = norm_backward(back * (1.0 + row_of(rows_ref, SCALE_ATTN)), normed, inverse)
            out_ref[tile] = (dmiddle_ref[tile] + back).astype(jnp.bfloat16)
        sums_ref[0:1] = shift
        sums_ref[1:2] = scale


def tokens_back(place, grads, tokens, dmiddle, rows, squares):
    length, width = tokens.shape
    held = pl.BlockSpec((length, width), lambda step, place: (0, 0), pipeline_mode=pl.Buffered(1))
    return pl.pallas_call(
        functools.partial(tokens_back_kernel, sets=squares),
        grid_spec=pltpu.PrefetchScalarGridSpec(
            num_scalar_prefetch=1,
            grid=(4,),
            in_specs=[
                pl.BlockSpec(
                    (1, length, width),
                    lambda step, place: (jnp.minimum(jnp.bitwise_xor(place[2], step), 2), 0, 0),
                ),
                held,
                held,
                pl.BlockSpec(rows.shape, lambda step, place: (0, 0)),
            ]
            + [ANY] * len(flat(squares)),
            out_specs=[
                pl.BlockSpec((length, width), lambda step, place: (0, 0)),
                pl.BlockSpec((8, width), lambda step, place: (0, 0)),
            ],
            scratch_shapes=[
                pltpu.VMEM((length, width), jnp.float32),
                pltpu.VMEM((2, width, width), jnp.bfloat16),
                pltpu.SemaphoreType.DMA((2,)),
            ],
        ),
        out_shape=[
            jax.ShapeDtypeStruct((length, width), jnp.bfloat16),
            jax.ShapeDtypeStruct((8, width), jnp.float32),
        ],
        compiler_params=vmem_params(),
        cost_estimate=cost(6 * length * width * width, 20 * length * width),
        name="tokens_back",
    )(place, grads, tokens, dmiddle, rows, *flat(squares))


def gather_rows(rows, axis, size):
    place = lax.axis_index(axis)
    step = 1
    while step < size:
        other = lax.ppermute(rows, axis, [(i, i ^ step) for i in range(size)])
        high = (place // step) % 2 == 1
        rows = jnp.concatenate([jnp.where(high, other, rows), jnp.where(high, rows, other)], axis=0)
        step *= 2
    return rows


def swap(value, axis, size, step):
    return lax.ppermute(value, axis, [(i, i ^ step) for i in range(size)])


def both(value, axis, size, step, dim):
    other = swap(value, axis, size, step)
    first = lax.axis_index(axis) // step % 2 == 0
    return jnp.stack([jnp.where(first, value, other), jnp.where(first, other, value)], axis=dim)


def after(value, *others):
    return lax.optimization_barrier((value, others))[0]


def add(*terms):
    return sum(term.astype(jnp.float32) for term in terms).astype(jnp.bfloat16)


class Pairwise:
    def __init__(self, shards, group):
        self.shards, self.group = shards, group

    def partner(self, value, kind):
        if kind == "x":
            return swap(value, "fsdp", self.shards, 1)
        return swap(value, "dp", self.group, 2 if kind == "y" else 1)

    def ahead(self, value, count):
        pairs = [((target // 2 + count) % 4 * 2 + target % 2, target) for target in range(8)]
        return lax.ppermute(value, "fsdp", pairs)

    def along_z(self, block):
        return jnp.stack([block] + [self.ahead(block, count) for count in (1, 2, 3)])

    def widen(self, blocks, kind):
        return blocks | {key + kind: self.partner(value, kind) for key, value in blocks.items()}

    def listed(self, blocks, kinds):
        found = {"".join(sorted(key)): value for key, value in blocks.items()}
        names = [""]
        for kind in kinds:
            names = [name + more for name in names for more in ("", kind)]
        return [found["".join(sorted(name))] for name in names]

    def first_sum(self, kept, other, kind):
        dim = 0 if kind == "y" else 1
        stay, go = [
            [lax.index_in_dim(half, i, dim, keepdims=False) for half in (kept, other)] for i in (0, 1)
        ]
        return add(*go), stay

    def second_sum(self, stay, back):
        return add(stay[0][1], stay[1][1], back[1]), add(stay[0][0], stay[1][0], back[0])

    def send_z(self, mine):
        return [self.ahead(mine[count], 4 - count) for count in (1, 2, 3)]

    def to_group(self, part):
        parts = both(both(part, "dp", self.group, 2, 0), "dp", self.group, 1, 1)
        return parts.reshape(4, *part.shape)


def reduce_all(grad):
    shard = lax.psum_scatter(grad, "fsdp", scatter_dimension=0, tiled=True)
    return lax.psum(shard, "dp").astype(jnp.float32)


def reduce_columns(parts):
    _, rows, width = parts.shape
    shard = reduce_all(parts.swapaxes(0, 1).reshape(rows, 4 * width))
    return [shard[:, i * width : (i + 1) * width] for i in range(4)]


def conditioning(times, labels, table, shard, width):
    class_count, columns = table.shape
    half = width // 2
    column = shard * columns + jnp.arange(columns, dtype=jnp.int32)
    frequency = jnp.exp(-math.log(10000.0) * (column % half).astype(jnp.float32) / half)
    angles = times.astype(jnp.float32)[:, None] * frequency[None, :]
    embed = jnp.where(column[None, :] < half, jnp.cos(angles), jnp.sin(angles))
    picked = labels[:, None] == jnp.arange(class_count, dtype=jnp.int32)[None, :]
    return embed + jnp.dot(
        picked.astype(jnp.bfloat16), table, preferred_element_type=jnp.float32
    )


def own_part(values, shard, size):
    return lax.dynamic_slice_in_dim(values, shard * size, size, axis=values.ndim - 1)


def body(
    shard_count,
    image_count,
    tokens,
    timesteps,
    labels,
    head_keep,
    chan_keep,
    cotangent,
    qkv_weight,
    qv_bias,
    out_weight,
    out_bias,
    up_weight,
    up_bias,
    down_weight,
    down_bias,
    ada_weight,
    ada_bias,
    class_table,
):
    _, length, width = tokens.shape
    hidden = chan_keep.shape[1]
    class_count = class_table.shape[0]
    columns = width // shard_count
    group_count = image_count // shard_count
    shard = lax.axis_index("fsdp")
    member = lax.axis_index("dp")
    bf16, f32 = jnp.bfloat16, jnp.float32

    facts = gather_rows(jnp.stack([timesteps, labels], axis=1), "fsdp", shard_count)
    group_act = jax.nn.silu(
        conditioning(facts[:, 0], facts[:, 1], class_table, shard, width)
    ).astype(bf16)
    partial = jnp.dot(group_act, ada_weight, preferred_element_type=f32)
    bias_row = lax.dynamic_update_slice_in_dim(
        jnp.zeros((6 * width,), f32), ada_bias.astype(f32), shard * ada_bias.shape[0], axis=0
    )
    small = jnp.concatenate([qv_bias.reshape(-1), out_bias, up_bias, down_bias]).astype(f32)
    sent = jnp.concatenate(
        [partial + bias_row, jnp.broadcast_to(small, (shard_count, small.shape[0]))], axis=1
    )
    parts = lax.all_to_all(sent, "fsdp", 0, 0, tiled=True)
    ada_rows = jnp.sum(parts[:, : 6 * width], axis=0).reshape(6, 1, width)
    shift_attn, scale_attn, gate_attn, shift_mlp, scale_mlp, gate_mlp = [ada_rows[i] for i in range(6)]
    small = parts[:, 6 * width :]
    query_bias = small[:, :columns].reshape(-1)
    value_bias = small[:, columns : 2 * columns].reshape(-1)
    out_bias_full = small[:, 2 * columns : 3 * columns].reshape(-1)
    up_end = 3 * columns + up_bias.shape[0]
    up_bias_full = small[:, 3 * columns : up_end].reshape(-1)
    down_bias_full = small[:, up_end:].reshape(-1)

    place = jnp.stack([shard // 2, shard % 2, member]).astype(jnp.int32)
    paired = shard_count == 8 and group_count == 4 and columns % 16 == 0
    four = jnp.concatenate([qkv_weight, out_weight], axis=1)
    rows = jnp.concatenate([ada_rows[:, 0], out_bias_full[None], down_bias_full[None]])
    qkv_bias = jnp.stack([query_bias, jnp.zeros((width,), f32), value_bias, out_bias_full])
    net = Pairwise(shard_count, group_count)
    splits = [width // 2 // 128 * 128]
    splits.append(width - splits[0])

    mod_one, mod_across, branch_grad, down_bias_g = prepare(tokens[0], cotangent[0], rows)
    if paired:
        mine = lax.dynamic_slice_in_dim(four, member * width, width, axis=1)
        first = {"": net.along_z(mine[:, : splits[0]])}
        second = {"": net.along_z(mine[:, splits[0] :])}
        mine = lax.dynamic_slice_in_dim(up_weight, member * width, width, axis=1)
        up = {"": net.along_z(after(mine, first, second))}
        mine = down_weight.reshape(2, 2, columns, width)
        mine = jnp.where(member % 2 == 0, mine[:, 0], mine[:, 1])
        down = {"": net.along_z(after(mine, up))}
        first = net.widen(first, "x")
        second = net.widen(second, "x")
        first = net.widen(first, "y")
        up = net.widen(after(up, second), "x")
        second = net.widen(after(second, first), "y")
        first = net.widen(first, "c")
        second = net.widen(second, "c")
        up = net.widen(after(up, second), "y")
        down = net.widen(after(down, up), "x")
        squares = [net.listed(blocks, "ycx") for blocks in (first, second)]
    else:
        parts = lax.all_gather(four, "fsdp", axis=0, tiled=True)
        squares = [[parts.reshape(width, 4, width).swapaxes(0, 1)]]
    qkv = project(place, mod_one, qkv_bias, squares)
    attn_low, lse = attend_forward(qkv, head_keep[0])
    if paired:
        attn_low, up, down = lax.optimization_barrier((attn_low, up, down))
        ups = [net.listed(net.widen(up, "c"), "ycx")]
        downs = net.listed(net.widen(down, "c"), "cx")
    else:
        parts = lax.all_gather(up_weight, "fsdp", axis=0, tiled=True)
        ups = [[parts.reshape(width, 4, width).swapaxes(0, 1)]]
        parts = lax.all_gather(down_weight, "fsdp", axis=0, tiled=True)
        downs = [parts.reshape(4, width, width)]
    attn_branch, middle, mod_two, mod_two_across = after_attention(
        place, attn_low, tokens[0], rows, squares
    )
    branch_mlp, mod_two_grad, up_bias_g, *stores = mlp(
        place,
        mod_two,
        mod_two_across,
        branch_grad,
        up_bias_full.reshape(4, width),
        chan_keep.astype(f32).reshape(4, width),
        ups,
        downs,
        columns,
    )
    up_bias_g = up_bias_g.reshape(-1)
    if paired:
        up_kept, up_sent, down_kept, down_sent = stores
        up_other, down_other = net.partner(up_sent, "c"), net.partner(down_sent, "c")
    else:
        up_shard = jnp.concatenate(reduce_columns(stores[0]), axis=1)
        down_shard = reduce_all(stores[1].reshape(hidden, width))
    block_out, middle_grad, low_grad, sums, out_weight_g = after_mlp(
        place,
        branch_mlp,
        mod_two_grad,
        middle,
        attn_branch,
        cotangent[0],
        attn_low,
        rows,
        squares,
        columns,
    )
    gate_mlp_grad, scale_mlp_grad, shift_mlp_grad, gate_attn_grad, out_bias_g = [
        sums[i] for i in range(5)
    ]
    if paired:
        low_grad, up_other, down_other = lax.optimization_barrier((low_grad, up_other, down_other))
        up_go, up_stay = net.first_sum(up_kept, up_other, "x")
        down_go, down_stay = net.first_sum(down_kept, down_other, "y")
        low_grad, up_go, down_go = lax.optimization_barrier((low_grad, up_go, down_go))
        up_back, down_back = net.partner(up_go, "x"), net.partner(down_go, "y")
    grads = attend_backward(qkv, attn_low, low_grad, lse, head_keep[0])
    if paired:
        grads, up_back, down_back = lax.optimization_barrier((grads, up_back, down_back))
        up_go, up_stay = net.second_sum(up_stay, up_back)
        down_go, down_stay = net.second_sum(down_stay, down_back)
        grads, up_go, down_go = lax.optimization_barrier((grads, up_go, down_go))
        up_back, down_back = net.partner(up_go, "y"), net.partner(down_go, "x")
    *stores, bias_sums = square_grads(place, mod_across, grads, out_weight_g, columns, splits)
    query_sum, value_sum = bias_sums[0], bias_sums[2]
    if paired:
        grads, stores = lax.optimization_barrier((grads, stores))
        others = [net.partner(sent, "c") for sent in stores[1::2]]
    tokens_grad, sums = tokens_back(place, grads, tokens[0], middle_grad, rows, squares)
    shift_attn_grad, scale_attn_grad = sums[0], sums[1]
    if paired:
        tokens_grad, up_back, down_back, others = lax.optimization_barrier(
            (tokens_grad, up_back, down_back, others)
        )
        goes, stays = zip(
            *[net.first_sum(stores[2 * i], others[i], kind) for i, kind in enumerate("yx")]
        )
        backs = [net.partner(go, kind) for go, kind in zip(goes, "yx")]
        up_mine, down_mine = add(up_stay, up_back), add(down_stay, down_back)
        up_terms, down_terms = net.send_z(up_mine), net.send_z(down_mine)
        backs, up_terms, down_terms = lax.optimization_barrier((backs, up_terms, down_terms))
        goes, stays = zip(*[net.second_sum(stay, back) for stay, back in zip(stays, backs)])
        backs = [net.partner(go, kind) for go, kind in zip(goes, "xy")]
        part = jnp.stack([add(up_mine[0], *up_terms), add(down_mine[0], *down_terms)])
        parts = net.to_group(part)
        up_shard = jnp.concatenate([parts[i, 0] for i in range(4)], axis=1).astype(f32)
        down_shard = parts[:, 1].reshape(down_weight.shape).astype(f32)
        mine = [add(stay, back) for stay, back in zip(stays, backs)]
        terms = [net.send_z(value) for value in mine]
        part = [add(value[0], *more) for value, more in zip(mine, terms)]
        parts = net.to_group(jnp.concatenate(part, axis=1)).astype(f32)
        query_g, key_g, value_g, out_shard = parts
    else:
        query_g, key_g, value_g, out_shard = reduce_columns(stores[0])
    qkv_shard = jnp.concatenate([query_g, key_g, value_g], axis=1)

    row = jnp.concatenate(
        [
            shift_attn_grad,
            scale_attn_grad,
            gate_attn_grad,
            shift_mlp_grad,
            scale_mlp_grad,
            gate_mlp_grad,
            query_sum,
            value_sum,
            out_bias_g,
            up_bias_g,
            down_bias_g[0],
        ]
    ).astype(bf16)[None]
    rows = gather_rows(gather_rows(row, "fsdp", shard_count), "dp", group_count)
    all_facts = gather_rows(facts, "dp", group_count)
    cond = conditioning(all_facts[:, 0], all_facts[:, 1], class_table, shard, width)
    cond_act, silu_pull = jax.vjp(jax.nn.silu, cond)
    ada_grad = rows[:, : 6 * width]
    ada_weight_g = jnp.einsum(
        "sd,se->de", cond_act.astype(bf16), ada_grad, preferred_element_type=f32
    )
    cond_act_grad = jnp.einsum("se,de->sd", ada_grad, ada_weight, preferred_element_type=f32)
    cond_grad = silu_pull(cond_act_grad)[0]
    picked = all_facts[:, 1][:, None] == jnp.arange(class_count, dtype=jnp.int32)[None, :]
    table_g = jnp.einsum(
        "sc,sd->cd", picked.astype(f32), cond_grad, precision=lax.Precision.HIGHEST
    )
    sums = jnp.sum(rows.astype(f32), axis=0)
    ada_bias_g = own_part(sums[: 6 * width], shard, ada_bias.shape[0])
    qv_bias_g = own_part(sums[6 * width : 8 * width].reshape(2, width), shard, columns)
    out_bias_g = own_part(sums[8 * width : 9 * width], shard, columns)
    up_bias_g = own_part(sums[9 * width : 9 * width + hidden], shard, up_bias.shape[0])
    down_bias_g = own_part(sums[9 * width + hidden :], shard, columns)
    return (
        block_out[None],
        tokens_grad[None],
        qkv_shard,
        qv_bias_g,
        out_shard,
        out_bias_g,
        up_shard,
        up_bias_g,
        down_shard,
        down_bias_g,
        ada_weight_g,
        ada_bias_g,
        table_g,
    )


def solution(mesh):
    shard_count = mesh.shape["fsdp"]
    image_count = shard_count * mesh.shape["dp"]
    images = ("fsdp", "dp")
    return jax.shard_map(
        functools.partial(body, shard_count, image_count),
        mesh=mesh,
        in_specs=(
            P(images, None, None),
            P(images),
            P(images),
            P(images, None),
            P(images, None),
            P(images, None, None),
            P("fsdp", None),
            P(None, "fsdp"),
            P("fsdp", None),
            P("fsdp"),
            P("fsdp", None),
            P("fsdp"),
            P("fsdp", None),
            P("fsdp"),
            P("fsdp", None),
            P("fsdp"),
            P(None, "fsdp"),
        ),
        out_specs=(
            P(images, None, None),
            P(images, None, None),
            P("fsdp", None),
            P(None, "fsdp"),
            P("fsdp", None),
            P("fsdp"),
            P("fsdp", None),
            P("fsdp"),
            P("fsdp", None),
            P("fsdp"),
            P("fsdp", None),
            P("fsdp"),
            P(None, "fsdp"),
        ),
        check_vma=False,
    )
```

```python
import functools
import math

import jax
import jax.numpy as jnp
from jax import lax
from jax.experimental import pallas as pl
from jax.experimental.pallas import tpu as pltpu
from jax.sharding import PartitionSpec as P

LOG2E = 1.4426950408889634
ROWS_NT = (((1,), (1,)), ((), ()))
ROWS_NN = (((1,), (0,)), ((), ()))


def matmul(left, right, dims):
    return lax.dot_general(left, right, dims, preferred_element_type=jnp.float32)


def norm_forward(values):
    row_mean = jnp.mean(values, axis=-1, keepdims=True)
    centred = values - row_mean
    inverse = lax.rsqrt(jnp.mean(centred * centred, axis=-1, keepdims=True) + 1e-06)
    return (centred * inverse, inverse)


def norm_backward(gradient, normed, inverse):
    return inverse * (
        gradient
        - jnp.mean(gradient, axis=-1, keepdims=True)
        - normed * jnp.mean(gradient * normed, axis=-1, keepdims=True)
    )


def head_window(head, head_size, width):
    tile = jnp.minimum((head * head_size) // 128, width // 128 - 2)
    base = pl.multiple_of(tile * 128, 128)
    lane = lax.broadcasted_iota(jnp.int32, (1, 256), 1) + (base - head * head_size)
    return base, (lane >= 0) & (lane < head_size)


def as_row(column):
    return jnp.transpose(jnp.broadcast_to(column, (column.shape[0], 128)))[0:1]


def attend_forward_kernel(
    keep_ref, query_ref, key_ref, value_ref, out_ref, lse_ref, *, head_size, width, rows
):
    query_ref, key_ref, value_ref = query_ref.at[0], key_ref.at[0], value_ref.at[0]
    head = pl.program_id(0)
    base, mask = head_window(head, head_size, width)
    scale = head_size**-0.5 * LOG2E
    zero = jnp.zeros((), jnp.bfloat16)
    window = (slice(None), pl.ds(base, 256))
    keys = key_ref[window]
    values = value_ref[window]
    keep = keep_ref[head].astype(jnp.float32)
    for start in range(0, query_ref.shape[0], rows):
        block = (pl.ds(start, rows), pl.ds(base, 256))
        query = jnp.where(mask, query_ref[block], zero)
        scores = matmul(query, keys, ROWS_NT)
        top = jnp.max(scores, axis=-1, keepdims=True)
        probs = jnp.exp2((scores - top) * scale)
        total = jnp.sum(probs, axis=-1, keepdims=True)
        mixed = matmul(probs.astype(jnp.bfloat16), values, ROWS_NN)
        mixed = (mixed * (keep / total)).astype(jnp.bfloat16)
        out_ref[block] = jnp.where(mask, mixed, out_ref[block])
        lse_ref[pl.ds(head, 1), pl.ds(start, rows)] = as_row(top * scale + jnp.log2(total))


def attend_backward_kernel(
    keep_ref,
    query_ref,
    key_ref,
    value_ref,
    out_ref,
    grad_ref,
    lse_ref,
    grads_ref,
    *,
    head_size,
    width,
    rows,
):
    query_ref, key_ref, value_ref = query_ref.at[0], key_ref.at[0], value_ref.at[0]
    dquery_ref, dkey_ref, dvalue_ref = grads_ref.at[0], grads_ref.at[1], grads_ref.at[2]
    head = pl.program_id(0)
    base, mask = head_window(head, head_size, width)
    scale = head_size**-0.5
    zero = jnp.zeros((), jnp.bfloat16)
    length = query_ref.shape[0]
    window = (slice(None), pl.ds(base, 256))
    keys = key_ref[window]
    values = value_ref[window]
    keys_across = jnp.transpose(keys)
    key_grad = jnp.zeros((length, 256), jnp.float32)
    value_grad = jnp.zeros((length, 256), jnp.float32)
    kept = mask & (keep_ref[head] > 0)
    for start in range(0, length, rows):
        block = (pl.ds(start, rows), pl.ds(base, 256))
        query = jnp.where(mask, query_ref[block], zero)
        grad = jnp.where(kept, grad_ref[block], zero)
        row_dot = as_row(
            jnp.sum(
                grad.astype(jnp.float32) * out_ref[block].astype(jnp.float32), axis=-1, keepdims=True
            )
        )
        lse = lse_ref[pl.ds(head, 1), pl.ds(start, rows)]
        probs = jnp.exp2(matmul(keys, query, ROWS_NT) * (scale * LOG2E) - lse)
        score_grad = (probs * (matmul(values, grad, ROWS_NT) - row_dot)).astype(jnp.bfloat16)
        value_grad = value_grad + matmul(probs.astype(jnp.bfloat16), grad, ROWS_NN)
        key_grad = key_grad + matmul(score_grad, query, ROWS_NN)
        query_grad = jnp.transpose(matmul(keys_across, score_grad, ROWS_NN)) * scale
        dquery_ref[block] = jnp.where(mask, query_grad.astype(jnp.bfloat16), dquery_ref[block])
    dkey_ref[window] = jnp.where(mask, (key_grad * scale).astype(jnp.bfloat16), dkey_ref[window])
    dvalue_ref[window] = jnp.where(mask, value_grad.astype(jnp.bfloat16), dvalue_ref[window])


def whole(shape):
    return pl.BlockSpec(shape, lambda *_: (0,) * len(shape), pipeline_mode=pl.Buffered(1))


def one_of(index, length, width):
    return pl.BlockSpec(
        (1, length, width), lambda head: (index, 0, 0), pipeline_mode=pl.Buffered(1)
    )


def attend_forward(qkv, keep, rows=512):
    _, length, width = qkv.shape
    heads = keep.shape[0]
    cells = heads * length * length
    return pl.pallas_call(
        functools.partial(
            attend_forward_kernel, head_size=width // heads, width=width, rows=min(rows, length)
        ),
        grid=(heads,),
        in_specs=[pl.BlockSpec(memory_space=pltpu.SMEM)]
        + [one_of(i, length, width) for i in range(3)],
        out_specs=[
            pl.BlockSpec((length, width), lambda head: (0, 0)),
            pl.BlockSpec((heads, length), lambda head: (0, 0)),
        ],
        out_shape=[
            jax.ShapeDtypeStruct((length, width), jnp.bfloat16),
            jax.ShapeDtypeStruct((heads, length), jnp.float32),
        ],
        compiler_params=pltpu.CompilerParams(vmem_limit_bytes=48 << 20),
        cost_estimate=pl.CostEstimate(
            flops=cells * 1024, transcendentals=cells, bytes_accessed=length * width * 8
        ),
        name="attend_forward",
    )(keep, qkv, qkv, qkv)


def attend_backward(qkv, out, grad, lse, keep, rows=256):
    _, length, width = qkv.shape
    heads = keep.shape[0]
    cells = heads * length * length
    return pl.pallas_call(
        functools.partial(
            attend_backward_kernel, head_size=width // heads, width=width, rows=min(rows, length)
        ),
        grid=(heads,),
        in_specs=[pl.BlockSpec(memory_space=pltpu.SMEM)]
        + [one_of(i, length, width) for i in range(3)]
        + [whole((length, width))] * 2
        + [whole((heads, length))],
        out_specs=pl.BlockSpec((3, length, width), lambda head: (0, 0, 0)),
        out_shape=jax.ShapeDtypeStruct((3, length, width), jnp.bfloat16),
        compiler_params=pltpu.CompilerParams(vmem_limit_bytes=56 << 20),
        cost_estimate=pl.CostEstimate(
            flops=cells * 2560, transcendentals=cells, bytes_accessed=length * width * 16
        ),
        name="attend_backward",
    )(keep, qkv, qkv, qkv, out, grad, lse)


ROWS_TN = (((0,), (0,)), ((), ()))
ANY = pl.BlockSpec(memory_space=pl.ANY)


class Blocks(list):
    def __init__(self, arrays, order):
        super().__init__(arrays)
        self.order = order

    def block(self, r, x_r, z_r):
        y_r, core_r = r // 2, r % 2
        first_r, second_r = (x_r, y_r) if self.order == "xy" else (y_r, x_r)
        return self[2 * core_r + second_r].at[first_r, z_r]


def square_copies(place, sets, r, target, sem):
    part = jnp.bitwise_xor(place[2], r)
    if len(sets[0]) == 1:
        return [pltpu.make_async_copy(sets[0][0].at[part], target, sem)]
    copies, column = [], 0
    for refs in sets:
        rows, columns = refs[0].shape[2:]
        for x_r in range(2):
            for z_r in range(4):
                shard = (place[0] + z_r) % 4 * 2 + (place[1] + x_r) % 2
                block = (pl.ds(pl.multiple_of(shard * rows, 16), rows), pl.ds(column, columns))
                source = refs.block(r, x_r, z_r)
                copies.append(pltpu.make_async_copy(source, target.at[block], sem))
        column += columns
    return copies


def strip_copies(place, refs, chunk, target, sem):
    if len(refs) == 1:
        return [pltpu.make_async_copy(refs[0].at[chunk], target, sem)]
    rows = refs[0].shape[2]
    copies = []
    for core_r in range(2):
        for y in range(2):
            part = 2 * y + (place[2] + core_r) % 2
            for x in range(2):
                start = pl.multiple_of(x * (4 * rows) + part * rows, 16)
                source = refs[core_r].at[2 * chunk + x, y]
                copies.append(pltpu.make_async_copy(source, target.at[pl.ds(start, rows)], sem))
    return copies


def square_stores(place, outs, r, source, sem):
    part = jnp.bitwise_xor(place[2], r)
    if len(outs) == 1:
        return [pltpu.make_async_copy(source, outs[0].at[part], sem)]
    copies, column = [], 0
    for pair in range(0, len(outs), 2):
        out = outs[pair + r % 2]
        out = out if len(out.shape) == 4 else out.at[r // 2]
        rows, columns = out.shape[2:]
        for shard in range(8):
            x_r, z_r = (place[1] + shard % 2) % 2, (shard // 2 + 4 - place[0]) % 4
            block = source.at[pl.ds(shard * rows, rows), pl.ds(column, columns)]
            copies.append(pltpu.make_async_copy(block, out.at[x_r, z_r], sem))
        column += columns
    return copies


def strip_stores(place, outs, chunk, source, sem):
    if len(outs) == 1:
        return [pltpu.make_async_copy(source, outs[0].at[chunk], sem)]
    rows = outs[0].shape[3]
    z_r = (chunk + 4 - place[0]) % 4
    copies = []
    for r in range(4):
        part = jnp.bitwise_xor(place[2], r)
        for x in range(2):
            block = source.at[pl.ds(pl.multiple_of(x * (4 * rows) + part * rows, 16), rows)]
            x_r = (place[1] + x) % 2
            copies.append(pltpu.make_async_copy(block, outs[r % 2].at[r // 2, x_r, z_r], sem))
    return copies


def in_sets(refs, sets):
    refs, found = list(refs), []
    for entry in sets:
        found.append(Blocks(refs[: len(entry)], entry.order))
        refs = refs[len(entry) :]
    return found


def flat(sets):
    return [array for entry in sets for array in entry]


def start_all(copies):
    for copy in copies:
        copy.start()


def wait_all(copies):
    for copy in copies:
        copy.wait()


def for_each(step, action):
    for r in range(4):

        @pl.when(step == r)
        def _(r=r):
            action(r)


def fetch_squares(place, sets, step, held, sems):
    @pl.when(step == 0)
    def _():
        start_all(square_copies(place, sets, 0, held.at[0], sems.at[0]))

    for_each(
        step + 1,
        lambda r: start_all(square_copies(place, sets, r, held.at[r % 2], sems.at[r % 2])),
    )
    for_each(
        step, lambda r: wait_all(square_copies(place, sets, r, held.at[r % 2], sems.at[r % 2]))
    )


def tiles(length, rows=256):
    return [pl.ds(start, min(rows, length)) for start in range(0, length, min(rows, length))]


def prepare_kernel(
    tokens_ref, cotangent_ref, parts_ref, mod_ref, across_ref, grad_ref, sum_ref, rows_ref
):
    width = tokens_ref.shape[1]

    @pl.when(pl.program_id(0) == 0)
    def _():
        for row in range(parts_ref.shape[1] // width):
            part = parts_ref[:, row * width : (row + 1) * width]
            rows_ref[row : row + 1] = jnp.sum(part, axis=0, keepdims=True)
        sum_ref[...] = jnp.zeros_like(sum_ref)

    normed, _ = norm_forward(tokens_ref[...].astype(jnp.float32))
    mod = normed * (1.0 + row_of(rows_ref, SCALE_ATTN)) + row_of(rows_ref, SHIFT_ATTN)
    mod_ref[...] = mod.astype(jnp.bfloat16)
    across_ref[...] = jnp.transpose(mod).astype(jnp.bfloat16)
    grad = (cotangent_ref[...].astype(jnp.float32) * row_of(rows_ref, GATE_MLP)).astype(jnp.bfloat16)
    grad_ref[...] = grad
    sum_ref[0:1] += jnp.sum(grad.astype(jnp.float32), axis=0, keepdims=True)


def prepare(tokens, cotangent, parts, tile=256):
    length, width = tokens.shape
    tile = min(tile, length)
    by_rows = pl.BlockSpec((tile, width), lambda step: (step, 0))
    fixed = pl.BlockSpec((8, width), lambda step: (0, 0))
    table = (16, width)
    return pl.pallas_call(
        prepare_kernel,
        grid=(length // tile,),
        in_specs=[by_rows, by_rows, pl.BlockSpec(parts.shape, lambda step: (0, 0))],
        out_specs=[
            by_rows,
            pl.BlockSpec((width, tile), lambda step: (0, step)),
            by_rows,
            fixed,
            pl.BlockSpec(table, lambda step: (0, 0)),
        ],
        out_shape=[
            jax.ShapeDtypeStruct((length, width), jnp.bfloat16),
            jax.ShapeDtypeStruct((width, length), jnp.bfloat16),
            jax.ShapeDtypeStruct((length, width), jnp.bfloat16),
            jax.ShapeDtypeStruct((8, width), jnp.float32),
            jax.ShapeDtypeStruct(table, jnp.float32),
        ],
        compiler_params=vmem_params(),
        cost_estimate=cost(20 * length * width, 10 * length * width),
        name="prepare",
    )(tokens, cotangent, parts)


def project_kernel(place, mod_ref, rows_ref, *rest, sets):
    *refs, out_ref, held, sems = rest
    step = pl.program_id(0)
    fetch_squares(place, in_sets(refs, sets), step, held, sems)
    part = jnp.bitwise_xor(place[2], step)

    @pl.when(part < 3)
    def _():
        weight = held[step % 2]
        bias = rows_ref[pl.ds(QUERY_BIAS + part // 2, 1)] * (part != 1).astype(jnp.float32)
        for tile in tiles(mod_ref.shape[0]):
            out_ref[0, tile] = (matmul(mod_ref[tile], weight, ROWS_NN) + bias).astype(jnp.bfloat16)


def vmem_params(mebibytes=56):
    return pltpu.CompilerParams(
        vmem_limit_bytes=mebibytes << 20, dimension_semantics=("arbitrary",)
    )


def cost(flops, moved):
    return pl.CostEstimate(flops=1, transcendentals=0, bytes_accessed=1)


def project(place, mod, rows, squares):
    length, width = mod.shape
    return pl.pallas_call(
        functools.partial(project_kernel, sets=squares),
        grid_spec=pltpu.PrefetchScalarGridSpec(
            num_scalar_prefetch=1,
            grid=(4,),
            in_specs=[
                pl.BlockSpec((length, width), lambda step, place: (0, 0)),
                pl.BlockSpec(rows.shape, lambda step, place: (0, 0)),
            ]
            + [ANY] * len(flat(squares)),
            out_specs=pl.BlockSpec(
                (1, length, width), lambda step, place: (jnp.bitwise_xor(place[2], step), 0, 0)
            ),
            scratch_shapes=[
                pltpu.VMEM((2, width, width), jnp.bfloat16),
                pltpu.SemaphoreType.DMA((2,)),
            ],
        ),
        out_shape=jax.ShapeDtypeStruct((4, length, width), jnp.bfloat16),
        compiler_params=vmem_params(),
        cost_estimate=cost(6 * length * width * width, 14 * length * width),
        name="project",
    )(place, mod, rows, *flat(squares))


def fetch_part(place, sets, wanted, target, sem):
    part = jnp.bitwise_xor(place[2], wanted)
    for_each(part, lambda r: start_all(square_copies(place, sets, r, target, sem)))
    for_each(part, lambda r: wait_all(square_copies(place, sets, r, target, sem)))


def row_of(rows_ref, index):
    return rows_ref[index : index + 1]


SHIFT_ATTN, SCALE_ATTN, GATE_ATTN, SHIFT_MLP, SCALE_MLP, GATE_MLP = range(6)
QUERY_BIAS, VALUE_BIAS, OUT_BIAS, UP_BIAS, DOWN_BIAS = 6, 7, 8, 9, 13


def after_attention_kernel(place, low_ref, tokens_ref, rows_ref, *rest, sets):
    *refs, branch_ref, middle_ref, mod_ref, across_ref, weight, sem = rest

    @pl.when(pl.program_id(0) == 0)
    def _():
        fetch_part(place, in_sets(refs, sets), 3, weight, sem)

    branch = matmul(low_ref[...], weight[...], ROWS_NN) + row_of(rows_ref, OUT_BIAS)
    middle = tokens_ref[...].astype(jnp.float32) + row_of(rows_ref, GATE_ATTN) * branch
    normed, _ = norm_forward(middle)
    mod = normed * (1.0 + row_of(rows_ref, SCALE_MLP)) + row_of(rows_ref, SHIFT_MLP)
    branch_ref[...] = branch
    middle_ref[...] = middle
    mod_ref[...] = mod.astype(jnp.bfloat16)
    across_ref[...] = jnp.transpose(mod).astype(jnp.bfloat16)


def after_attention(place, low, tokens, rows, squares, tile=256):
    length, width = low.shape
    tile = min(tile, length)
    by_rows = pl.BlockSpec((tile, width), lambda step, place: (step, 0))
    return pl.pallas_call(
        functools.partial(after_attention_kernel, sets=squares),
        grid_spec=pltpu.PrefetchScalarGridSpec(
            num_scalar_prefetch=1,
            grid=(length // tile,),
            in_specs=[by_rows, by_rows, pl.BlockSpec(rows.shape, lambda step, place: (0, 0))]
            + [ANY] * len(flat(squares)),
            out_specs=[by_rows] * 3 + [pl.BlockSpec((width, tile), lambda step, place: (0, step))],
            scratch_shapes=[pltpu.VMEM((width, width), jnp.bfloat16), pltpu.SemaphoreType.DMA],
        ),
        out_shape=[
            jax.ShapeDtypeStruct((length, width), jnp.float32),
            jax.ShapeDtypeStruct((length, width), jnp.float32),
            jax.ShapeDtypeStruct((length, width), jnp.bfloat16),
            jax.ShapeDtypeStruct((width, length), jnp.bfloat16),
        ],
        compiler_params=vmem_params(),
        cost_estimate=cost(2 * length * width * width, 18 * length * width),
        name="after_attention",
    )(place, low, tokens, rows, *flat(squares))


ROOT = 0.7978845608028654


def gelu_and_slope(values):
    square = values * values
    bend = jnp.tanh(values * (ROOT + (ROOT * 0.044715) * square))
    half = 0.5 + 0.5 * bend
    slope = half + (0.5 * values) * (1.0 - bend * bend) * (ROOT + (3 * 0.044715 * ROOT) * square)
    return values * half, slope


def mlp_kernel(place, mod_ref, across_ref, grad_ref, rows_ref, keep_ref, *rest, ups, downs):
    count = len(flat(ups)) + downs
    refs, rest = rest[:count], rest[count:]
    up_sets, down_refs = in_sets(refs, ups), refs[-downs:]
    branch_ref, dmod_ref, dbias_ref = rest[:3]
    *stores, act, dpre, up, down, up_out, down_out, in_sems, out_sems = rest[3:]
    up_stores, down_stores = stores[: len(stores) // 2], stores[len(stores) // 2 :]
    step = pl.program_id(0)
    length = mod_ref.shape[0]

    def chunk_of(r):
        return jnp.bitwise_xor(place[2], r)

    def fetch(r):
        slot = r % 2
        return square_copies(place, up_sets, r, up.at[slot], in_sems.at[slot, 0]) + strip_copies(
            place, down_refs, chunk_of(r), down.at[slot], in_sems.at[slot, 1]
        )

    @pl.when(step == 0)
    def _():
        start_all(fetch(0))
        branch_ref[...] = jnp.zeros_like(branch_ref)
        dmod_ref[...] = jnp.zeros_like(dmod_ref)

    for_each(step + 1, lambda r: start_all(fetch(r)))
    for_each(step, lambda r: wait_all(fetch(r)))
    chunk = chunk_of(step)
    slot = step % 2
    bias = rows_ref[pl.ds(UP_BIAS + chunk, 1)]
    keep = keep_ref[pl.ds(chunk, 1)]
    total = jnp.zeros_like(bias)
    for tile in tiles(length):
        gelu, slope = gelu_and_slope(matmul(mod_ref[tile], up[slot], ROWS_NN) + bias)
        act[tile] = (gelu * keep).astype(jnp.bfloat16)
        back = matmul(grad_ref[tile], down[slot], ROWS_NT)
        low = (slope * keep * back).astype(jnp.bfloat16)
        dpre[tile] = low
        total = total + jnp.sum(low.astype(jnp.float32), axis=0, keepdims=True)
        branch_ref[tile] += matmul(act[tile], down[slot], ROWS_NN)
        dmod_ref[tile] += matmul(low, up[slot], ROWS_NT)
    dbias_ref[pl.ds(chunk, 1)] = total

    def leave(r):
        return square_stores(place, up_stores, r, up_out, out_sems.at[0]), strip_stores(
            place, down_stores, chunk_of(r), down_out, out_sems.at[1]
        )

    for_each(step - 1, lambda r: wait_all(leave(r)[0]))
    up_out[...] = matmul(across_ref[...], dpre[...], ROWS_NN).astype(jnp.bfloat16)
    for_each(step, lambda r: start_all(leave(r)[0]))
    for_each(step - 1, lambda r: wait_all(leave(r)[1]))
    down_out[...] = matmul(act[...], grad_ref[...], ROWS_TN).astype(jnp.bfloat16)
    for_each(step, lambda r: start_all(leave(r)[1]))

    @pl.when(step == 3)
    def _():
        wait_all(leave(3)[0])
        wait_all(leave(3)[1])


def gradient_shapes(paired, rows, columns):
    if paired:
        return [
            jax.ShapeDtypeStruct((2, 2, 4, rows, count), jnp.bfloat16)
            for count in columns
            for _ in range(2)
        ]
    return [jax.ShapeDtypeStruct((4, sum(columns), sum(columns)), jnp.bfloat16)]


def mlp(place, mod, across, grad, rows, keep, ups, downs, block_rows):
    length, width = mod.shape
    stores = gradient_shapes(len(downs) > 1, block_rows, [width])
    quarter = jax.ShapeDtypeStruct((4, width), jnp.float32)
    table = pl.BlockSpec((4, width), lambda step, place: (0, 0))
    held = pl.BlockSpec((length, width), lambda step, place: (0, 0), pipeline_mode=pl.Buffered(1))
    square = pltpu.VMEM((width, width), jnp.bfloat16)
    pair = pltpu.VMEM((2, width, width), jnp.bfloat16)
    tall = pltpu.VMEM((length, width), jnp.bfloat16)
    wide = pl.BlockSpec((length, width), lambda step, place: (0, 0))
    return pl.pallas_call(
        functools.partial(mlp_kernel, ups=ups, downs=len(downs)),
        grid_spec=pltpu.PrefetchScalarGridSpec(
            num_scalar_prefetch=1,
            grid=(4,),
            in_specs=[
                held,
                pl.BlockSpec((width, length), lambda step, place: (0, 0), pipeline_mode=pl.Buffered(1)),
                held,
                pl.BlockSpec(rows.shape, lambda step, place: (0, 0)),
                table,
            ]
            + [ANY] * (len(flat(ups)) + len(downs)),
            out_specs=[wide, wide, table] + [ANY] * (2 * len(stores)),
            scratch_shapes=[
                tall,
                tall,
                pair,
                pair,
                square,
                square,
                pltpu.SemaphoreType.DMA((2, 2)),
                pltpu.SemaphoreType.DMA((2,)),
            ],
        ),
        out_shape=[jax.ShapeDtypeStruct((length, width), jnp.float32)] * 2
        + [quarter]
        + stores
        + stores,
        compiler_params=vmem_params(60),
        cost_estimate=cost(48 * length * width * width, 32 * width * width),
        name="mlp",
    )(place, mod, across, grad, rows, keep, *flat(ups), *downs)


def after_mlp_kernel(
    place, mlp_ref, dmod_ref, middle_ref, branch_ref, cotangent_ref, low_ref, rows_ref, *rest, sets
):
    *refs, out_ref, dmiddle_ref, dlow_ref, sums_ref, dweight_ref, weight, dbranch, staged, sems = rest
    step = pl.program_id(0)
    tile = out_ref.shape[0]

    @pl.when(step == 0)
    def _():
        fetch_part(place, in_sets(refs, sets), 3, weight, sems.at[0])
        sums_ref[...] = jnp.zeros_like(sums_ref)

    middle = middle_ref[...]
    grad = cotangent_ref[...].astype(jnp.float32)
    mlp_branch = mlp_ref[...] + row_of(rows_ref, DOWN_BIAS)
    out_ref[...] = (middle + row_of(rows_ref, GATE_MLP) * mlp_branch).astype(jnp.bfloat16)
    normed, inverse = norm_forward(middle)
    dmod = dmod_ref[...]
    dmiddle = grad + norm_backward(dmod * (1.0 + row_of(rows_ref, SCALE_MLP)), normed, inverse)
    dmiddle_ref[...] = dmiddle
    low = (dmiddle * row_of(rows_ref, GATE_ATTN)).astype(jnp.bfloat16)
    dbranch[pl.ds(pl.multiple_of(step * tile, tile), tile)] = low
    dlow_ref[...] = matmul(low, weight[...], ROWS_NT).astype(jnp.bfloat16)

    def add(index, values):
        sums_ref[index : index + 1] += jnp.sum(values, axis=0, keepdims=True)

    add(0, grad * mlp_branch)
    add(1, dmod * normed)
    add(2, dmod)
    add(3, dmiddle * branch_ref[...])
    add(4, low.astype(jnp.float32))

    @pl.when(step == pl.num_programs(0) - 1)
    def _():
        staged[...] = matmul(low_ref[...], dbranch[...], ROWS_TN).astype(jnp.bfloat16)
        if len(dweight_ref.shape) == 2:
            copies = [pltpu.make_async_copy(staged, dweight_ref, sems.at[1])]
        else:
            rows = dweight_ref.shape[2]
            copies = []
            for shard in range(8):
                x_r, z_r = (place[1] + shard % 2) % 2, (shard // 2 + 4 - place[0]) % 4
                block = staged.at[pl.ds(shard * rows, rows)]
                copies.append(pltpu.make_async_copy(block, dweight_ref.at[x_r, z_r], sems.at[1]))
        start_all(copies)
        wait_all(copies)


def after_mlp(place, branch_mlp, dmod, middle, branch, cotangent, low, rows, squares, block_rows, tile=256):
    length, width = low.shape
    tile = min(tile, length)
    by_rows = pl.BlockSpec((tile, width), lambda step, place: (step, 0))
    fixed = lambda shape: pl.BlockSpec(shape, lambda step, place: (0, 0))
    wgrad = (2, 4, block_rows, width) if len(squares[0]) > 1 else (width, width)
    return pl.pallas_call(
        functools.partial(after_mlp_kernel, sets=squares),
        grid_spec=pltpu.PrefetchScalarGridSpec(
            num_scalar_prefetch=1,
            grid=(length // tile,),
            in_specs=[by_rows] * 5 + [fixed((length, width)), fixed(rows.shape)] + [ANY] * len(flat(squares)),
            out_specs=[by_rows] * 3 + [fixed((8, width)), ANY],
            scratch_shapes=[
                pltpu.VMEM((width, width), jnp.bfloat16),
                pltpu.VMEM((length, width), jnp.bfloat16),
                pltpu.VMEM((width, width), jnp.bfloat16),
                pltpu.SemaphoreType.DMA((2,)),
            ],
        ),
        out_shape=[
            jax.ShapeDtypeStruct((length, width), jnp.bfloat16),
            jax.ShapeDtypeStruct((length, width), jnp.float32),
            jax.ShapeDtypeStruct((length, width), jnp.bfloat16),
            jax.ShapeDtypeStruct((8, width), jnp.float32),
            jax.ShapeDtypeStruct(wgrad, jnp.bfloat16),
        ],
        compiler_params=vmem_params(),
        cost_estimate=cost(4 * length * width * width, 30 * length * width),
        name="after_mlp",
    )(place, branch_mlp, dmod, middle, branch, cotangent, low, rows, *flat(squares))


def square_grads_kernel(place, across_ref, grads_ref, out_grad_ref, *rest):
    *stores, staged, sems = rest
    step = pl.program_id(0)
    part = jnp.bitwise_xor(place[2], step)

    def leave(r):
        return square_stores(place, stores, r, staged.at[r % 2], sems.at[r % 2])

    def pass_on(r):
        if len(stores) == 1:
            return [pltpu.make_async_copy(out_grad_ref, stores[0].at[3], sems.at[r % 2])]
        copies, column = [], 0
        for pair in range(0, len(stores), 2):
            out = stores[pair + r % 2]
            columns = out.shape[4]
            source = out_grad_ref.at[:, :, :, pl.ds(column, columns)]
            copies.append(pltpu.make_async_copy(source, out.at[r // 2], sems.at[r % 2]))
            column += columns
        return copies

    def wait(r):
        wait_all(pass_on(r))

    for_each(step - 2, wait)

    @pl.when(part < 3)
    def _():
        grads = grads_ref[0]
        staged[step % 2] = matmul(across_ref[...], grads, ROWS_NN).astype(jnp.bfloat16)
        for_each(step, lambda r: start_all(leave(r)))

    @pl.when(part == 3)
    def _():
        for_each(step, lambda r: start_all(pass_on(r)))

    @pl.when(step == 3)
    def _():
        wait(2)
        wait(3)


def square_grads(place, across, grads, out_grad, block_rows, columns):
    width, length = across.shape
    paired = len(out_grad.shape) > 2
    stores = gradient_shapes(paired, block_rows, columns)
    return pl.pallas_call(
        square_grads_kernel,
        grid_spec=pltpu.PrefetchScalarGridSpec(
            num_scalar_prefetch=1,
            grid=(4,),
            in_specs=[
                pl.BlockSpec((width, length), lambda step, place: (0, 0)),
                pl.BlockSpec(
                    (1, length, width),
                    lambda step, place: (jnp.minimum(jnp.bitwise_xor(place[2], step), 2), 0, 0),
                ),
                pl.BlockSpec(
                    out_grad.shape,
                    lambda step, place: (0,) * len(out_grad.shape),
                    pipeline_mode=pl.Buffered(1),
                ),
            ],
            out_specs=[ANY] * len(stores),
            scratch_shapes=[
                pltpu.VMEM((2, width, width), jnp.bfloat16),
                pltpu.SemaphoreType.DMA((2,)),
            ],
        ),
        out_shape=stores,
        compiler_params=vmem_params(),
        cost_estimate=cost(6 * length * width * width, 16 * length * width),
        name="square_grads",
    )(place, across, grads, out_grad)


def tokens_back_kernel(place, grads_ref, tokens_ref, dmiddle_ref, rows_ref, *rest, sets):
    *refs, out_ref, sums_ref, dmod, held, sems = rest
    step = pl.program_id(0)
    fetch_squares(place, in_sets(refs, sets), step, held, sems)
    part = jnp.bitwise_xor(place[2], step)
    length = tokens_ref.shape[0]

    @pl.when(step == 0)
    def _():
        dmod[...] = jnp.zeros_like(dmod)

    @pl.when(part < 3)
    def _():
        for tile in tiles(length):
            dmod[tile] += matmul(grads_ref[0, tile], held[step % 2], ROWS_NT)
        total = jnp.sum(grads_ref[0].astype(jnp.float32), axis=0, keepdims=True)
        sums_ref[pl.ds(2 + part, 1)] = total

    @pl.when(step == 3)
    def _():
        shift = jnp.zeros((1, dmod.shape[1]), jnp.float32)
        scale = shift
        for tile in tiles(length):
            back = dmod[tile]
            normed, inverse = norm_forward(tokens_ref[tile].astype(jnp.float32))
            scale = scale + jnp.sum(back * normed, axis=0, keepdims=True)
            shift = shift + jnp.sum(back, axis=0, keepdims=True)
            back = norm_backward(back * (1.0 + row_of(rows_ref, SCALE_ATTN)), normed, inverse)
            out_ref[tile] = (dmiddle_ref[tile] + back).astype(jnp.bfloat16)
        sums_ref[0:1] = shift
        sums_ref[1:2] = scale


def tokens_back(place, grads, tokens, dmiddle, rows, squares):
    length, width = tokens.shape
    held = pl.BlockSpec((length, width), lambda step, place: (0, 0), pipeline_mode=pl.Buffered(1))
    return pl.pallas_call(
        functools.partial(tokens_back_kernel, sets=squares),
        grid_spec=pltpu.PrefetchScalarGridSpec(
            num_scalar_prefetch=1,
            grid=(4,),
            in_specs=[
                pl.BlockSpec(
                    (1, length, width),
                    lambda step, place: (jnp.minimum(jnp.bitwise_xor(place[2], step), 2), 0, 0),
                ),
                held,
                held,
                pl.BlockSpec(rows.shape, lambda step, place: (0, 0)),
            ]
            + [ANY] * len(flat(squares)),
            out_specs=[
                pl.BlockSpec((length, width), lambda step, place: (0, 0)),
                pl.BlockSpec((8, width), lambda step, place: (0, 0)),
            ],
            scratch_shapes=[
                pltpu.VMEM((length, width), jnp.float32),
                pltpu.VMEM((2, width, width), jnp.bfloat16),
                pltpu.SemaphoreType.DMA((2,)),
            ],
        ),
        out_shape=[
            jax.ShapeDtypeStruct((length, width), jnp.bfloat16),
            jax.ShapeDtypeStruct((8, width), jnp.float32),
        ],
        compiler_params=vmem_params(),
        cost_estimate=cost(6 * length * width * width, 20 * length * width),
        name="tokens_back",
    )(place, grads, tokens, dmiddle, rows, *flat(squares))


def gather_rows(rows, axis, size):
    place = lax.axis_index(axis)
    step = 1
    while step < size:
        other = lax.ppermute(rows, axis, [(i, i ^ step) for i in range(size)])
        high = (place // step) % 2 == 1
        rows = jnp.concatenate([jnp.where(high, other, rows), jnp.where(high, rows, other)], axis=0)
        step *= 2
    return rows


def swap(value, axis, size, step):
    return lax.ppermute(value, axis, [(i, i ^ step) for i in range(size)])


def both(value, axis, size, step, dim):
    other = swap(value, axis, size, step)
    first = lax.axis_index(axis) // step % 2 == 0
    return jnp.stack([jnp.where(first, value, other), jnp.where(first, other, value)], axis=dim)


def barrier(values):
    return lax.optimization_barrier(values)


def after(value, *others):
    return barrier((value, others))[0]


def add(*terms):
    return sum(term.astype(jnp.float32) for term in terms).astype(jnp.bfloat16)


class Pairwise:
    def __init__(self, shards, group):
        self.shards, self.group = shards, group

    def partner(self, value, kind):
        if kind == "x":
            return swap(value, "fsdp", self.shards, 1)
        return swap(value, "dp", self.group, 2 if kind == "y" else 1)

    def ahead(self, value, count):
        pairs = [((target // 2 + count) % 4 * 2 + target % 2, target) for target in range(8)]
        return lax.ppermute(value, "fsdp", pairs)

    def along_z(self, block):
        return jnp.stack([block] + [self.ahead(block, count) for count in (1, 2, 3)])

    def along_x(self, block):
        return jnp.stack([block, self.partner(block, "x")])

    def pair(self, block, kind):
        return jnp.stack([block, self.partner(block, kind)])

    def first_sum(self, kept, other, kind):
        dim = 0 if kind == "y" else 1
        stay, go = [
            [lax.index_in_dim(half, i, dim, keepdims=False) for half in (kept, other)] for i in (0, 1)
        ]
        return add(*go), stay

    def second_sum(self, stay, back):
        return add(stay[0][1], stay[1][1], back[1]), add(stay[0][0], stay[1][0], back[0])

    def send_z(self, mine):
        return [self.ahead(mine[count], 4 - count) for count in (1, 2, 3)]

    def to_group(self, part):
        parts = both(both(part, "dp", self.group, 2, 0), "dp", self.group, 1, 1)
        return parts.reshape(4, *part.shape)


def reduce_all(grad):
    shard = lax.psum_scatter(grad, "fsdp", scatter_dimension=0, tiled=True)
    return lax.psum(shard, "dp").astype(jnp.float32)


def reduce_columns(parts):
    _, rows, width = parts.shape
    shard = reduce_all(parts.swapaxes(0, 1).reshape(rows, 4 * width))
    return [shard[:, i * width : (i + 1) * width] for i in range(4)]


def conditioning(times, labels, table, shard, width):
    class_count, columns = table.shape
    half = width // 2
    column = shard * columns + jnp.arange(columns, dtype=jnp.int32)
    frequency = jnp.exp(-math.log(10000.0) * (column % half).astype(jnp.float32) / half)
    angles = times.astype(jnp.float32)[:, None] * frequency[None, :]
    embed = jnp.where(column[None, :] < half, jnp.cos(angles), jnp.sin(angles))
    picked = labels[:, None] == jnp.arange(class_count, dtype=jnp.int32)[None, :]
    return embed + jnp.dot(
        picked.astype(jnp.bfloat16), table, preferred_element_type=jnp.float32
    )


def own_part(values, shard, size):
    return lax.dynamic_slice_in_dim(values, shard * size, size, axis=values.ndim - 1)


def body(
    shard_count,
    image_count,
    tokens,
    timesteps,
    labels,
    head_keep,
    chan_keep,
    cotangent,
    qkv_weight,
    qv_bias,
    out_weight,
    out_bias,
    up_weight,
    up_bias,
    down_weight,
    down_bias,
    ada_weight,
    ada_bias,
    class_table,
):
    _, length, width = tokens.shape
    hidden = chan_keep.shape[1]
    class_count = class_table.shape[0]
    columns = width // shard_count
    group_count = image_count // shard_count
    shard = lax.axis_index("fsdp")
    member = lax.axis_index("dp")
    bf16, f32 = jnp.bfloat16, jnp.float32

    place = jnp.stack([shard // 2, shard % 2, member]).astype(jnp.int32)
    paired = shard_count == 8 and group_count == 4 and columns % 16 == 0
    net = Pairwise(shard_count, group_count)
    splits = [width // 2 // 128 * 128]
    splits.append(width - splits[0])
    four = jnp.concatenate([qkv_weight, out_weight], axis=1)

    fact = jnp.stack([timesteps[0], labels[0]])
    if paired:
        near = net.along_z(fact)
        mine = lax.dynamic_slice_in_dim(four, member * width, width, axis=1)
        mine, near = barrier((mine, near))
        square = net.along_z(mine)
        near = net.along_x(near).swapaxes(0, 1)
        facts = jnp.where(place[1] == 0, near, near[:, ::-1])
        facts = lax.dynamic_slice_in_dim(
            jnp.concatenate([facts, facts]), (4 - place[0]) % 4, 4, axis=0
        ).reshape(8, 2)
    else:
        facts = gather_rows(fact[None], "fsdp", shard_count)
    group_act = jax.nn.silu(
        conditioning(facts[:, 0], facts[:, 1], class_table, shard, width)
    ).astype(bf16)
    partial = jnp.dot(group_act, ada_weight, preferred_element_type=f32)

    def own_columns(values):
        values = values.astype(f32)
        full = jnp.zeros((values.shape[0] * shard_count,), f32)
        return lax.dynamic_update_slice_in_dim(full, values, shard * values.shape[0], axis=0)

    biases = jnp.concatenate(
        [own_columns(values) for values in (qv_bias[0], qv_bias[1], out_bias, up_bias, down_bias)]
    )
    sent = jnp.concatenate(
        [
            partial + own_columns(ada_bias),
            jnp.broadcast_to(biases, (shard_count, biases.shape[0])),
        ],
        axis=1,
    )
    if paired:
        square, sent, near = barrier((square, sent, near))
        parts = lax.all_to_all(sent, "fsdp", 0, 0, tiled=True)
        all_facts = net.pair(net.pair(near.swapaxes(0, 1), "y"), "c").reshape(image_count, 2)
        first = net.pair(square[:, :, : splits[0]], "x")
        second = net.pair(square[:, :, splits[0] :], "y")
        mine = lax.dynamic_slice_in_dim(up_weight, member * width, width, axis=1)
        down_mine = down_weight.reshape(2, 2, columns, width)
        down_mine = jnp.where(member % 2 == 0, down_mine[:, 0], down_mine[:, 1])
        mine, down_mine, first, second, parts = barrier((mine, down_mine, first, second, parts))
        first_y, second_x = net.partner(first, "y"), net.partner(second, "x")
        up = net.along_z(mine)
        first, second, first_y, second_x, up = barrier((first, second, first_y, second_x, up))
        down = lax.all_gather(after(down_mine, first_y), "fsdp", axis=0)
        squares = [
            Blocks([first, first_y, net.partner(first, "c"), net.partner(first_y, "c")], "xy"),
            Blocks([second, second_x, net.partner(second, "c"), net.partner(second_x, "c")], "yx"),
        ]
    else:
        parts = lax.all_to_all(sent, "fsdp", 0, 0, tiled=True)
        all_facts = gather_rows(facts, "dp", group_count)
        found = lax.all_gather(four, "fsdp", axis=0, tiled=True)
        squares = [Blocks([found.reshape(width, 4, width).swapaxes(0, 1)], "xy")]
    mod_one, mod_across, branch_grad, down_bias_g, rows = prepare(tokens[0], cotangent[0], parts)
    if paired:
        up_x, up_y = net.partner(up, "x"), net.partner(up, "y")
    qkv = project(place, mod_one, rows, squares)
    if paired:
        qkv, up_x, up_y = barrier((qkv, up_x, up_y))
        up_xy = net.partner(up_x, "y")
    attn_low, lse = attend_forward(qkv, head_keep[0])
    if paired:
        attn_low, up_xy, down = barrier((attn_low, up_xy, down))
        up, up_y = jnp.stack([up, up_x]), jnp.stack([up_y, up_xy])
        ups = [Blocks([up, up_y, net.partner(up, "c"), net.partner(up_y, "c")], "xy")]
        downs = [down, net.partner(down, "c")]
    else:
        found = lax.all_gather(up_weight, "fsdp", axis=0, tiled=True)
        ups = [Blocks([found.reshape(width, 4, width).swapaxes(0, 1)], "xy")]
        found = lax.all_gather(down_weight, "fsdp", axis=0, tiled=True)
        downs = [found.reshape(4, width, width)]
    attn_branch, middle, mod_two, mod_two_across = after_attention(
        place, attn_low, tokens[0], rows, squares
    )
    branch_mlp, mod_two_grad, up_bias_g, *stores = mlp(
        place,
        mod_two,
        mod_two_across,
        branch_grad,
        rows,
        chan_keep.astype(f32).reshape(4, width),
        ups,
        downs,
        columns,
    )
    up_bias_g = up_bias_g.reshape(-1)
    if paired:
        up_kept, up_sent, down_kept, down_sent = stores
        up_other, down_other = net.partner(up_sent, "c"), net.partner(down_sent, "c")
    else:
        up_shard = jnp.concatenate(reduce_columns(stores[0]), axis=1)
        down_shard = reduce_all(stores[1].reshape(hidden, width))
    block_out, middle_grad, low_grad, sums, out_weight_g = after_mlp(
        place,
        branch_mlp,
        mod_two_grad,
        middle,
        attn_branch,
        cotangent[0],
        attn_low,
        rows,
        squares,
        columns,
    )
    gate_mlp_grad, scale_mlp_grad, shift_mlp_grad, gate_attn_grad, out_bias_g = [
        sums[i] for i in range(5)
    ]
    if paired:
        low_grad, up_other, down_other = barrier((low_grad, up_other, down_other))
        up_go, up_stay = net.first_sum(up_kept, up_other, "x")
        down_go, down_stay = net.first_sum(down_kept, down_other, "y")
        low_grad, up_go, down_go = barrier((low_grad, up_go, down_go))
        up_back, down_back = net.partner(up_go, "x"), net.partner(down_go, "y")
    grads = attend_backward(qkv, attn_low, low_grad, lse, head_keep[0])
    if paired:
        grads, up_back, down_back = barrier((grads, up_back, down_back))
        up_go, up_stay = net.second_sum(up_stay, up_back)
        down_go, down_stay = net.second_sum(down_stay, down_back)
        grads, up_go, down_go = barrier((grads, up_go, down_go))
        up_back, down_back = net.partner(up_go, "y"), net.partner(down_go, "x")
    tokens_grad, sums = tokens_back(place, grads, tokens[0], middle_grad, rows, squares)
    if paired:
        sums, up_back, down_back, grads = barrier((sums, up_back, down_back, grads))
    row = jnp.concatenate(
        [
            sums[0],
            sums[1],
            gate_attn_grad,
            shift_mlp_grad,
            scale_mlp_grad,
            gate_mlp_grad,
            sums[2],
            sums[4],
            out_bias_g,
            up_bias_g,
            down_bias_g[0],
        ]
    ).astype(bf16)[None]
    if paired:
        up_mine, down_mine = add(up_stay, up_back), add(down_stay, down_back)
        row, up_mine, down_mine, grads = barrier((row, up_mine, down_mine, grads))
        up_terms = net.send_z(up_mine)
        row = net.along_z(row)
    stores = square_grads(place, mod_across, grads, out_weight_g, columns, splits)
    if paired:
        stores, row, up_terms = barrier((stores, row, up_terms))
        others = [net.partner(sent, "c") for sent in stores[1::2]]
        row = net.pair(row, "x")
        others, row = barrier((others, row))
        goes, stays = zip(
            *[net.first_sum(stores[2 * i], others[i], kind) for i, kind in enumerate("yx")]
        )
        goes, row, down_mine = barrier((goes, row, down_mine))
        row = net.pair(row, "y")
        backs = [net.partner(go, kind) for go, kind in zip(goes, "yx")]
        down_terms = net.send_z(down_mine)
        backs, down_terms, row = barrier((backs, down_terms, row))
        goes, stays = zip(*[net.second_sum(stay, back) for stay, back in zip(stays, backs)])
        goes, row = barrier((goes, row))
        all_rows = net.pair(row, "c").reshape(image_count, -1)
        backs = [net.partner(go, kind) for go, kind in zip(goes, "xy")]
        part = jnp.stack([add(up_mine[0], *up_terms), add(down_mine[0], *down_terms)])
        backs, part, all_rows = barrier((backs, part, all_rows))
        mine = jnp.concatenate([add(stay, back) for stay, back in zip(stays, backs)], axis=2)
        mine, part = barrier((mine, part))
        terms = net.send_z(mine)
        mlp_parts = both(part, "dp", group_count, 2, 0)
        terms, mlp_parts = barrier((terms, mlp_parts))
        mlp_parts = both(mlp_parts, "dp", group_count, 1, 1).reshape(4, *part.shape)
        parts = net.to_group(add(mine[0], *terms)).astype(f32)
        up_shard = jnp.concatenate([mlp_parts[i, 0] for i in range(4)], axis=1).astype(f32)
        down_shard = mlp_parts[:, 1].reshape(down_weight.shape).astype(f32)
        query_g, key_g, value_g, out_shard = parts
    else:
        query_g, key_g, value_g, out_shard = reduce_columns(stores[0])
        all_rows = gather_rows(gather_rows(row, "fsdp", shard_count), "dp", group_count)
    qkv_shard = jnp.concatenate([query_g, key_g, value_g], axis=1)
    cond = conditioning(all_facts[:, 0], all_facts[:, 1], class_table, shard, width)
    cond_act, silu_pull = jax.vjp(jax.nn.silu, cond)
    ada_grad = all_rows[:, : 6 * width]
    ada_weight_g = jnp.einsum(
        "sd,se->de", cond_act.astype(bf16), ada_grad, preferred_element_type=f32
    )
    cond_act_grad = jnp.einsum("se,de->sd", ada_grad, ada_weight, preferred_element_type=f32)
    cond_grad = silu_pull(cond_act_grad)[0]
    picked = all_facts[:, 1][:, None] == jnp.arange(class_count, dtype=jnp.int32)[None, :]
    table_g = jnp.einsum(
        "sc,sd->cd", picked.astype(f32), cond_grad, precision=lax.Precision.HIGHEST
    )
    sums = jnp.sum(all_rows.astype(f32), axis=0)
    ada_bias_g = own_part(sums[: 6 * width], shard, ada_bias.shape[0])
    qv_bias_g = own_part(sums[6 * width : 8 * width].reshape(2, width), shard, columns)
    out_bias_g = own_part(sums[8 * width : 9 * width], shard, columns)
    up_bias_g = own_part(sums[9 * width : 9 * width + hidden], shard, up_bias.shape[0])
    down_bias_g = own_part(sums[9 * width + hidden :], shard, columns)
    return (
        block_out[None],
        tokens_grad[None],
        qkv_shard,
        qv_bias_g,
        out_shard,
        out_bias_g,
        up_shard,
        up_bias_g,
        down_shard,
        down_bias_g,
        ada_weight_g,
        ada_bias_g,
        table_g,
    )


def solution(mesh):
    shard_count = mesh.shape["fsdp"]
    image_count = shard_count * mesh.shape["dp"]
    images = ("fsdp", "dp")
    return jax.shard_map(
        functools.partial(body, shard_count, image_count),
        mesh=mesh,
        in_specs=(
            P(images, None, None),
            P(images),
            P(images),
            P(images, None),
            P(images, None),
            P(images, None, None),
            P("fsdp", None),
            P(None, "fsdp"),
            P("fsdp", None),
            P("fsdp"),
            P("fsdp", None),
            P("fsdp"),
            P("fsdp", None),
            P("fsdp"),
            P("fsdp", None),
            P("fsdp"),
            P(None, "fsdp"),
        ),
        out_specs=(
            P(images, None, None),
            P(images, None, None),
            P("fsdp", None),
            P(None, "fsdp"),
            P("fsdp", None),
            P("fsdp"),
            P("fsdp", None),
            P("fsdp"),
            P("fsdp", None),
            P("fsdp"),
            P("fsdp", None),
            P("fsdp"),
            P(None, "fsdp"),
        ),
        check_vma=False,
    )
```

```python
import functools
import math

import jax
import jax.numpy as jnp
from jax import lax
from jax.experimental import pallas as pl
from jax.experimental.pallas import tpu as pltpu
from jax.sharding import PartitionSpec as P

LOG2E = 1.4426950408889634
ROWS_NT = (((1,), (1,)), ((), ()))
ROWS_NN = (((1,), (0,)), ((), ()))


def matmul(left, right, dims):
    return lax.dot_general(left, right, dims, preferred_element_type=jnp.float32)


def norm_forward(values):
    row_mean = jnp.mean(values, axis=-1, keepdims=True)
    centred = values - row_mean
    inverse = lax.rsqrt(jnp.mean(centred * centred, axis=-1, keepdims=True) + 1e-06)
    return (centred * inverse, inverse)


def norm_backward(gradient, normed, inverse):
    return inverse * (
        gradient
        - jnp.mean(gradient, axis=-1, keepdims=True)
        - normed * jnp.mean(gradient * normed, axis=-1, keepdims=True)
    )


def head_window(head, head_size, width):
    tile = jnp.minimum((head * head_size) // 128, width // 128 - 2)
    base = pl.multiple_of(tile * 128, 128)
    lane = lax.broadcasted_iota(jnp.int32, (1, 256), 1) + (base - head * head_size)
    return base, (lane >= 0) & (lane < head_size)


def as_row(column):
    return jnp.transpose(jnp.broadcast_to(column, (column.shape[0], 128)))[0:1]


def attend_forward_kernel(
    keep_ref, query_ref, key_ref, value_ref, out_ref, lse_ref, *, head_size, width, rows
):
    query_ref, key_ref, value_ref = query_ref.at[0], key_ref.at[0], value_ref.at[0]
    head = pl.program_id(0)
    base, mask = head_window(head, head_size, width)
    scale = head_size**-0.5 * LOG2E
    zero = jnp.zeros((), jnp.bfloat16)
    window = (slice(None), pl.ds(base, 256))
    keys = key_ref[window]
    values = value_ref[window]
    keep = keep_ref[head].astype(jnp.float32)
    for start in range(0, query_ref.shape[0], rows):
        block = (pl.ds(start, rows), pl.ds(base, 256))
        query = jnp.where(mask, query_ref[block], zero)
        scores = matmul(query, keys, ROWS_NT)
        top = jnp.max(scores, axis=-1, keepdims=True)
        probs = jnp.exp2((scores - top) * scale)
        total = jnp.sum(probs, axis=-1, keepdims=True)
        mixed = matmul(probs.astype(jnp.bfloat16), values, ROWS_NN)
        mixed = (mixed * (keep / total)).astype(jnp.bfloat16)
        out_ref[block] = jnp.where(mask, mixed, out_ref[block])
        lse_ref[pl.ds(head, 1), pl.ds(start, rows)] = as_row(top * scale + jnp.log2(total))


def attend_backward_kernel(
    keep_ref,
    query_ref,
    key_ref,
    value_ref,
    out_ref,
    grad_ref,
    lse_ref,
    grads_ref,
    *,
    head_size,
    width,
    rows,
):
    query_ref, key_ref, value_ref = query_ref.at[0], key_ref.at[0], value_ref.at[0]
    dquery_ref, dkey_ref, dvalue_ref = grads_ref.at[0], grads_ref.at[1], grads_ref.at[2]
    head = pl.program_id(0)
    base, mask = head_window(head, head_size, width)
    scale = head_size**-0.5
    zero = jnp.zeros((), jnp.bfloat16)
    length = query_ref.shape[0]
    window = (slice(None), pl.ds(base, 256))
    keys = key_ref[window]
    values = value_ref[window]
    keys_across = jnp.transpose(keys)
    key_grad = jnp.zeros((length, 256), jnp.float32)
    value_grad = jnp.zeros((length, 256), jnp.float32)
    kept = mask & (keep_ref[head] > 0)
    for start in range(0, length, rows):
        block = (pl.ds(start, rows), pl.ds(base, 256))
        query = jnp.where(mask, query_ref[block], zero)
        grad = jnp.where(kept, grad_ref[block], zero)
        row_dot = as_row(
            jnp.sum(
                grad.astype(jnp.float32) * out_ref[block].astype(jnp.float32), axis=-1, keepdims=True
            )
        )
        lse = lse_ref[pl.ds(head, 1), pl.ds(start, rows)]
        probs = jnp.exp2(matmul(keys, query, ROWS_NT) * (scale * LOG2E) - lse)
        score_grad = (probs * (matmul(values, grad, ROWS_NT) - row_dot)).astype(jnp.bfloat16)
        value_grad = value_grad + matmul(probs.astype(jnp.bfloat16), grad, ROWS_NN)
        key_grad = key_grad + matmul(score_grad, query, ROWS_NN)
        query_grad = jnp.transpose(matmul(keys_across, score_grad, ROWS_NN)) * scale
        dquery_ref[block] = jnp.where(mask, query_grad.astype(jnp.bfloat16), dquery_ref[block])
    dkey_ref[window] = jnp.where(mask, (key_grad * scale).astype(jnp.bfloat16), dkey_ref[window])
    dvalue_ref[window] = jnp.where(mask, value_grad.astype(jnp.bfloat16), dvalue_ref[window])


def whole(shape):
    return pl.BlockSpec(shape, lambda *_: (0,) * len(shape), pipeline_mode=pl.Buffered(1))


def one_of(index, length, width):
    return pl.BlockSpec(
        (1, length, width), lambda head: (index, 0, 0), pipeline_mode=pl.Buffered(1)
    )


def attend_forward(qkv, keep, rows=512):
    _, length, width = qkv.shape
    heads = keep.shape[0]
    cells = heads * length * length
    return pl.pallas_call(
        functools.partial(
            attend_forward_kernel, head_size=width // heads, width=width, rows=min(rows, length)
        ),
        grid=(heads,),
        in_specs=[pl.BlockSpec(memory_space=pltpu.SMEM)]
        + [one_of(i, length, width) for i in range(3)],
        out_specs=[
            pl.BlockSpec((length, width), lambda head: (0, 0)),
            pl.BlockSpec((heads, length), lambda head: (0, 0)),
        ],
        out_shape=[
            jax.ShapeDtypeStruct((length, width), jnp.bfloat16),
            jax.ShapeDtypeStruct((heads, length), jnp.float32),
        ],
        compiler_params=pltpu.CompilerParams(vmem_limit_bytes=48 << 20),
        cost_estimate=pl.CostEstimate(
            flops=cells * 1024, transcendentals=cells, bytes_accessed=length * width * 8
        ),
        name="attend_forward",
    )(keep, qkv, qkv, qkv)


def attend_backward(qkv, out, grad, lse, keep, rows=256):
    _, length, width = qkv.shape
    heads = keep.shape[0]
    cells = heads * length * length
    return pl.pallas_call(
        functools.partial(
            attend_backward_kernel, head_size=width // heads, width=width, rows=min(rows, length)
        ),
        grid=(heads,),
        in_specs=[pl.BlockSpec(memory_space=pltpu.SMEM)]
        + [one_of(i, length, width) for i in range(3)]
        + [whole((length, width))] * 2
        + [whole((heads, length))],
        out_specs=pl.BlockSpec((3, length, width), lambda head: (0, 0, 0)),
        out_shape=jax.ShapeDtypeStruct((3, length, width), jnp.bfloat16),
        compiler_params=pltpu.CompilerParams(vmem_limit_bytes=56 << 20),
        cost_estimate=pl.CostEstimate(
            flops=cells * 2560, transcendentals=cells, bytes_accessed=length * width * 16
        ),
        name="attend_backward",
    )(keep, qkv, qkv, qkv, out, grad, lse)


ROWS_TN = (((0,), (0,)), ((), ()))
ANY = pl.BlockSpec(memory_space=pl.ANY)


class Blocks(list):
    def __init__(self, arrays, order):
        super().__init__(arrays)
        self.order = order

    def block(self, r, x_r, z_r):
        y_r, core_r = r // 2, r % 2
        first_r, second_r = (x_r, y_r) if self.order == "xy" else (y_r, x_r)
        return self[2 * core_r + second_r].at[first_r, z_r]


def square_copies(place, sets, r, target, sem):
    part = jnp.bitwise_xor(place[2], r)
    if len(sets[0]) == 1:
        return [pltpu.make_async_copy(sets[0][0].at[part], target, sem)]
    copies, column = [], 0
    for refs in sets:
        rows, columns = refs[0].shape[2:]
        for x_r in range(2):
            for z_r in range(4):
                shard = (place[0] + z_r) % 4 * 2 + (place[1] + x_r) % 2
                block = (pl.ds(pl.multiple_of(shard * rows, 16), rows), pl.ds(column, columns))
                source = refs.block(r, x_r, z_r)
                copies.append(pltpu.make_async_copy(source, target.at[block], sem))
        column += columns
    return copies


def strip_copies(place, refs, chunk, target, sem):
    if len(refs) == 1:
        return [pltpu.make_async_copy(refs[0].at[chunk], target, sem)]
    rows = refs[0].shape[2]
    copies = []
    for core_r in range(2):
        for y in range(2):
            part = 2 * y + (place[2] + core_r) % 2
            for x in range(2):
                start = pl.multiple_of(x * (4 * rows) + part * rows, 16)
                source = refs[core_r].at[2 * chunk + x, y]
                copies.append(pltpu.make_async_copy(source, target.at[pl.ds(start, rows)], sem))
    return copies


def square_stores(place, outs, r, source, sem):
    part = jnp.bitwise_xor(place[2], r)
    if len(outs) == 1:
        return [pltpu.make_async_copy(source, outs[0].at[part], sem)]
    copies, column = [], 0
    for pair in range(0, len(outs), 2):
        out = outs[pair + r % 2]
        out = out if len(out.shape) == 4 else out.at[r // 2]
        rows, columns = out.shape[2:]
        for shard in range(8):
            x_r, z_r = (place[1] + shard % 2) % 2, (shard // 2 + 4 - place[0]) % 4
            block = source.at[pl.ds(shard * rows, rows), pl.ds(column, columns)]
            copies.append(pltpu.make_async_copy(block, out.at[x_r, z_r], sem))
        column += columns
    return copies


def strip_stores(place, outs, chunk, source, sem):
    if len(outs) == 1:
        return [pltpu.make_async_copy(source, outs[0].at[chunk], sem)]
    rows = outs[0].shape[3]
    z_r = (chunk + 4 - place[0]) % 4
    copies = []
    for r in range(4):
        part = jnp.bitwise_xor(place[2], r)
        for x in range(2):
            block = source.at[pl.ds(pl.multiple_of(x * (4 * rows) + part * rows, 16), rows)]
            x_r = (place[1] + x) % 2
            copies.append(pltpu.make_async_copy(block, outs[r % 2].at[r // 2, x_r, z_r], sem))
    return copies


def in_sets(refs, sets):
    refs, found = list(refs), []
    for entry in sets:
        found.append(Blocks(refs[: len(entry)], entry.order))
        refs = refs[len(entry) :]
    return found


def flat(sets):
    return [array for entry in sets for array in entry]


def start_all(copies):
    for copy in copies:
        copy.start()


def wait_all(copies):
    for copy in copies:
        copy.wait()


def for_each(step, action):
    for r in range(4):

        @pl.when(step == r)
        def _(r=r):
            action(r)


def fetch_squares(place, sets, step, held, sems):
    @pl.when(step == 0)
    def _():
        start_all(square_copies(place, sets, 0, held.at[0], sems.at[0]))

    for_each(
        step + 1,
        lambda r: start_all(square_copies(place, sets, r, held.at[r % 2], sems.at[r % 2])),
    )
    for_each(
        step, lambda r: wait_all(square_copies(place, sets, r, held.at[r % 2], sems.at[r % 2]))
    )


def tiles(length, rows=256):
    return [pl.ds(start, min(rows, length)) for start in range(0, length, min(rows, length))]


def prepare_kernel(
    tokens_ref, cotangent_ref, parts_ref, mod_ref, across_ref, grad_ref, sum_ref, rows_ref
):
    width = tokens_ref.shape[1]

    @pl.when(pl.program_id(0) == 0)
    def _():
        for row in range(parts_ref.shape[1] // width):
            part = parts_ref[:, row * width : (row + 1) * width]
            rows_ref[row : row + 1] = jnp.sum(part, axis=0, keepdims=True)
        sum_ref[...] = jnp.zeros_like(sum_ref)

    normed, _ = norm_forward(tokens_ref[...].astype(jnp.float32))
    mod = normed * (1.0 + row_of(rows_ref, SCALE_ATTN)) + row_of(rows_ref, SHIFT_ATTN)
    mod_ref[...] = mod.astype(jnp.bfloat16)
    across_ref[...] = jnp.transpose(mod).astype(jnp.bfloat16)
    grad = (cotangent_ref[...].astype(jnp.float32) * row_of(rows_ref, GATE_MLP)).astype(jnp.bfloat16)
    grad_ref[...] = grad
    sum_ref[0:1] += jnp.sum(grad.astype(jnp.float32), axis=0, keepdims=True)


def prepare(tokens, cotangent, parts, tile=256):
    length, width = tokens.shape
    tile = min(tile, length)
    by_rows = pl.BlockSpec((tile, width), lambda step: (step, 0))
    fixed = pl.BlockSpec((8, width), lambda step: (0, 0))
    table = (16, width)
    return pl.pallas_call(
        prepare_kernel,
        grid=(length // tile,),
        in_specs=[by_rows, by_rows, pl.BlockSpec(parts.shape, lambda step: (0, 0))],
        out_specs=[
            by_rows,
            pl.BlockSpec((width, tile), lambda step: (0, step)),
            by_rows,
            fixed,
            pl.BlockSpec(table, lambda step: (0, 0)),
        ],
        out_shape=[
            jax.ShapeDtypeStruct((length, width), jnp.bfloat16),
            jax.ShapeDtypeStruct((width, length), jnp.bfloat16),
            jax.ShapeDtypeStruct((length, width), jnp.bfloat16),
            jax.ShapeDtypeStruct((8, width), jnp.float32),
            jax.ShapeDtypeStruct(table, jnp.float32),
        ],
        compiler_params=vmem_params(),
        cost_estimate=cost(20 * length * width, 10 * length * width),
        name="prepare",
    )(tokens, cotangent, parts)


def project_kernel(place, mod_ref, rows_ref, *rest, sets):
    *refs, out_ref, held, sems = rest
    step = pl.program_id(0)
    fetch_squares(place, in_sets(refs, sets), step, held, sems)
    part = jnp.bitwise_xor(place[2], step)

    @pl.when(part < 3)
    def _():
        weight = held[step % 2]
        bias = rows_ref[pl.ds(QUERY_BIAS + part // 2, 1)] * (part != 1).astype(jnp.float32)
        for tile in tiles(mod_ref.shape[0]):
            out_ref[0, tile] = (matmul(mod_ref[tile], weight, ROWS_NN) + bias).astype(jnp.bfloat16)


def vmem_params(mebibytes=56):
    return pltpu.CompilerParams(
        vmem_limit_bytes=mebibytes << 20, dimension_semantics=("arbitrary",)
    )


def cost(flops, moved):
    return pl.CostEstimate(flops=1, transcendentals=0, bytes_accessed=1)


def project(place, mod, rows, squares):
    length, width = mod.shape
    return pl.pallas_call(
        functools.partial(project_kernel, sets=squares),
        grid_spec=pltpu.PrefetchScalarGridSpec(
            num_scalar_prefetch=1,
            grid=(4,),
            in_specs=[
                pl.BlockSpec((length, width), lambda step, place: (0, 0)),
                pl.BlockSpec(rows.shape, lambda step, place: (0, 0)),
            ]
            + [ANY] * len(flat(squares)),
            out_specs=pl.BlockSpec(
                (1, length, width), lambda step, place: (jnp.bitwise_xor(place[2], step), 0, 0)
            ),
            scratch_shapes=[
                pltpu.VMEM((2, width, width), jnp.bfloat16),
                pltpu.SemaphoreType.DMA((2,)),
            ],
        ),
        out_shape=jax.ShapeDtypeStruct((4, length, width), jnp.bfloat16),
        compiler_params=vmem_params(),
        cost_estimate=cost(6 * length * width * width, 14 * length * width),
        name="project",
    )(place, mod, rows, *flat(squares))


def fetch_part(place, sets, wanted, target, sem):
    part = jnp.bitwise_xor(place[2], wanted)
    for_each(part, lambda r: start_all(square_copies(place, sets, r, target, sem)))
    for_each(part, lambda r: wait_all(square_copies(place, sets, r, target, sem)))


def row_of(rows_ref, index):
    return rows_ref[index : index + 1]


SHIFT_ATTN, SCALE_ATTN, GATE_ATTN, SHIFT_MLP, SCALE_MLP, GATE_MLP = range(6)
QUERY_BIAS, VALUE_BIAS, OUT_BIAS, UP_BIAS, DOWN_BIAS = 6, 7, 8, 9, 13


def after_attention_kernel(place, low_ref, tokens_ref, rows_ref, *rest, sets):
    *refs, branch_ref, middle_ref, mod_ref, across_ref, weight, sem = rest

    @pl.when(pl.program_id(0) == 0)
    def _():
        fetch_part(place, in_sets(refs, sets), 3, weight, sem)

    branch = matmul(low_ref[...], weight[...], ROWS_NN) + row_of(rows_ref, OUT_BIAS)
    middle = tokens_ref[...].astype(jnp.float32) + row_of(rows_ref, GATE_ATTN) * branch
    normed, _ = norm_forward(middle)
    mod = normed * (1.0 + row_of(rows_ref, SCALE_MLP)) + row_of(rows_ref, SHIFT_MLP)
    branch_ref[...] = branch
    middle_ref[...] = middle
    mod_ref[...] = mod.astype(jnp.bfloat16)
    across_ref[...] = jnp.transpose(mod).astype(jnp.bfloat16)


def after_attention(place, low, tokens, rows, squares, tile=256):
    length, width = low.shape
    tile = min(tile, length)
    by_rows = pl.BlockSpec((tile, width), lambda step, place: (step, 0))
    return pl.pallas_call(
        functools.partial(after_attention_kernel, sets=squares),
        grid_spec=pltpu.PrefetchScalarGridSpec(
            num_scalar_prefetch=1,
            grid=(length // tile,),
            in_specs=[by_rows, by_rows, pl.BlockSpec(rows.shape, lambda step, place: (0, 0))]
            + [ANY] * len(flat(squares)),
            out_specs=[by_rows] * 3 + [pl.BlockSpec((width, tile), lambda step, place: (0, step))],
            scratch_shapes=[pltpu.VMEM((width, width), jnp.bfloat16), pltpu.SemaphoreType.DMA],
        ),
        out_shape=[
            jax.ShapeDtypeStruct((length, width), jnp.float32),
            jax.ShapeDtypeStruct((length, width), jnp.float32),
            jax.ShapeDtypeStruct((length, width), jnp.bfloat16),
            jax.ShapeDtypeStruct((width, length), jnp.bfloat16),
        ],
        compiler_params=vmem_params(),
        cost_estimate=cost(2 * length * width * width, 18 * length * width),
        name="after_attention",
    )(place, low, tokens, rows, *flat(squares))


ROOT = 0.7978845608028654


def gelu_and_slope(values):
    square = values * values
    bend = jnp.tanh(values * (ROOT + (ROOT * 0.044715) * square))
    half = 0.5 + 0.5 * bend
    slope = half + (0.5 * values) * (1.0 - bend * bend) * (ROOT + (3 * 0.044715 * ROOT) * square)
    return values * half, slope


def mlp_kernel(place, mod_ref, across_ref, grad_ref, rows_ref, keep_ref, *rest, ups, downs):
    count = len(flat(ups)) + downs
    refs, rest = rest[:count], rest[count:]
    up_sets, down_refs = in_sets(refs, ups), refs[-downs:]
    branch_ref, dmod_ref, dbias_ref = rest[:3]
    *stores, act, dpre, up, down, up_out, down_out, in_sems, out_sems = rest[3:]
    up_stores, down_stores = stores[: len(stores) // 2], stores[len(stores) // 2 :]
    step = pl.program_id(0)
    length = mod_ref.shape[0]

    def chunk_of(r):
        return jnp.bitwise_xor(place[2], r)

    def fetch(r):
        slot = r % 2
        return square_copies(place, up_sets, r, up.at[slot], in_sems.at[slot, 0]) + strip_copies(
            place, down_refs, chunk_of(r), down.at[slot], in_sems.at[slot, 1]
        )

    @pl.when(step == 0)
    def _():
        start_all(fetch(0))
        branch_ref[...] = jnp.zeros_like(branch_ref)
        dmod_ref[...] = jnp.zeros_like(dmod_ref)

    for_each(step + 1, lambda r: start_all(fetch(r)))
    for_each(step, lambda r: wait_all(fetch(r)))
    chunk = chunk_of(step)
    slot = step % 2
    bias = rows_ref[pl.ds(UP_BIAS + chunk, 1)]
    keep = keep_ref[pl.ds(chunk, 1)]
    total = jnp.zeros_like(bias)
    for tile in tiles(length, 512):
        gelu, slope = gelu_and_slope(matmul(mod_ref[tile], up[slot], ROWS_NN) + bias)
        act[tile] = (gelu * keep).astype(jnp.bfloat16)
        back = matmul(grad_ref[tile], down[slot], ROWS_NT)
        low = (slope * keep * back).astype(jnp.bfloat16)
        dpre[tile] = low
        total = total + jnp.sum(low.astype(jnp.float32), axis=0, keepdims=True)
        branch_ref[tile] += matmul(act[tile], down[slot], ROWS_NN)
        dmod_ref[tile] += matmul(low, up[slot], ROWS_NT)
    dbias_ref[pl.ds(chunk, 1)] = total

    def leave(r):
        return square_stores(place, up_stores, r, up_out, out_sems.at[0]), strip_stores(
            place, down_stores, chunk_of(r), down_out, out_sems.at[1]
        )

    for_each(step - 1, lambda r: wait_all(leave(r)[0]))
    up_out[...] = matmul(across_ref[...], dpre[...], ROWS_NN).astype(jnp.bfloat16)
    for_each(step, lambda r: start_all(leave(r)[0]))
    for_each(step - 1, lambda r: wait_all(leave(r)[1]))
    down_out[...] = matmul(act[...], grad_ref[...], ROWS_TN).astype(jnp.bfloat16)
    for_each(step, lambda r: start_all(leave(r)[1]))

    @pl.when(step == 3)
    def _():
        wait_all(leave(3)[0])
        wait_all(leave(3)[1])


def gradient_shapes(paired, rows, columns):
    if paired:
        return [
            jax.ShapeDtypeStruct((2, 2, 4, rows, count), jnp.bfloat16)
            for count in columns
            for _ in range(2)
        ]
    return [jax.ShapeDtypeStruct((4, sum(columns), sum(columns)), jnp.bfloat16)]


def mlp(place, mod, across, grad, rows, keep, ups, downs, block_rows):
    length, width = mod.shape
    stores = gradient_shapes(len(downs) > 1, block_rows, [width])
    quarter = jax.ShapeDtypeStruct((4, width), jnp.float32)
    table = pl.BlockSpec((4, width), lambda step, place: (0, 0))
    held = pl.BlockSpec((length, width), lambda step, place: (0, 0), pipeline_mode=pl.Buffered(1))
    square = pltpu.VMEM((width, width), jnp.bfloat16)
    pair = pltpu.VMEM((2, width, width), jnp.bfloat16)
    tall = pltpu.VMEM((length, width), jnp.bfloat16)
    wide = pl.BlockSpec((length, width), lambda step, place: (0, 0))
    return pl.pallas_call(
        functools.partial(mlp_kernel, ups=ups, downs=len(downs)),
        grid_spec=pltpu.PrefetchScalarGridSpec(
            num_scalar_prefetch=1,
            grid=(4,),
            in_specs=[
                held,
                pl.BlockSpec((width, length), lambda step, place: (0, 0), pipeline_mode=pl.Buffered(1)),
                held,
                pl.BlockSpec(rows.shape, lambda step, place: (0, 0)),
                table,
            ]
            + [ANY] * (len(flat(ups)) + len(downs)),
            out_specs=[wide, wide, table] + [ANY] * (2 * len(stores)),
            scratch_shapes=[
                tall,
                tall,
                pair,
                pair,
                square,
                square,
                pltpu.SemaphoreType.DMA((2, 2)),
                pltpu.SemaphoreType.DMA((2,)),
            ],
        ),
        out_shape=[jax.ShapeDtypeStruct((length, width), jnp.float32)] * 2
        + [quarter]
        + stores
        + stores,
        compiler_params=vmem_params(60),
        cost_estimate=cost(48 * length * width * width, 32 * width * width),
        name="mlp",
    )(place, mod, across, grad, rows, keep, *flat(ups), *downs)


def after_mlp_kernel(
    place, dmod_ref, middle_ref, cotangent_ref, rows_ref, *rest, sets
):
    *refs, dmiddle_ref, dbranch_ref, dlow_ref, sums_ref, weight, sem = rest

    @pl.when(pl.program_id(0) == 0)
    def _():
        fetch_part(place, in_sets(refs, sets), 3, weight, sem)
        sums_ref[...] = jnp.zeros_like(sums_ref)

    normed, inverse = norm_forward(middle_ref[...])
    dmod = dmod_ref[...]
    dmiddle = cotangent_ref[...].astype(jnp.float32) + norm_backward(
        dmod * (1.0 + row_of(rows_ref, SCALE_MLP)), normed, inverse
    )
    dmiddle_ref[...] = dmiddle
    low = (dmiddle * row_of(rows_ref, GATE_ATTN)).astype(jnp.bfloat16)
    dbranch_ref[...] = low
    dlow_ref[...] = matmul(low, weight[...], ROWS_NT).astype(jnp.bfloat16)
    sums_ref[0:1] += jnp.sum(dmod * normed, axis=0, keepdims=True)
    sums_ref[1:2] += jnp.sum(dmod, axis=0, keepdims=True)
    sums_ref[2:3] += jnp.sum(low.astype(jnp.float32), axis=0, keepdims=True)


def after_mlp(place, dmod, middle, cotangent, rows, squares, tile=256):
    length, width = middle.shape
    tile = min(tile, length)
    by_rows = pl.BlockSpec((tile, width), lambda step, place: (step, 0))
    fixed = lambda shape: pl.BlockSpec(shape, lambda step, place: (0, 0))
    return pl.pallas_call(
        functools.partial(after_mlp_kernel, sets=squares),
        grid_spec=pltpu.PrefetchScalarGridSpec(
            num_scalar_prefetch=1,
            grid=(length // tile,),
            in_specs=[by_rows] * 3 + [fixed(rows.shape)] + [ANY] * len(flat(squares)),
            out_specs=[by_rows] * 3 + [fixed((8, width))],
            scratch_shapes=[pltpu.VMEM((width, width), jnp.bfloat16), pltpu.SemaphoreType.DMA],
        ),
        out_shape=[
            jax.ShapeDtypeStruct((length, width), jnp.float32),
            jax.ShapeDtypeStruct((length, width), jnp.bfloat16),
            jax.ShapeDtypeStruct((length, width), jnp.bfloat16),
            jax.ShapeDtypeStruct((8, width), jnp.float32),
        ],
        compiler_params=vmem_params(),
        cost_estimate=cost(2 * length * width * width, 20 * length * width),
        name="after_mlp",
    )(place, dmod, middle, cotangent, rows, *flat(squares))


def finish_kernel(
    mlp_ref, middle_ref, branch_ref, dmiddle_ref, cotangent_ref, rows_ref, out_ref, sums_ref
):
    @pl.when(pl.program_id(0) == 0)
    def _():
        sums_ref[...] = jnp.zeros_like(sums_ref)

    mlp_branch = mlp_ref[...] + row_of(rows_ref, DOWN_BIAS)
    out_ref[...] = (middle_ref[...] + row_of(rows_ref, GATE_MLP) * mlp_branch).astype(jnp.bfloat16)
    grad = cotangent_ref[...].astype(jnp.float32) * mlp_branch
    sums_ref[0:1] += jnp.sum(grad, axis=0, keepdims=True)
    sums_ref[1:2] += jnp.sum(dmiddle_ref[...] * branch_ref[...], axis=0, keepdims=True)


def finish(branch_mlp, middle, branch, dmiddle, cotangent, rows, tile=256):
    length, width = middle.shape
    tile = min(tile, length)
    by_rows = pl.BlockSpec((tile, width), lambda step: (step, 0))
    return pl.pallas_call(
        finish_kernel,
        grid=(length // tile,),
        in_specs=[by_rows] * 5 + [pl.BlockSpec(rows.shape, lambda step: (0, 0))],
        out_specs=[by_rows, pl.BlockSpec((8, width), lambda step: (0, 0))],
        out_shape=[
            jax.ShapeDtypeStruct((length, width), jnp.bfloat16),
            jax.ShapeDtypeStruct((8, width), jnp.float32),
        ],
        compiler_params=vmem_params(),
        cost_estimate=cost(8 * length * width, 20 * length * width),
        name="finish",
    )(branch_mlp, middle, branch, dmiddle, cotangent, rows)


def square_grads_kernel(place, across_ref, grads_ref, low_ref, dbranch_ref, *rest):
    *stores, staged, sems = rest
    step = pl.program_id(0)
    part = jnp.bitwise_xor(place[2], step)

    def leave(r):
        return square_stores(place, stores, r, staged.at[r % 2], sems.at[r % 2])

    for_each(step - 2, lambda r: wait_all(leave(r)))

    @pl.when(part < 3)
    def _():
        staged[step % 2] = matmul(across_ref[...], grads_ref[0], ROWS_NN).astype(jnp.bfloat16)

    @pl.when(part == 3)
    def _():
        staged[step % 2] = matmul(low_ref[...], dbranch_ref[...], ROWS_TN).astype(jnp.bfloat16)

    for_each(step, lambda r: start_all(leave(r)))

    @pl.when(step == 3)
    def _():
        wait_all(leave(2))
        wait_all(leave(3))


def square_grads(place, across, grads, low, dbranch, paired, block_rows, columns):
    width, length = across.shape
    stores = gradient_shapes(paired, block_rows, columns)
    held = pl.BlockSpec((length, width), lambda step, place: (0, 0), pipeline_mode=pl.Buffered(1))
    return pl.pallas_call(
        square_grads_kernel,
        grid_spec=pltpu.PrefetchScalarGridSpec(
            num_scalar_prefetch=1,
            grid=(4,),
            in_specs=[
                pl.BlockSpec((width, length), lambda step, place: (0, 0), pipeline_mode=pl.Buffered(1)),
                pl.BlockSpec(
                    (1, length, width),
                    lambda step, place: (jnp.minimum(jnp.bitwise_xor(place[2], step), 2), 0, 0),
                ),
                held,
                held,
            ],
            out_specs=[ANY] * len(stores),
            scratch_shapes=[
                pltpu.VMEM((2, width, width), jnp.bfloat16),
                pltpu.SemaphoreType.DMA((2,)),
            ],
        ),
        out_shape=stores,
        compiler_params=vmem_params(),
        cost_estimate=cost(8 * length * width * width, 20 * length * width),
        name="square_grads",
    )(place, across, grads, low, dbranch)


def tokens_back_kernel(place, grads_ref, tokens_ref, dmiddle_ref, rows_ref, *rest, sets):
    *refs, out_ref, sums_ref, dmod, held, sems = rest
    step = pl.program_id(0)
    fetch_squares(place, in_sets(refs, sets), step, held, sems)
    part = jnp.bitwise_xor(place[2], step)
    length = tokens_ref.shape[0]

    @pl.when(step == 0)
    def _():
        dmod[...] = jnp.zeros_like(dmod)

    @pl.when(part < 3)
    def _():
        for tile in tiles(length):
            dmod[tile] += matmul(grads_ref[0, tile], held[step % 2], ROWS_NT)
        total = jnp.sum(grads_ref[0].astype(jnp.float32), axis=0, keepdims=True)
        sums_ref[pl.ds(2 + part, 1)] = total

    @pl.when(step == 3)
    def _():
        shift = jnp.zeros((1, dmod.shape[1]), jnp.float32)
        scale = shift
        for tile in tiles(length):
            back = dmod[tile]
            normed, inverse = norm_forward(tokens_ref[tile].astype(jnp.float32))
            scale = scale + jnp.sum(back * normed, axis=0, keepdims=True)
            shift = shift + jnp.sum(back, axis=0, keepdims=True)
            back = norm_backward(back * (1.0 + row_of(rows_ref, SCALE_ATTN)), normed, inverse)
            out_ref[tile] = (dmiddle_ref[tile] + back).astype(jnp.bfloat16)
        sums_ref[0:1] = shift
        sums_ref[1:2] = scale


def tokens_back(place, grads, tokens, dmiddle, rows, squares):
    length, width = tokens.shape
    held = pl.BlockSpec((length, width), lambda step, place: (0, 0), pipeline_mode=pl.Buffered(1))
    return pl.pallas_call(
        functools.partial(tokens_back_kernel, sets=squares),
        grid_spec=pltpu.PrefetchScalarGridSpec(
            num_scalar_prefetch=1,
            grid=(4,),
            in_specs=[
                pl.BlockSpec(
                    (1, length, width),
                    lambda step, place: (jnp.minimum(jnp.bitwise_xor(place[2], step), 2), 0, 0),
                ),
                held,
                held,
                pl.BlockSpec(rows.shape, lambda step, place: (0, 0)),
            ]
            + [ANY] * len(flat(squares)),
            out_specs=[
                pl.BlockSpec((length, width), lambda step, place: (0, 0)),
                pl.BlockSpec((8, width), lambda step, place: (0, 0)),
            ],
            scratch_shapes=[
                pltpu.VMEM((length, width), jnp.float32),
                pltpu.VMEM((2, width, width), jnp.bfloat16),
                pltpu.SemaphoreType.DMA((2,)),
            ],
        ),
        out_shape=[
            jax.ShapeDtypeStruct((length, width), jnp.bfloat16),
            jax.ShapeDtypeStruct((8, width), jnp.float32),
        ],
        compiler_params=vmem_params(),
        cost_estimate=cost(6 * length * width * width, 20 * length * width),
        name="tokens_back",
    )(place, grads, tokens, dmiddle, rows, *flat(squares))


def gather_rows(rows, axis, size):
    place = lax.axis_index(axis)
    step = 1
    while step < size:
        other = lax.ppermute(rows, axis, [(i, i ^ step) for i in range(size)])
        high = (place // step) % 2 == 1
        rows = jnp.concatenate([jnp.where(high, other, rows), jnp.where(high, rows, other)], axis=0)
        step *= 2
    return rows


def swap(value, axis, size, step):
    return lax.ppermute(value, axis, [(i, i ^ step) for i in range(size)])


def both(value, axis, size, step, dim):
    other = swap(value, axis, size, step)
    first = lax.axis_index(axis) // step % 2 == 0
    return jnp.stack([jnp.where(first, value, other), jnp.where(first, other, value)], axis=dim)


def barrier(values):
    return lax.optimization_barrier(values)


def after(value, *others):
    return barrier((value, others))[0]


def add(*terms):
    return sum(term.astype(jnp.float32) for term in terms).astype(jnp.bfloat16)


class Pairwise:
    def __init__(self, shards, group):
        self.shards, self.group = shards, group

    def partner(self, value, kind):
        if kind == "x":
            return swap(value, "fsdp", self.shards, 1)
        return swap(value, "dp", self.group, 2 if kind == "y" else 1)

    def corners(self, block):
        size = self.shards * self.group
        x, y, far = [
            lax.ppermute(block, ("fsdp", "dp"), [(i, i ^ step) for i in range(size)])
            for step in (self.group, 2, self.group + 2)
        ]
        return jnp.stack([jnp.stack([block, x]), jnp.stack([y, far])])

    def ahead(self, value, count):
        pairs = [((target // 2 + count) % 4 * 2 + target % 2, target) for target in range(8)]
        return lax.ppermute(value, "fsdp", pairs)

    def along_z(self, block):
        return jnp.stack([block] + [self.ahead(block, count) for count in (1, 2, 3)])

    def pair(self, block, kind):
        return jnp.stack([block, self.partner(block, kind)])

    def first_sum(self, kept, other, kind):
        dim = 0 if kind == "y" else 1
        stay, go = [
            [lax.index_in_dim(half, i, dim, keepdims=False) for half in (kept, other)] for i in (0, 1)
        ]
        return add(*go), stay

    def second_sum(self, stay, back):
        return add(stay[0][1], stay[1][1], back[1]), add(stay[0][0], stay[1][0], back[0])

    def send_z(self, mine):
        return [self.ahead(mine[count], 4 - count) for count in (1, 2, 3)]

    def to_group(self, part):
        parts = both(both(part, "dp", self.group, 2, 0), "dp", self.group, 1, 1)
        return parts.reshape(4, *part.shape)


def reduce_all(grad):
    shard = lax.psum_scatter(grad, "fsdp", scatter_dimension=0, tiled=True)
    return lax.psum(shard, "dp").astype(jnp.float32)


def reduce_columns(parts):
    _, rows, width = parts.shape
    shard = reduce_all(parts.swapaxes(0, 1).reshape(rows, 4 * width))
    return [shard[:, i * width : (i + 1) * width] for i in range(4)]


def conditioning(times, labels, table, shard, width):
    class_count, columns = table.shape
    half = width // 2
    column = shard * columns + jnp.arange(columns, dtype=jnp.int32)
    frequency = jnp.exp(-math.log(10000.0) * (column % half).astype(jnp.float32) / half)
    angles = times.astype(jnp.float32)[:, None] * frequency[None, :]
    embed = jnp.where(column[None, :] < half, jnp.cos(angles), jnp.sin(angles))
    picked = labels[:, None] == jnp.arange(class_count, dtype=jnp.int32)[None, :]
    return embed + jnp.dot(
        picked.astype(jnp.bfloat16), table, preferred_element_type=jnp.float32
    )


def own_part(values, shard, size):
    return lax.dynamic_slice_in_dim(values, shard * size, size, axis=values.ndim - 1)


def body(
    shard_count,
    image_count,
    tokens,
    timesteps,
    labels,
    head_keep,
    chan_keep,
    cotangent,
    qkv_weight,
    qv_bias,
    out_weight,
    out_bias,
    up_weight,
    up_bias,
    down_weight,
    down_bias,
    ada_weight,
    ada_bias,
    class_table,
):
    _, length, width = tokens.shape
    hidden = chan_keep.shape[1]
    class_count = class_table.shape[0]
    columns = width // shard_count
    group_count = image_count // shard_count
    shard = lax.axis_index("fsdp")
    member = lax.axis_index("dp")
    bf16, f32 = jnp.bfloat16, jnp.float32

    place = jnp.stack([shard // 2, shard % 2, member]).astype(jnp.int32)
    paired = shard_count == 8 and group_count == 4 and columns % 16 == 0
    net = Pairwise(shard_count, group_count)
    splits = [width // 2 // 128 * 128]
    splits.append(width - splits[0])
    four = jnp.concatenate([qkv_weight, out_weight], axis=1)

    fact = jnp.stack([timesteps[0], labels[0]])
    if paired:
        near = net.pair(fact, "x")
        mine = lax.dynamic_slice_in_dim(four, member * width, width, axis=1)
        mine, near = barrier((mine, near))
        near = net.along_z(near)
        square = net.along_z(mine)
        facts = jnp.where(place[1] == 0, near, near[:, ::-1])
        facts = lax.dynamic_slice_in_dim(
            jnp.concatenate([facts, facts]), (4 - place[0]) % 4, 4, axis=0
        ).reshape(8, 2)
    else:
        facts = gather_rows(fact[None], "fsdp", shard_count)
    group_act = jax.nn.silu(
        conditioning(facts[:, 0], facts[:, 1], class_table, shard, width)
    ).astype(bf16)
    partial = jnp.dot(group_act, ada_weight, preferred_element_type=f32)

    def own_columns(values):
        values = values.astype(f32)
        full = jnp.zeros((values.shape[0] * shard_count,), f32)
        return lax.dynamic_update_slice_in_dim(full, values, shard * values.shape[0], axis=0)

    biases = jnp.concatenate(
        [own_columns(values) for values in (qv_bias[0], qv_bias[1], out_bias, up_bias, down_bias)]
    )
    sent = jnp.concatenate(
        [
            partial + own_columns(ada_bias),
            jnp.broadcast_to(biases, (shard_count, biases.shape[0])),
        ],
        axis=1,
    )
    if paired:
        square, sent, near = barrier((square, sent, near))
        parts = lax.all_to_all(sent, "fsdp", 0, 0, tiled=True)
        all_facts = net.pair(net.pair(near.swapaxes(0, 1), "c").swapaxes(0, 1), "y")
        all_facts = all_facts.reshape(image_count, 2)
        first = net.pair(square[:, :, : splits[0]], "x")
        second = net.pair(square[:, :, splits[0] :], "y")
        mine = lax.dynamic_slice_in_dim(up_weight, member * width, width, axis=1)
        down_mine = down_weight.reshape(2, 2, columns, width)
        down_mine = jnp.where(member % 2 == 0, down_mine[:, 0], down_mine[:, 1])
        mine, down_mine, first, second, parts = barrier((mine, down_mine, first, second, parts))
        first_y, second_x = net.partner(first, "y"), net.partner(second, "x")
        up = net.along_z(mine)
        prepared = prepare(tokens[0], cotangent[0], parts)
        first, second, first_y, second_x, up, prepared = barrier(
            (first, second, first_y, second_x, up, prepared)
        )
        down = lax.all_gather(after(down_mine, first_y), "fsdp", axis=0)
        squares = [
            Blocks([first, first_y, net.partner(first, "c"), net.partner(first_y, "c")], "xy"),
            Blocks([second, second_x, net.partner(second, "c"), net.partner(second_x, "c")], "yx"),
        ]
    else:
        parts = lax.all_to_all(sent, "fsdp", 0, 0, tiled=True)
        all_facts = gather_rows(facts, "dp", group_count)
        found = lax.all_gather(four, "fsdp", axis=0, tiled=True)
        squares = [Blocks([found.reshape(width, 4, width).swapaxes(0, 1)], "xy")]
        prepared = prepare(tokens[0], cotangent[0], parts)
    mod_one, mod_across, branch_grad, down_bias_g, rows = prepared
    if paired:
        up_x, up_y = net.partner(up, "x"), net.partner(up, "y")
    qkv = project(place, mod_one, rows, squares)
    if paired:
        qkv, up_x, up_y, all_facts = barrier((qkv, up_x, up_y, all_facts))
        up = jnp.stack([up, up_x])
        up_xy, up_c = net.partner(up_x, "y"), net.partner(up, "c")
    attn_low, lse = attend_forward(qkv, head_keep[0])
    if paired:
        attn_low, up, up_xy, up_c = barrier((attn_low, up, up_xy, up_c))
        up_y = jnp.stack([up_y, up_xy])
        up_y_c = net.partner(up_y, "c")
    attn_branch, middle, mod_two, mod_two_across = after_attention(
        place, attn_low, tokens[0], rows, squares
    )
    if paired:
        mod_two, down, up_y_c = barrier((mod_two, down, up_y_c))
        ups = [Blocks([up, up_y, up_c, up_y_c], "xy")]
        downs = [down, net.partner(down, "c")]
    else:
        found = lax.all_gather(up_weight, "fsdp", axis=0, tiled=True)
        ups = [Blocks([found.reshape(width, 4, width).swapaxes(0, 1)], "xy")]
        found = lax.all_gather(down_weight, "fsdp", axis=0, tiled=True)
        downs = [found.reshape(4, width, width)]
    branch_mlp, mod_two_grad, up_bias_g, *stores = mlp(
        place,
        mod_two,
        mod_two_across,
        branch_grad,
        rows,
        chan_keep.astype(f32).reshape(4, width),
        ups,
        downs,
        columns,
    )
    up_bias_g = up_bias_g.reshape(-1)
    if paired:
        up_kept, up_sent, down_kept, down_sent = stores
        up_other, down_other = net.partner(up_sent, "c"), net.partner(down_sent, "c")
    else:
        up_shard = jnp.concatenate(reduce_columns(stores[0]), axis=1)
        down_shard = reduce_all(stores[1].reshape(hidden, width))
    middle_grad, dbranch, low_grad, sums = after_mlp(
        place, mod_two_grad, middle, cotangent[0], rows, squares
    )
    scale_mlp_grad, shift_mlp_grad, out_bias_g = sums[0], sums[1], sums[2]
    if paired:
        low_grad, up_other, down_other = barrier((low_grad, up_other, down_other))
        up_go, up_stay = net.first_sum(up_kept, up_other, "x")
        down_go, down_stay = net.first_sum(down_kept, down_other, "y")
        low_grad, up_go, down_go = barrier((low_grad, up_go, down_go))
        up_back, down_back = net.partner(up_go, "x"), net.partner(down_go, "y")
    grads = attend_backward(qkv, attn_low, low_grad, lse, head_keep[0])
    if paired:
        grads, up_back, down_back = barrier((grads, up_back, down_back))
        up_go, up_stay = net.second_sum(up_stay, up_back)
        down_go, down_stay = net.second_sum(down_stay, down_back)
        grads, up_go, down_go = barrier((grads, up_go, down_go))
        up_back, down_back = net.partner(up_go, "y"), net.partner(down_go, "x")
    stores = square_grads(
        place, mod_across, grads, attn_low, dbranch, paired, columns, splits
    )
    block_out, gate_sums = finish(branch_mlp, middle, attn_branch, middle_grad, cotangent[0], rows)
    if paired:
        stores, grads, up_back, down_back, block_out, gate_sums = barrier(
            (stores, grads, up_back, down_back, block_out, gate_sums)
        )
        others = [net.partner(sent, "c") for sent in stores[1::2]]
        others = barrier(others)
        goes, stays = zip(
            *[net.first_sum(stores[2 * i], others[i], kind) for i, kind in enumerate("yx")]
        )
        up_mine = add(up_stay, up_back)
        goes, up_mine, grads = barrier((goes, up_mine, grads))
        backs = [net.partner(go, kind) for go, kind in zip(goes, "yx")]
        up_terms = net.send_z(up_mine)
    def small_grads(all_rows):
        cond = conditioning(all_facts[:, 0], all_facts[:, 1], class_table, shard, width)
        cond_act, silu_pull = jax.vjp(jax.nn.silu, cond)
        ada_grad = all_rows[:, : 6 * width]
        ada_weight_g = jnp.einsum(
            "sd,se->de", cond_act.astype(bf16), ada_grad, preferred_element_type=f32
        )
        cond_act_grad = jnp.einsum("se,de->sd", ada_grad, ada_weight, preferred_element_type=f32)
        cond_grad = silu_pull(cond_act_grad)[0]
        picked = all_facts[:, 1][:, None] == jnp.arange(class_count, dtype=jnp.int32)[None, :]
        table_g = jnp.einsum(
            "sc,sd->cd", picked.astype(f32), cond_grad, precision=lax.Precision.HIGHEST
        )
        sums = jnp.sum(all_rows.astype(f32), axis=0)
        ada_bias_g = own_part(sums[: 6 * width], shard, ada_bias.shape[0])
        qv_bias_g = own_part(sums[6 * width : 8 * width].reshape(2, width), shard, columns)
        out_bias_own = own_part(sums[8 * width : 9 * width], shard, columns)
        up_bias_own = own_part(sums[9 * width : 9 * width + hidden], shard, up_bias.shape[0])
        down_bias_own = own_part(sums[9 * width + hidden :], shard, columns)
        return qv_bias_g, out_bias_own, up_bias_own, down_bias_own, ada_weight_g, ada_bias_g, table_g

    tokens_grad, sums = tokens_back(place, grads, tokens[0], middle_grad, rows, squares)
    if paired:
        tokens_grad, sums, backs, up_terms = barrier((tokens_grad, sums, backs, up_terms))
    gate_mlp_grad, gate_attn_grad = gate_sums[0], gate_sums[1]
    row = jnp.concatenate(
        [
            sums[0],
            sums[1],
            gate_attn_grad,
            shift_mlp_grad,
            scale_mlp_grad,
            gate_mlp_grad,
            sums[2],
            sums[4],
            out_bias_g,
            up_bias_g,
            down_bias_g[0],
        ]
    ).astype(bf16)[None]
    if paired:
        down_mine = add(down_stay, down_back)
        goes, stays = zip(*[net.second_sum(stay, back) for stay, back in zip(stays, backs)])
        goes, row, down_mine = barrier((goes, row, down_mine))
        row = net.along_z(row)
        backs = [net.partner(go, kind) for go, kind in zip(goes, "xy")]
        down_terms = net.send_z(down_mine)
        backs, down_terms, row = barrier((backs, down_terms, row))
        mine = jnp.concatenate([add(stay, back) for stay, back in zip(stays, backs)], axis=2)
        part = jnp.stack([add(up_mine[0], *up_terms), add(down_mine[0], *down_terms)])
        mine, part, row = barrier((mine, part, row))
        terms = net.send_z(mine)
        row = net.corners(net.pair(row, "c"))
        mlp_parts = both(part, "dp", group_count, 2, 0)
        terms, row, mlp_parts = barrier((terms, row, mlp_parts))
        small = small_grads(row.reshape(image_count, -1))
        mlp_parts = both(mlp_parts, "dp", group_count, 1, 1).reshape(4, *part.shape)
        parts = net.to_group(add(mine[0], *terms)).astype(f32)
        up_shard = jnp.concatenate([mlp_parts[i, 0] for i in range(4)], axis=1).astype(f32)
        down_shard = mlp_parts[:, 1].reshape(down_weight.shape).astype(f32)
        query_g, key_g, value_g, out_shard = parts
    else:
        query_g, key_g, value_g, out_shard = reduce_columns(stores[0])
        all_rows = gather_rows(gather_rows(row, "fsdp", shard_count), "dp", group_count)
        small = small_grads(all_rows)
    qkv_shard = jnp.concatenate([query_g, key_g, value_g], axis=1)
    (
        qv_bias_g,
        out_bias_g,
        up_bias_g,
        down_bias_g,
        ada_weight_g,
        ada_bias_g,
        table_g,
    ) = small
    return (
        block_out[None],
        tokens_grad[None],
        qkv_shard,
        qv_bias_g,
        out_shard,
        out_bias_g,
        up_shard,
        up_bias_g,
        down_shard,
        down_bias_g,
        ada_weight_g,
        ada_bias_g,
        table_g,
    )


def solution(mesh):
    shard_count = mesh.shape["fsdp"]
    image_count = shard_count * mesh.shape["dp"]
    images = ("fsdp", "dp")
    return jax.shard_map(
        functools.partial(body, shard_count, image_count),
        mesh=mesh,
        in_specs=(
            P(images, None, None),
            P(images),
            P(images),
            P(images, None),
            P(images, None),
            P(images, None, None),
            P("fsdp", None),
            P(None, "fsdp"),
            P("fsdp", None),
            P("fsdp"),
            P("fsdp", None),
            P("fsdp"),
            P("fsdp", None),
            P("fsdp"),
            P("fsdp", None),
            P("fsdp"),
            P(None, "fsdp"),
        ),
        out_specs=(
            P(images, None, None),
            P(images, None, None),
            P("fsdp", None),
            P(None, "fsdp"),
            P("fsdp", None),
            P("fsdp"),
            P("fsdp", None),
            P("fsdp"),
            P("fsdp", None),
            P("fsdp"),
            P("fsdp", None),
            P("fsdp"),
            P(None, "fsdp"),
        ),
        check_vma=False,
    )
```

```python
import functools
import math

import jax
import jax.numpy as jnp
from jax import lax
from jax.experimental import pallas as pl
from jax.experimental.pallas import tpu as pltpu
from jax.sharding import PartitionSpec as P

LOG2E = 1.4426950408889634
ROWS_NT = (((1,), (1,)), ((), ()))
ROWS_NN = (((1,), (0,)), ((), ()))


def matmul(left, right, dims):
    return lax.dot_general(left, right, dims, preferred_element_type=jnp.float32)


def norm_forward(values):
    row_mean = jnp.mean(values, axis=-1, keepdims=True)
    centred = values - row_mean
    inverse = lax.rsqrt(jnp.mean(centred * centred, axis=-1, keepdims=True) + 1e-06)
    return (centred * inverse, inverse)


def norm_backward(gradient, normed, inverse):
    return inverse * (
        gradient
        - jnp.mean(gradient, axis=-1, keepdims=True)
        - normed * jnp.mean(gradient * normed, axis=-1, keepdims=True)
    )


def head_window(head, head_size, width):
    tile = jnp.minimum((head * head_size) // 128, width // 128 - 2)
    base = pl.multiple_of(tile * 128, 128)
    lane = lax.broadcasted_iota(jnp.int32, (1, 256), 1) + (base - head * head_size)
    return base, (lane >= 0) & (lane < head_size)


def as_row(column):
    return jnp.transpose(jnp.broadcast_to(column, (column.shape[0], 128)))[0:1]


def attend_forward_kernel(
    keep_ref, query_ref, key_ref, value_ref, out_ref, lse_ref, *, head_size, width, rows
):
    query_ref, key_ref, value_ref = query_ref.at[0], key_ref.at[0], value_ref.at[0]
    head = pl.program_id(0)
    base, mask = head_window(head, head_size, width)
    scale = head_size**-0.5 * LOG2E
    zero = jnp.zeros((), jnp.bfloat16)
    window = (slice(None), pl.ds(base, 256))
    keys = key_ref[window]
    values = value_ref[window]
    keep = keep_ref[head].astype(jnp.float32)
    for start in range(0, query_ref.shape[0], rows):
        block = (pl.ds(start, rows), pl.ds(base, 256))
        query = jnp.where(mask, query_ref[block], zero)
        scores = matmul(query, keys, ROWS_NT)
        top = jnp.max(scores, axis=-1, keepdims=True)
        probs = jnp.exp2((scores - top) * scale)
        total = jnp.sum(probs, axis=-1, keepdims=True)
        mixed = matmul(probs.astype(jnp.bfloat16), values, ROWS_NN)
        mixed = (mixed * (keep / total)).astype(jnp.bfloat16)
        out_ref[block] = jnp.where(mask, mixed, out_ref[block])
        lse_ref[pl.ds(head, 1), pl.ds(start, rows)] = as_row(top * scale + jnp.log2(total))


def attend_backward_kernel(
    keep_ref,
    query_ref,
    key_ref,
    value_ref,
    out_ref,
    grad_ref,
    lse_ref,
    grads_ref,
    *,
    head_size,
    width,
    rows,
):
    query_ref, key_ref, value_ref = query_ref.at[0], key_ref.at[0], value_ref.at[0]
    dquery_ref, dkey_ref, dvalue_ref = grads_ref.at[0], grads_ref.at[1], grads_ref.at[2]
    head = pl.program_id(0)
    base, mask = head_window(head, head_size, width)
    scale = head_size**-0.5
    zero = jnp.zeros((), jnp.bfloat16)
    length = query_ref.shape[0]
    window = (slice(None), pl.ds(base, 256))
    keys = key_ref[window]
    values = value_ref[window]
    keys_across = jnp.transpose(keys)
    key_grad = jnp.zeros((length, 256), jnp.float32)
    value_grad = jnp.zeros((length, 256), jnp.float32)
    kept = mask & (keep_ref[head] > 0)
    for start in range(0, length, rows):
        block = (pl.ds(start, rows), pl.ds(base, 256))
        query = jnp.where(mask, query_ref[block], zero)
        grad = jnp.where(kept, grad_ref[block], zero)
        row_dot = as_row(
            jnp.sum(
                grad.astype(jnp.float32) * out_ref[block].astype(jnp.float32), axis=-1, keepdims=True
            )
        )
        lse = lse_ref[pl.ds(head, 1), pl.ds(start, rows)]
        probs = jnp.exp2(matmul(keys, query, ROWS_NT) * (scale * LOG2E) - lse)
        score_grad = (probs * (matmul(values, grad, ROWS_NT) - row_dot)).astype(jnp.bfloat16)
        value_grad = value_grad + matmul(probs.astype(jnp.bfloat16), grad, ROWS_NN)
        key_grad = key_grad + matmul(score_grad, query, ROWS_NN)
        query_grad = jnp.transpose(matmul(keys_across, score_grad, ROWS_NN)) * scale
        dquery_ref[block] = jnp.where(mask, query_grad.astype(jnp.bfloat16), dquery_ref[block])
    dkey_ref[window] = jnp.where(mask, (key_grad * scale).astype(jnp.bfloat16), dkey_ref[window])
    dvalue_ref[window] = jnp.where(mask, value_grad.astype(jnp.bfloat16), dvalue_ref[window])


def whole(shape):
    return pl.BlockSpec(shape, lambda *_: (0,) * len(shape), pipeline_mode=pl.Buffered(1))


def one_of(index, length, width):
    return pl.BlockSpec(
        (1, length, width), lambda head: (index, 0, 0), pipeline_mode=pl.Buffered(1)
    )


def attend_forward(qkv, keep, rows=512):
    _, length, width = qkv.shape
    heads = keep.shape[0]
    cells = heads * length * length
    return pl.pallas_call(
        functools.partial(
            attend_forward_kernel, head_size=width // heads, width=width, rows=min(rows, length)
        ),
        grid=(heads,),
        in_specs=[pl.BlockSpec(memory_space=pltpu.SMEM)]
        + [one_of(i, length, width) for i in range(3)],
        out_specs=[
            pl.BlockSpec((length, width), lambda head: (0, 0)),
            pl.BlockSpec((heads, length), lambda head: (0, 0)),
        ],
        out_shape=[
            jax.ShapeDtypeStruct((length, width), jnp.bfloat16),
            jax.ShapeDtypeStruct((heads, length), jnp.float32),
        ],
        compiler_params=pltpu.CompilerParams(vmem_limit_bytes=48 << 20),
        cost_estimate=pl.CostEstimate(
            flops=cells * 1024, transcendentals=cells, bytes_accessed=length * width * 8
        ),
        name="attend_forward",
    )(keep, qkv, qkv, qkv)


def attend_backward(qkv, out, grad, lse, keep, rows=256):
    _, length, width = qkv.shape
    heads = keep.shape[0]
    cells = heads * length * length
    return pl.pallas_call(
        functools.partial(
            attend_backward_kernel, head_size=width // heads, width=width, rows=min(rows, length)
        ),
        grid=(heads,),
        in_specs=[pl.BlockSpec(memory_space=pltpu.SMEM)]
        + [one_of(i, length, width) for i in range(3)]
        + [whole((length, width))] * 2
        + [whole((heads, length))],
        out_specs=pl.BlockSpec((3, length, width), lambda head: (0, 0, 0)),
        out_shape=jax.ShapeDtypeStruct((3, length, width), jnp.bfloat16),
        compiler_params=pltpu.CompilerParams(vmem_limit_bytes=56 << 20),
        cost_estimate=pl.CostEstimate(
            flops=cells * 2560, transcendentals=cells, bytes_accessed=length * width * 16
        ),
        name="attend_backward",
    )(keep, qkv, qkv, qkv, out, grad, lse)


ROWS_TN = (((0,), (0,)), ((), ()))
ANY = pl.BlockSpec(memory_space=pl.ANY)


class Blocks(list):
    def __init__(self, arrays, order):
        super().__init__(arrays)
        self.order = order

    def block(self, r, x_r, z_r):
        y_r, core_r = r // 2, r % 2
        first_r, second_r = (x_r, y_r) if self.order == "xy" else (y_r, x_r)
        return self[2 * core_r + second_r].at[first_r, z_r]


def square_copies(place, sets, r, target, sem):
    part = jnp.bitwise_xor(place[2], r)
    if len(sets[0]) == 1:
        return [pltpu.make_async_copy(sets[0][0].at[part], target, sem)]
    copies, column = [], 0
    for refs in sets:
        rows, columns = refs[0].shape[2:]
        for x_r in range(2):
            for z_r in range(4):
                shard = (place[0] + z_r) % 4 * 2 + (place[1] + x_r) % 2
                block = (pl.ds(pl.multiple_of(shard * rows, 16), rows), pl.ds(column, columns))
                source = refs.block(r, x_r, z_r)
                copies.append(pltpu.make_async_copy(source, target.at[block], sem))
        column += columns
    return copies


def strip_copies(place, refs, chunk, target, sem):
    if len(refs) == 1:
        return [pltpu.make_async_copy(refs[0].at[chunk], target, sem)]
    rows = refs[0].shape[2]
    copies = []
    for core_r in range(2):
        for y in range(2):
            part = 2 * y + (place[2] + core_r) % 2
            for x in range(2):
                start = pl.multiple_of(x * (4 * rows) + part * rows, 16)
                source = refs[core_r].at[2 * chunk + x, y]
                copies.append(pltpu.make_async_copy(source, target.at[pl.ds(start, rows)], sem))
    return copies


def square_stores(place, outs, r, source, sem):
    part = jnp.bitwise_xor(place[2], r)
    if len(outs) == 1:
        return [pltpu.make_async_copy(source, outs[0].at[part], sem)]
    copies, column = [], 0
    for pair in range(0, len(outs), 2):
        out = outs[pair + r % 2]
        out = out if len(out.shape) == 4 else out.at[r // 2]
        rows, columns = out.shape[2:]
        for shard in range(8):
            x_r, z_r = (place[1] + shard % 2) % 2, (shard // 2 + 4 - place[0]) % 4
            block = source.at[pl.ds(shard * rows, rows), pl.ds(column, columns)]
            copies.append(pltpu.make_async_copy(block, out.at[x_r, z_r], sem))
        column += columns
    return copies


def strip_stores(place, outs, chunk, source, sem):
    if len(outs) == 1:
        return [pltpu.make_async_copy(source, outs[0].at[chunk], sem)]
    rows = outs[0].shape[3]
    z_r = (chunk + 4 - place[0]) % 4
    copies = []
    for r in range(4):
        part = jnp.bitwise_xor(place[2], r)
        for x in range(2):
            block = source.at[pl.ds(pl.multiple_of(x * (4 * rows) + part * rows, 16), rows)]
            x_r = (place[1] + x) % 2
            copies.append(pltpu.make_async_copy(block, outs[r % 2].at[r // 2, x_r, z_r], sem))
    return copies


def in_sets(refs, sets):
    refs, found = list(refs), []
    for entry in sets:
        found.append(Blocks(refs[: len(entry)], entry.order))
        refs = refs[len(entry) :]
    return found


def flat(sets):
    return [array for entry in sets for array in entry]


def start_all(copies):
    for copy in copies:
        copy.start()


def wait_all(copies):
    for copy in copies:
        copy.wait()


def for_each(step, action):
    for r in range(4):

        @pl.when(step == r)
        def _(r=r):
            action(r)


def fetch_squares(place, sets, step, count, held, sems):
    def at(step, action):
        slot = step % 2

        @pl.when(step < count)
        def _():
            for_each(
                jnp.bitwise_xor(place[2], step),
                lambda r: action(square_copies(place, sets, r, held.at[slot], sems.at[slot])),
            )

    @pl.when(step == 0)
    def _():
        at(step, start_all)

    at(step + 1, start_all)
    at(step, wait_all)


def tiles(length, rows=256):
    return [pl.ds(start, min(rows, length)) for start in range(0, length, min(rows, length))]


def prepare_kernel(
    tokens_ref, cotangent_ref, parts_ref, mod_ref, across_ref, grad_ref, sum_ref, rows_ref
):
    width = tokens_ref.shape[1]

    @pl.when(pl.program_id(0) == 0)
    def _():
        for row in range(parts_ref.shape[1] // width):
            part = parts_ref[:, row * width : (row + 1) * width]
            rows_ref[row : row + 1] = jnp.sum(part, axis=0, keepdims=True)
        sum_ref[...] = jnp.zeros_like(sum_ref)

    normed, _ = norm_forward(tokens_ref[...].astype(jnp.float32))
    mod = normed * (1.0 + row_of(rows_ref, SCALE_ATTN)) + row_of(rows_ref, SHIFT_ATTN)
    mod_ref[...] = mod.astype(jnp.bfloat16)
    across_ref[...] = jnp.transpose(mod).astype(jnp.bfloat16)
    grad = (cotangent_ref[...].astype(jnp.float32) * row_of(rows_ref, GATE_MLP)).astype(jnp.bfloat16)
    grad_ref[...] = grad
    sum_ref[0:1] += jnp.sum(grad.astype(jnp.float32), axis=0, keepdims=True)


def prepare(tokens, cotangent, parts, tile=256):
    length, width = tokens.shape
    tile = min(tile, length)
    by_rows = pl.BlockSpec((tile, width), lambda step: (step, 0))
    fixed = pl.BlockSpec((8, width), lambda step: (0, 0))
    table = (16, width)
    return pl.pallas_call(
        prepare_kernel,
        grid=(length // tile,),
        in_specs=[by_rows, by_rows, pl.BlockSpec(parts.shape, lambda step: (0, 0))],
        out_specs=[
            by_rows,
            pl.BlockSpec((width, tile), lambda step: (0, step)),
            by_rows,
            fixed,
            pl.BlockSpec(table, lambda step: (0, 0)),
        ],
        out_shape=[
            jax.ShapeDtypeStruct((length, width), jnp.bfloat16),
            jax.ShapeDtypeStruct((width, length), jnp.bfloat16),
            jax.ShapeDtypeStruct((length, width), jnp.bfloat16),
            jax.ShapeDtypeStruct((8, width), jnp.float32),
            jax.ShapeDtypeStruct(table, jnp.float32),
        ],
        compiler_params=vmem_params(),
        cost_estimate=cost(20 * length * width, 10 * length * width),
        name="prepare",
    )(tokens, cotangent, parts)


def project_kernel(place, mod_ref, rows_ref, *rest, sets):
    *refs, out_ref, held, sems = rest
    step = pl.program_id(0)
    fetch_squares(place, in_sets(refs, sets), step, 3, held, sems)
    weight = held.at[step % 2]
    bias = rows_ref[pl.ds(QUERY_BIAS + step // 2, 1)] * (step != 1).astype(jnp.float32)
    for tile in tiles(mod_ref.shape[0]):
        out_ref[0, tile] = (matmul(mod_ref[tile], weight[...], ROWS_NN) + bias).astype(jnp.bfloat16)


def vmem_params(mebibytes=56):
    return pltpu.CompilerParams(
        vmem_limit_bytes=mebibytes << 20, dimension_semantics=("arbitrary",)
    )


def cost(flops, moved):
    return pl.CostEstimate(flops=1, transcendentals=0, bytes_accessed=1)


def project(place, mod, rows, squares):
    length, width = mod.shape
    return pl.pallas_call(
        functools.partial(project_kernel, sets=squares),
        grid_spec=pltpu.PrefetchScalarGridSpec(
            num_scalar_prefetch=1,
            grid=(3,),
            in_specs=[
                pl.BlockSpec((length, width), lambda step, place: (0, 0)),
                pl.BlockSpec(rows.shape, lambda step, place: (0, 0)),
            ]
            + [ANY] * len(flat(squares)),
            out_specs=pl.BlockSpec(
                (1, length, width), lambda step, place: (step, 0, 0)
            ),
            scratch_shapes=[
                pltpu.VMEM((2, width, width), jnp.bfloat16),
                pltpu.SemaphoreType.DMA((2,)),
            ],
        ),
        out_shape=jax.ShapeDtypeStruct((3, length, width), jnp.bfloat16),
        compiler_params=vmem_params(),
        cost_estimate=cost(6 * length * width * width, 14 * length * width),
        name="project",
    )(place, mod, rows, *flat(squares))


def fetch_part(place, sets, wanted, target, sem):
    part = jnp.bitwise_xor(place[2], wanted)
    for_each(part, lambda r: start_all(square_copies(place, sets, r, target, sem)))
    for_each(part, lambda r: wait_all(square_copies(place, sets, r, target, sem)))


def row_of(rows_ref, index):
    return rows_ref[index : index + 1]


SHIFT_ATTN, SCALE_ATTN, GATE_ATTN, SHIFT_MLP, SCALE_MLP, GATE_MLP = range(6)
QUERY_BIAS, VALUE_BIAS, OUT_BIAS, UP_BIAS, DOWN_BIAS = 6, 7, 8, 9, 13


def after_attention_kernel(place, low_ref, tokens_ref, rows_ref, *rest, sets):
    *refs, branch_ref, middle_ref, mod_ref, across_ref, weight, sem = rest

    @pl.when(pl.program_id(0) == 0)
    def _():
        fetch_part(place, in_sets(refs, sets), 3, weight, sem)

    branch = matmul(low_ref[...], weight[...], ROWS_NN) + row_of(rows_ref, OUT_BIAS)
    middle = tokens_ref[...].astype(jnp.float32) + row_of(rows_ref, GATE_ATTN) * branch
    normed, _ = norm_forward(middle)
    mod = normed * (1.0 + row_of(rows_ref, SCALE_MLP)) + row_of(rows_ref, SHIFT_MLP)
    branch_ref[...] = branch
    middle_ref[...] = middle
    mod_ref[...] = mod.astype(jnp.bfloat16)
    across_ref[...] = jnp.transpose(mod).astype(jnp.bfloat16)


def after_attention(place, low, tokens, rows, squares, tile=256):
    length, width = low.shape
    tile = min(tile, length)
    by_rows = pl.BlockSpec((tile, width), lambda step, place: (step, 0))
    return pl.pallas_call(
        functools.partial(after_attention_kernel, sets=squares),
        grid_spec=pltpu.PrefetchScalarGridSpec(
            num_scalar_prefetch=1,
            grid=(length // tile,),
            in_specs=[by_rows, by_rows, pl.BlockSpec(rows.shape, lambda step, place: (0, 0))]
            + [ANY] * len(flat(squares)),
            out_specs=[by_rows] * 3 + [pl.BlockSpec((width, tile), lambda step, place: (0, step))],
            scratch_shapes=[pltpu.VMEM((width, width), jnp.bfloat16), pltpu.SemaphoreType.DMA],
        ),
        out_shape=[
            jax.ShapeDtypeStruct((length, width), jnp.float32),
            jax.ShapeDtypeStruct((length, width), jnp.float32),
            jax.ShapeDtypeStruct((length, width), jnp.bfloat16),
            jax.ShapeDtypeStruct((width, length), jnp.bfloat16),
        ],
        compiler_params=vmem_params(),
        cost_estimate=cost(2 * length * width * width, 18 * length * width),
        name="after_attention",
    )(place, low, tokens, rows, *flat(squares))


ROOT = 0.7978845608028654


def gelu_and_slope(values):
    square = values * values
    bend = jnp.tanh(values * (ROOT + (ROOT * 0.044715) * square))
    half = 0.5 + 0.5 * bend
    slope = half + (0.5 * values) * (1.0 - bend * bend) * (ROOT + (3 * 0.044715 * ROOT) * square)
    return values * half, slope


def mlp_kernel(place, rows_ref, keep_ref, *rest, ups, downs):
    inputs, rest = rest[:3], rest[3:]
    count = len(flat(ups)) + downs
    refs, rest = rest[:count], rest[count:]
    up_sets, down_refs = in_sets(refs, ups), refs[-downs:]
    branch_out, dmod_out, dbias_ref, *stores = rest[:-12]
    mod_ref, across_ref, grad_ref, branch_ref, dmod_ref, act, dpre, up_all, down_all = rest[-12:-3]
    in_sems, out_sem, sum_sem = rest[-3:]
    up_stores, down_stores = stores[: len(stores) // 2], stores[len(stores) // 2 :]
    length, width = mod_ref.shape

    def chunk_of(r):
        return jnp.bitwise_xor(place[2], r)

    first = place[2] % 2

    def spot(r):
        start = pl.multiple_of(jnp.bitwise_xor(first, r % 2) * width, 128)
        return pl.ds(start, width)

    halves = ((0, 1), (2, 3))
    loads = [
        [pltpu.make_async_copy(inputs[0], mod_ref, in_sems.at[0])],
        [pltpu.make_async_copy(inputs[2], grad_ref, in_sems.at[1])],
        [],
        [],
        [pltpu.make_async_copy(inputs[1], across_ref, in_sems.at[4])],
    ]
    for index, pair in enumerate(halves):
        for r in pair:
            target = up_all.at[index, :, spot(r)]
            loads[2 * index] += square_copies(place, up_sets, r, target, in_sems.at[2 * index])
            target = down_all.at[index, spot(r)]
            loads[2 * index + 1] += strip_copies(
                place, down_refs, chunk_of(r), target, in_sems.at[2 * index + 1]
            )
    for index in (0, 1, 4, 2, 3):
        start_all(loads[index])
    rows = min(512, length)
    columns = 768 if 2 * width % 768 == 0 else width
    leaving = []
    for index, pair in enumerate(halves):
        up, down = up_all.at[index], down_all.at[index]
        low_chunk = chunk_of(pair[0]) // 2 * 2

        def row_pair(ref, at):
            return jnp.concatenate([ref[pl.ds(at, 1)], ref[pl.ds(at + 1, 1)]], axis=1)

        bias = row_pair(rows_ref, UP_BIAS + low_chunk)
        keep = row_pair(keep_ref, low_chunk)
        wait_all(loads[2 * index])
        wait_all(loads[2 * index + 1])

        def row_tile(number, total):
            tile = pl.ds(pl.multiple_of(number * rows, rows), rows)
            sums = []
            for column in range(0, 2 * width, columns):
                part = slice(column, column + columns)
                gelu, slope = gelu_and_slope(
                    matmul(mod_ref[tile], up[:, part], ROWS_NN) + bias[:, part]
                )
                act[tile, part] = (gelu * keep[:, part]).astype(jnp.bfloat16)
                back = matmul(grad_ref[tile], down[part], ROWS_NT)
                low = (slope * keep[:, part] * back).astype(jnp.bfloat16)
                dpre[tile, part] = low
                sums.append(jnp.sum(low.astype(jnp.float32), axis=0, keepdims=True))
            branch = matmul(act[tile], down[...], ROWS_NN)
            dmod = matmul(dpre[tile], up[...], ROWS_NT)
            if index:
                branch_ref[tile] += branch
                dmod_ref[tile] += dmod
            else:
                branch_ref[tile] = branch
                dmod_ref[tile] = dmod
            return total + jnp.concatenate(sums, axis=1)

        total = lax.fori_loop(0, length // rows, row_tile, jnp.zeros_like(bias))
        dbias_ref[pl.ds(low_chunk, 1)] = total[:, :width]
        dbias_ref[pl.ds(low_chunk + 1, 1)] = total[:, width:]
        if index == 1:
            copies = [
                pltpu.make_async_copy(branch_ref, branch_out, sum_sem),
                pltpu.make_async_copy(dmod_ref, dmod_out, sum_sem),
            ]
            start_all(copies)
            leaving += copies
        else:
            wait_all(loads[4])

        for r in pair:
            up[:, spot(r)] = matmul(across_ref[...], dpre[:, spot(r)], ROWS_NN).astype(jnp.bfloat16)
            copies = square_stores(place, up_stores, r, up.at[:, spot(r)], out_sem)
            start_all(copies)
            leaving += copies
        for r in pair:
            down[spot(r)] = matmul(act[:, spot(r)], grad_ref[...], ROWS_TN).astype(jnp.bfloat16)
            copies = strip_stores(place, down_stores, chunk_of(r), down.at[spot(r)], out_sem)
            start_all(copies)
            leaving += copies
    wait_all(leaving)


def gradient_shapes(paired, rows, columns):
    if paired:
        return [
            jax.ShapeDtypeStruct((2, 2, 4, rows, count), jnp.bfloat16)
            for count in columns
            for _ in range(2)
        ]
    return [jax.ShapeDtypeStruct((4, sum(columns), sum(columns)), jnp.bfloat16)]


def mlp(place, mod, across, grad, rows, keep, ups, downs, block_rows):
    length, width = mod.shape
    stores = gradient_shapes(len(downs) > 1, block_rows, [width])
    count = len(flat(ups)) + len(downs)
    table = pl.BlockSpec((4, width), lambda step, place: (0, 0))
    return pl.pallas_call(
        functools.partial(mlp_kernel, ups=ups, downs=len(downs)),
        grid_spec=pltpu.PrefetchScalarGridSpec(
            num_scalar_prefetch=1,
            grid=(1,),
            in_specs=[pl.BlockSpec(rows.shape, lambda step, place: (0, 0)), table]
            + [ANY] * (3 + count),
            out_specs=[ANY, ANY, table] + [ANY] * (2 * len(stores)),
            scratch_shapes=[
                pltpu.VMEM((length, width), jnp.bfloat16),
                pltpu.VMEM((width, length), jnp.bfloat16),
                pltpu.VMEM((length, width), jnp.bfloat16),
                pltpu.VMEM((length, width), jnp.float32),
                pltpu.VMEM((length, width), jnp.float32),
                pltpu.VMEM((length, 2 * width), jnp.bfloat16),
                pltpu.VMEM((length, 2 * width), jnp.bfloat16),
                pltpu.VMEM((2, width, 2 * width), jnp.bfloat16),
                pltpu.VMEM((2, 2 * width, width), jnp.bfloat16),
                pltpu.SemaphoreType.DMA((5,)),
                pltpu.SemaphoreType.DMA,
                pltpu.SemaphoreType.DMA,
            ],
        ),
        out_shape=[jax.ShapeDtypeStruct((length, width), jnp.float32)] * 2
        + [jax.ShapeDtypeStruct((4, width), jnp.float32)]
        + stores
        + stores,
        compiler_params=vmem_params(62),
        cost_estimate=cost(48 * length * width * width, 32 * width * width),
        name="mlp",
    )(place, rows, keep, mod, across, grad, *flat(ups), *downs)


def after_mlp_kernel(
    place, dmod_ref, middle_ref, cotangent_ref, rows_ref, *rest, sets
):
    *refs, dmiddle_ref, dbranch_ref, dlow_ref, sums_ref, weight, sem = rest

    @pl.when(pl.program_id(0) == 0)
    def _():
        fetch_part(place, in_sets(refs, sets), 3, weight, sem)
        sums_ref[...] = jnp.zeros_like(sums_ref)

    normed, inverse = norm_forward(middle_ref[...])
    dmod = dmod_ref[...]
    dmiddle = cotangent_ref[...].astype(jnp.float32) + norm_backward(
        dmod * (1.0 + row_of(rows_ref, SCALE_MLP)), normed, inverse
    )
    dmiddle_ref[...] = dmiddle
    low = (dmiddle * row_of(rows_ref, GATE_ATTN)).astype(jnp.bfloat16)
    dbranch_ref[...] = low
    dlow_ref[...] = matmul(low, weight[...], ROWS_NT).astype(jnp.bfloat16)
    sums_ref[0:1] += jnp.sum(dmod * normed, axis=0, keepdims=True)
    sums_ref[1:2] += jnp.sum(dmod, axis=0, keepdims=True)
    sums_ref[2:3] += jnp.sum(low.astype(jnp.float32), axis=0, keepdims=True)


def after_mlp(place, dmod, middle, cotangent, rows, squares, tile=256):
    length, width = middle.shape
    tile = min(tile, length)
    by_rows = pl.BlockSpec((tile, width), lambda step, place: (step, 0))
    fixed = lambda shape: pl.BlockSpec(shape, lambda step, place: (0, 0))
    return pl.pallas_call(
        functools.partial(after_mlp_kernel, sets=squares),
        grid_spec=pltpu.PrefetchScalarGridSpec(
            num_scalar_prefetch=1,
            grid=(length // tile,),
            in_specs=[by_rows] * 3 + [fixed(rows.shape)] + [ANY] * len(flat(squares)),
            out_specs=[by_rows] * 3 + [fixed((8, width))],
            scratch_shapes=[pltpu.VMEM((width, width), jnp.bfloat16), pltpu.SemaphoreType.DMA],
        ),
        out_shape=[
            jax.ShapeDtypeStruct((length, width), jnp.float32),
            jax.ShapeDtypeStruct((length, width), jnp.bfloat16),
            jax.ShapeDtypeStruct((length, width), jnp.bfloat16),
            jax.ShapeDtypeStruct((8, width), jnp.float32),
        ],
        compiler_params=vmem_params(),
        cost_estimate=cost(2 * length * width * width, 20 * length * width),
        name="after_mlp",
    )(place, dmod, middle, cotangent, rows, *flat(squares))


def finish_kernel(
    mlp_ref, middle_ref, branch_ref, dmiddle_ref, cotangent_ref, rows_ref, out_ref, sums_ref
):
    @pl.when(pl.program_id(0) == 0)
    def _():
        sums_ref[...] = jnp.zeros_like(sums_ref)

    mlp_branch = mlp_ref[...] + row_of(rows_ref, DOWN_BIAS)
    out_ref[...] = (middle_ref[...] + row_of(rows_ref, GATE_MLP) * mlp_branch).astype(jnp.bfloat16)
    grad = cotangent_ref[...].astype(jnp.float32) * mlp_branch
    sums_ref[0:1] += jnp.sum(grad, axis=0, keepdims=True)
    sums_ref[1:2] += jnp.sum(dmiddle_ref[...] * branch_ref[...], axis=0, keepdims=True)


def finish(branch_mlp, middle, branch, dmiddle, cotangent, rows, tile=256):
    length, width = middle.shape
    tile = min(tile, length)
    by_rows = pl.BlockSpec((tile, width), lambda step: (step, 0))
    return pl.pallas_call(
        finish_kernel,
        grid=(length // tile,),
        in_specs=[by_rows] * 5 + [pl.BlockSpec(rows.shape, lambda step: (0, 0))],
        out_specs=[by_rows, pl.BlockSpec((8, width), lambda step: (0, 0))],
        out_shape=[
            jax.ShapeDtypeStruct((length, width), jnp.bfloat16),
            jax.ShapeDtypeStruct((8, width), jnp.float32),
        ],
        compiler_params=vmem_params(),
        cost_estimate=cost(8 * length * width, 20 * length * width),
        name="finish",
    )(branch_mlp, middle, branch, dmiddle, cotangent, rows)


def square_grads_kernel(place, across_ref, grads_ref, low_ref, dbranch_ref, *rest):
    *stores, staged, sems = rest
    step = pl.program_id(0)
    part = jnp.bitwise_xor(place[2], step)

    def leave(r):
        return square_stores(place, stores, r, staged.at[r % 2], sems.at[r % 2])

    for_each(step - 2, lambda r: wait_all(leave(r)))

    @pl.when(part < 3)
    def _():
        staged[step % 2] = matmul(across_ref[...], grads_ref[0], ROWS_NN).astype(jnp.bfloat16)

    @pl.when(part == 3)
    def _():
        staged[step % 2] = matmul(low_ref[...], dbranch_ref[...], ROWS_TN).astype(jnp.bfloat16)

    for_each(step, lambda r: start_all(leave(r)))

    @pl.when(step == 3)
    def _():
        wait_all(leave(2))
        wait_all(leave(3))


def square_grads(place, across, grads, low, dbranch, paired, block_rows, columns):
    width, length = across.shape
    stores = gradient_shapes(paired, block_rows, columns)
    held = pl.BlockSpec((length, width), lambda step, place: (0, 0), pipeline_mode=pl.Buffered(1))
    return pl.pallas_call(
        square_grads_kernel,
        grid_spec=pltpu.PrefetchScalarGridSpec(
            num_scalar_prefetch=1,
            grid=(4,),
            in_specs=[
                pl.BlockSpec((width, length), lambda step, place: (0, 0), pipeline_mode=pl.Buffered(1)),
                pl.BlockSpec(
                    (1, length, width),
                    lambda step, place: (jnp.minimum(jnp.bitwise_xor(place[2], step), 2), 0, 0),
                ),
                held,
                held,
            ],
            out_specs=[ANY] * len(stores),
            scratch_shapes=[
                pltpu.VMEM((2, width, width), jnp.bfloat16),
                pltpu.SemaphoreType.DMA((2,)),
            ],
        ),
        out_shape=stores,
        compiler_params=vmem_params(),
        cost_estimate=cost(8 * length * width * width, 20 * length * width),
        name="square_grads",
    )(place, across, grads, low, dbranch)


def tokens_back_kernel(place, grads_ref, tokens_ref, dmiddle_ref, rows_ref, *rest, sets):
    *refs, out_ref, sums_ref, dmod, held, sems = rest
    step = pl.program_id(0)
    fetch_squares(place, in_sets(refs, sets), step, 3, held, sems)
    length = tokens_ref.shape[0]

    @pl.when(step == 0)
    def _():
        dmod[...] = jnp.zeros_like(dmod)

    for tile in tiles(length):
        dmod[tile] += matmul(grads_ref[0, tile], held[step % 2], ROWS_NT)
    total = jnp.sum(grads_ref[0].astype(jnp.float32), axis=0, keepdims=True)
    sums_ref[pl.ds(2 + step, 1)] = total

    @pl.when(step == 2)
    def _():
        shift = jnp.zeros((1, dmod.shape[1]), jnp.float32)
        scale = shift
        for tile in tiles(length):
            back = dmod[tile]
            normed, inverse = norm_forward(tokens_ref[tile].astype(jnp.float32))
            scale = scale + jnp.sum(back * normed, axis=0, keepdims=True)
            shift = shift + jnp.sum(back, axis=0, keepdims=True)
            back = norm_backward(back * (1.0 + row_of(rows_ref, SCALE_ATTN)), normed, inverse)
            out_ref[tile] = (dmiddle_ref[tile] + back).astype(jnp.bfloat16)
        sums_ref[0:1] = shift
        sums_ref[1:2] = scale


def tokens_back(place, grads, tokens, dmiddle, rows, squares):
    length, width = tokens.shape
    held = pl.BlockSpec((length, width), lambda step, place: (0, 0), pipeline_mode=pl.Buffered(1))
    return pl.pallas_call(
        functools.partial(tokens_back_kernel, sets=squares),
        grid_spec=pltpu.PrefetchScalarGridSpec(
            num_scalar_prefetch=1,
            grid=(3,),
            in_specs=[
                pl.BlockSpec(
                    (1, length, width),
                    lambda step, place: (step, 0, 0),
                ),
                held,
                held,
                pl.BlockSpec(rows.shape, lambda step, place: (0, 0)),
            ]
            + [ANY] * len(flat(squares)),
            out_specs=[
                pl.BlockSpec((length, width), lambda step, place: (0, 0)),
                pl.BlockSpec((8, width), lambda step, place: (0, 0)),
            ],
            scratch_shapes=[
                pltpu.VMEM((length, width), jnp.float32),
                pltpu.VMEM((2, width, width), jnp.bfloat16),
                pltpu.SemaphoreType.DMA((2,)),
            ],
        ),
        out_shape=[
            jax.ShapeDtypeStruct((length, width), jnp.bfloat16),
            jax.ShapeDtypeStruct((8, width), jnp.float32),
        ],
        compiler_params=vmem_params(),
        cost_estimate=cost(6 * length * width * width, 20 * length * width),
        name="tokens_back",
    )(place, grads, tokens, dmiddle, rows, *flat(squares))


def gather_rows(rows, axis, size):
    place = lax.axis_index(axis)
    step = 1
    while step < size:
        other = lax.ppermute(rows, axis, [(i, i ^ step) for i in range(size)])
        high = (place // step) % 2 == 1
        rows = jnp.concatenate([jnp.where(high, other, rows), jnp.where(high, rows, other)], axis=0)
        step *= 2
    return rows


def swap(value, axis, size, step):
    return lax.ppermute(value, axis, [(i, i ^ step) for i in range(size)])


def both(value, axis, size, step, dim):
    other = swap(value, axis, size, step)
    first = lax.axis_index(axis) // step % 2 == 0
    return jnp.stack([jnp.where(first, value, other), jnp.where(first, other, value)], axis=dim)


def barrier(values):
    return lax.optimization_barrier(values)


def after(value, *others):
    return barrier((value, others))[0]


def add(*terms):
    return sum(term.astype(jnp.float32) for term in terms).astype(jnp.bfloat16)


class Pairwise:
    def __init__(self, shards, group):
        self.shards, self.group = shards, group

    def partner(self, value, kind):
        if kind == "x":
            return swap(value, "fsdp", self.shards, 1)
        return swap(value, "dp", self.group, 2 if kind == "y" else 1)

    def corners(self, block):
        size = self.shards * self.group
        x, y, far = [
            lax.ppermute(block, ("fsdp", "dp"), [(i, i ^ step) for i in range(size)])
            for step in (self.group, 2, self.group + 2)
        ]
        return jnp.stack([jnp.stack([block, x]), jnp.stack([y, far])])

    def ahead(self, value, count):
        pairs = [((target // 2 + count) % 4 * 2 + target % 2, target) for target in range(8)]
        return lax.ppermute(value, "fsdp", pairs)

    def along_z(self, block):
        return jnp.stack([block] + [self.ahead(block, count) for count in (1, 2, 3)])

    def pair(self, block, kind):
        return jnp.stack([block, self.partner(block, kind)])

    def first_sum(self, kept, other, kind):
        dim = 0 if kind == "y" else 1
        stay, go = [
            [lax.index_in_dim(half, i, dim, keepdims=False) for half in (kept, other)] for i in (0, 1)
        ]
        return add(*go), stay

    def second_sum(self, stay, back):
        return add(stay[0][1], stay[1][1], back[1]), add(stay[0][0], stay[1][0], back[0])

    def send_z(self, mine):
        return [self.ahead(mine[count], 4 - count) for count in (1, 2, 3)]

    def to_group(self, part):
        parts = both(both(part, "dp", self.group, 2, 0), "dp", self.group, 1, 1)
        return parts.reshape(4, *part.shape)


def reduce_all(grad):
    shard = lax.psum_scatter(grad, "fsdp", scatter_dimension=0, tiled=True)
    return lax.psum(shard, "dp").astype(jnp.float32)


def reduce_columns(parts):
    _, rows, width = parts.shape
    shard = reduce_all(parts.swapaxes(0, 1).reshape(rows, 4 * width))
    return [shard[:, i * width : (i + 1) * width] for i in range(4)]


def conditioning(times, labels, table, shard, width):
    class_count, columns = table.shape
    half = width // 2
    column = shard * columns + jnp.arange(columns, dtype=jnp.int32)
    frequency = jnp.exp(-math.log(10000.0) * (column % half).astype(jnp.float32) / half)
    angles = times.astype(jnp.float32)[:, None] * frequency[None, :]
    embed = jnp.where(column[None, :] < half, jnp.cos(angles), jnp.sin(angles))
    picked = labels[:, None] == jnp.arange(class_count, dtype=jnp.int32)[None, :]
    return embed + jnp.dot(
        picked.astype(jnp.bfloat16), table, preferred_element_type=jnp.float32
    )


def own_part(values, shard, size):
    return lax.dynamic_slice_in_dim(values, shard * size, size, axis=values.ndim - 1)


def body(
    shard_count,
    image_count,
    tokens,
    timesteps,
    labels,
    head_keep,
    chan_keep,
    cotangent,
    qkv_weight,
    qv_bias,
    out_weight,
    out_bias,
    up_weight,
    up_bias,
    down_weight,
    down_bias,
    ada_weight,
    ada_bias,
    class_table,
):
    _, length, width = tokens.shape
    hidden = chan_keep.shape[1]
    class_count = class_table.shape[0]
    columns = width // shard_count
    group_count = image_count // shard_count
    shard = lax.axis_index("fsdp")
    member = lax.axis_index("dp")
    bf16, f32 = jnp.bfloat16, jnp.float32

    place = jnp.stack([shard // 2, shard % 2, member]).astype(jnp.int32)
    paired = shard_count == 8 and group_count == 4 and columns % 16 == 0
    net = Pairwise(shard_count, group_count)
    splits = [width // 2 // 128 * 128]
    splits.append(width - splits[0])
    four = jnp.concatenate([qkv_weight, out_weight], axis=1)

    fact = jnp.stack([timesteps[0], labels[0]])
    if paired:
        near = net.pair(fact, "x")
        mine = lax.dynamic_slice_in_dim(four, member * width, width, axis=1)
        near = net.along_z(near)
        square = net.along_z(mine)
        facts = jnp.where(place[1] == 0, near, near[:, ::-1])
        facts = lax.dynamic_slice_in_dim(
            jnp.concatenate([facts, facts]), (4 - place[0]) % 4, 4, axis=0
        ).reshape(8, 2)
    else:
        facts = gather_rows(fact[None], "fsdp", shard_count)
    group_act = jax.nn.silu(
        conditioning(facts[:, 0], facts[:, 1], class_table, shard, width)
    ).astype(bf16)
    partial = jnp.dot(group_act, ada_weight, preferred_element_type=f32)

    def own_columns(values):
        values = values.astype(f32)
        full = jnp.zeros((values.shape[0] * shard_count,), f32)
        return lax.dynamic_update_slice_in_dim(full, values, shard * values.shape[0], axis=0)

    biases = jnp.concatenate(
        [own_columns(values) for values in (qv_bias[0], qv_bias[1], out_bias, up_bias, down_bias)]
    )
    sent = jnp.concatenate(
        [
            partial + own_columns(ada_bias),
            jnp.broadcast_to(biases, (shard_count, biases.shape[0])),
        ],
        axis=1,
    )
    if paired:
        square, sent, near = barrier((square, sent, near))
        parts = lax.all_to_all(sent, "fsdp", 0, 0, tiled=True)
        all_facts = near.swapaxes(0, 1)
        first = net.pair(square[:, :, : splits[0]], "x")
        second = net.pair(square[:, :, splits[0] :], "y")
        mine = lax.dynamic_slice_in_dim(up_weight, member * width, width, axis=1)
        down_mine = down_weight.reshape(2, 2, columns, width)
        down_mine = jnp.where(member % 2 == 0, down_mine[:, 0], down_mine[:, 1])
        mine, down_mine, first, second, parts = barrier((mine, down_mine, first, second, parts))
        first_y, second_x = net.partner(first, "y"), net.partner(second, "x")
        up = net.along_z(mine)
        prepared = prepare(tokens[0], cotangent[0], parts)
        first, second, first_y, second_x, up, prepared = barrier(
            (first, second, first_y, second_x, up, prepared)
        )
        squares = [
            Blocks([first, first_y, net.partner(first, "c"), net.partner(first_y, "c")], "xy"),
            Blocks([second, second_x, net.partner(second, "c"), net.partner(second_x, "c")], "yx"),
        ]
    else:
        parts = lax.all_to_all(sent, "fsdp", 0, 0, tiled=True)
        all_facts = gather_rows(facts, "dp", group_count)
        found = lax.all_gather(four, "fsdp", axis=0, tiled=True)
        squares = [Blocks([found.reshape(width, 4, width).swapaxes(0, 1)], "xy")]
        prepared = prepare(tokens[0], cotangent[0], parts)
    mod_one, mod_across, branch_grad, down_bias_g, rows = prepared
    if paired:
        up_x, up_y = net.partner(up, "x"), net.partner(up, "y")
        down = lax.all_gather(after(down_mine, squares[0][3]), "fsdp", axis=0)
    qkv = project(place, mod_one, rows, squares)
    if paired:
        qkv, up_x, up_y, all_facts = barrier((qkv, up_x, up_y, all_facts))
        up = jnp.stack([up, up_x])
        up_xy, up_c = net.partner(up_x, "y"), net.partner(up, "c")
        all_facts = net.pair(all_facts, "c").swapaxes(0, 1)
    attn_low, lse = attend_forward(qkv, head_keep[0])
    if paired:
        attn_low, up, up_xy, up_c, all_facts = barrier((attn_low, up, up_xy, up_c, all_facts))
        all_facts = net.pair(all_facts, "y").reshape(image_count, 2)
        up_y = jnp.stack([up_y, up_xy])
        up_y_c = net.partner(up_y, "c")
    attn_branch, middle, mod_two, mod_two_across = after_attention(
        place, attn_low, tokens[0], rows, squares
    )
    if paired:
        mod_two, down, up_y_c, all_facts = barrier((mod_two, down, up_y_c, all_facts))
        ups = [Blocks([up, up_y, up_c, up_y_c], "xy")]
        downs = [down, net.partner(down, "c")]
    else:
        found = lax.all_gather(up_weight, "fsdp", axis=0, tiled=True)
        ups = [Blocks([found.reshape(width, 4, width).swapaxes(0, 1)], "xy")]
        found = lax.all_gather(down_weight, "fsdp", axis=0, tiled=True)
        downs = [found.reshape(4, width, width)]
    branch_mlp, mod_two_grad, up_bias_g, *stores = mlp(
        place,
        mod_two,
        mod_two_across,
        branch_grad,
        rows,
        chan_keep.astype(f32).reshape(4, width),
        ups,
        downs,
        columns,
    )
    up_bias_g = up_bias_g.reshape(-1)
    if paired:
        up_kept, up_sent, down_kept, down_sent = stores
        up_other, down_other = net.partner(up_sent, "c"), net.partner(down_sent, "c")
    else:
        up_shard = jnp.concatenate(reduce_columns(stores[0]), axis=1)
        down_shard = reduce_all(stores[1].reshape(hidden, width))
    middle_grad, dbranch, low_grad, sums = after_mlp(
        place, mod_two_grad, middle, cotangent[0], rows, squares
    )
    scale_mlp_grad, shift_mlp_grad, out_bias_g = sums[0], sums[1], sums[2]
    if paired:
        low_grad, up_other, down_other = barrier((low_grad, up_other, down_other))
        up_go, up_stay = net.first_sum(up_kept, up_other, "x")
        down_go, down_stay = net.first_sum(down_kept, down_other, "y")
        low_grad, up_go, down_go = barrier((low_grad, up_go, down_go))
        up_back, down_back = net.partner(up_go, "x"), net.partner(down_go, "y")
    grads = attend_backward(qkv, attn_low, low_grad, lse, head_keep[0])
    if paired:
        grads, up_back, down_back = barrier((grads, up_back, down_back))
        up_go, up_stay = net.second_sum(up_stay, up_back)
        down_go, down_stay = net.second_sum(down_stay, down_back)
        grads, up_go, down_go = barrier((grads, up_go, down_go))
        up_back, down_back = net.partner(up_go, "y"), net.partner(down_go, "x")
    stores = square_grads(
        place, mod_across, grads, attn_low, dbranch, paired, columns, splits
    )
    block_out, gate_sums = finish(branch_mlp, middle, attn_branch, middle_grad, cotangent[0], rows)
    if paired:
        stores, grads, up_back, down_back, block_out, gate_sums = barrier(
            (stores, grads, up_back, down_back, block_out, gate_sums)
        )
        others = [net.partner(sent, "c") for sent in stores[1::2]]
        others = barrier(others)
        goes, stays = zip(
            *[net.first_sum(stores[2 * i], others[i], kind) for i, kind in enumerate("yx")]
        )
        up_mine = add(up_stay, up_back)
        goes, up_mine, grads = barrier((goes, up_mine, grads))
        backs = [net.partner(go, kind) for go, kind in zip(goes, "yx")]
        up_terms = net.send_z(up_mine)
    def small_grads(all_rows):
        cond = conditioning(all_facts[:, 0], all_facts[:, 1], class_table, shard, width)
        cond_act, silu_pull = jax.vjp(jax.nn.silu, cond)
        ada_grad = all_rows[:, : 6 * width]
        ada_weight_g = jnp.einsum(
            "sd,se->de", cond_act.astype(bf16), ada_grad, preferred_element_type=f32
        )
        cond_act_grad = jnp.einsum("se,de->sd", ada_grad, ada_weight, preferred_element_type=f32)
        cond_grad = silu_pull(cond_act_grad)[0]
        picked = all_facts[:, 1][:, None] == jnp.arange(class_count, dtype=jnp.int32)[None, :]
        table_g = jnp.einsum(
            "sc,sd->cd", picked.astype(f32), cond_grad, precision=lax.Precision.HIGHEST
        )
        sums = jnp.sum(all_rows.astype(f32), axis=0)
        ada_bias_g = own_part(sums[: 6 * width], shard, ada_bias.shape[0])
        qv_bias_g = own_part(sums[6 * width : 8 * width].reshape(2, width), shard, columns)
        out_bias_own = own_part(sums[8 * width : 9 * width], shard, columns)
        up_bias_own = own_part(sums[9 * width : 9 * width + hidden], shard, up_bias.shape[0])
        down_bias_own = own_part(sums[9 * width + hidden :], shard, columns)
        return qv_bias_g, out_bias_own, up_bias_own, down_bias_own, ada_weight_g, ada_bias_g, table_g

    tokens_grad, sums = tokens_back(place, grads, tokens[0], middle_grad, rows, squares)
    if paired:
        tokens_grad, sums, backs, up_terms = barrier((tokens_grad, sums, backs, up_terms))
    gate_mlp_grad, gate_attn_grad = gate_sums[0], gate_sums[1]
    row = jnp.concatenate(
        [
            sums[0],
            sums[1],
            gate_attn_grad,
            shift_mlp_grad,
            scale_mlp_grad,
            gate_mlp_grad,
            sums[2],
            sums[4],
            out_bias_g,
            up_bias_g,
            down_bias_g[0],
        ]
    ).astype(bf16)[None]
    if paired:
        down_mine = add(down_stay, down_back)
        goes, stays = zip(*[net.second_sum(stay, back) for stay, back in zip(stays, backs)])
        goes, row, down_mine = barrier((goes, row, down_mine))
        row = net.along_z(row)
        backs = [net.partner(go, kind) for go, kind in zip(goes, "xy")]
        down_terms = net.send_z(down_mine)
        backs, down_terms, row = barrier((backs, down_terms, row))
        mine = jnp.concatenate([add(stay, back) for stay, back in zip(stays, backs)], axis=2)
        part = jnp.stack([add(up_mine[0], *up_terms), add(down_mine[0], *down_terms)])
        mine, part, row = barrier((mine, part, row))
        terms = net.send_z(mine)
        row = net.corners(net.pair(row, "c"))
        mlp_parts = both(part, "dp", group_count, 2, 0)
        terms, row, mlp_parts = barrier((terms, row, mlp_parts))
        small = small_grads(row.reshape(image_count, -1))
        mlp_parts = both(mlp_parts, "dp", group_count, 1, 1).reshape(4, *part.shape)
        parts = net.to_group(add(mine[0], *terms)).astype(f32)
        up_shard = jnp.concatenate([mlp_parts[i, 0] for i in range(4)], axis=1).astype(f32)
        down_shard = mlp_parts[:, 1].reshape(down_weight.shape).astype(f32)
        query_g, key_g, value_g, out_shard = parts
    else:
        query_g, key_g, value_g, out_shard = reduce_columns(stores[0])
        all_rows = gather_rows(gather_rows(row, "fsdp", shard_count), "dp", group_count)
        small = small_grads(all_rows)
    qkv_shard = jnp.concatenate([query_g, key_g, value_g], axis=1)
    (
        qv_bias_g,
        out_bias_g,
        up_bias_g,
        down_bias_g,
        ada_weight_g,
        ada_bias_g,
        table_g,
    ) = small
    return (
        block_out[None],
        tokens_grad[None],
        qkv_shard,
        qv_bias_g,
        out_shard,
        out_bias_g,
        up_shard,
        up_bias_g,
        down_shard,
        down_bias_g,
        ada_weight_g,
        ada_bias_g,
        table_g,
    )


def solution(mesh):
    shard_count = mesh.shape["fsdp"]
    image_count = shard_count * mesh.shape["dp"]
    images = ("fsdp", "dp")
    return jax.shard_map(
        functools.partial(body, shard_count, image_count),
        mesh=mesh,
        in_specs=(
            P(images, None, None),
            P(images),
            P(images),
            P(images, None),
            P(images, None),
            P(images, None, None),
            P("fsdp", None),
            P(None, "fsdp"),
            P("fsdp", None),
            P("fsdp"),
            P("fsdp", None),
            P("fsdp"),
            P("fsdp", None),
            P("fsdp"),
            P("fsdp", None),
            P("fsdp"),
            P(None, "fsdp"),
        ),
        out_specs=(
            P(images, None, None),
            P(images, None, None),
            P("fsdp", None),
            P(None, "fsdp"),
            P("fsdp", None),
            P("fsdp"),
            P("fsdp", None),
            P("fsdp"),
            P("fsdp", None),
            P("fsdp"),
            P("fsdp", None),
            P("fsdp"),
            P(None, "fsdp"),
        ),
        check_vma=False,
    )
```

```python
import functools
import math

import jax
import jax.numpy as jnp
from jax import lax
from jax.experimental import pallas as pl
from jax.experimental.pallas import tpu as pltpu
from jax.sharding import PartitionSpec as P

LOG2E = 1.4426950408889634
ROWS_NT = (((1,), (1,)), ((), ()))
ROWS_NN = (((1,), (0,)), ((), ()))


def matmul(left, right, dims):
    return lax.dot_general(left, right, dims, preferred_element_type=jnp.float32)


def norm_forward(values):
    row_mean = jnp.mean(values, axis=-1, keepdims=True)
    centred = values - row_mean
    inverse = lax.rsqrt(jnp.mean(centred * centred, axis=-1, keepdims=True) + 1e-06)
    return (centred * inverse, inverse)


def norm_backward(gradient, normed, inverse):
    return inverse * (
        gradient
        - jnp.mean(gradient, axis=-1, keepdims=True)
        - normed * jnp.mean(gradient * normed, axis=-1, keepdims=True)
    )


def head_window(head, head_size, width):
    tile = jnp.minimum((head * head_size) // 128, width // 128 - 2)
    base = pl.multiple_of(tile * 128, 128)
    lane = lax.broadcasted_iota(jnp.int32, (1, 256), 1) + (base - head * head_size)
    return base, (lane >= 0) & (lane < head_size)


def as_row(column):
    return jnp.transpose(jnp.broadcast_to(column, (column.shape[0], 128)))[0:1]


def attend_forward_kernel(
    keep_ref, query_ref, key_ref, value_ref, out_ref, lse_ref, *, head_size, width, rows, together
):
    query_ref, key_ref, value_ref = query_ref.at[0], key_ref.at[0], value_ref.at[0]
    scale = head_size**-0.5 * LOG2E
    zero = jnp.zeros((), jnp.bfloat16)
    length = query_ref.shape[0]
    units = []
    for index in range(together):
        head = pl.program_id(0) * together + index
        base, mask = head_window(head, head_size, width)
        window = (slice(None), pl.ds(base, 256))
        units += [(head, base, mask, window, start) for start in range(0, length, rows)]

    def score(unit):
        head, base, mask, window, start = unit
        query = jnp.where(mask, query_ref[pl.ds(start, rows), pl.ds(base, 256)], zero)
        return matmul(query, key_ref[window], ROWS_NT)

    scores = score(units[0])
    for number, unit in enumerate(units):
        later = score(units[number + 1]) if number + 1 < len(units) else None
        head, base, mask, window, start = unit
        block = (pl.ds(start, rows), pl.ds(base, 256))
        top = jnp.max(scores, axis=-1, keepdims=True)
        probs = jnp.exp2((scores - top) * scale)
        total = jnp.sum(probs, axis=-1, keepdims=True)
        mixed = matmul(probs.astype(jnp.bfloat16), value_ref[window], ROWS_NN)
        mixed = (mixed * (keep_ref[head].astype(jnp.float32) / total)).astype(jnp.bfloat16)
        out_ref[block] = jnp.where(mask, mixed, out_ref[block])
        lse_ref[pl.ds(head, 1), pl.ds(start, rows)] = as_row(top * scale + jnp.log2(total))
        scores = later


def attend_backward_kernel(
    keep_ref,
    query_ref,
    key_ref,
    value_ref,
    out_ref,
    grad_ref,
    lse_ref,
    grads_ref,
    *,
    head_size,
    width,
    rows,
    together,
):
    query_ref, key_ref, value_ref = query_ref.at[0], key_ref.at[0], value_ref.at[0]
    dquery_ref, dkey_ref, dvalue_ref = grads_ref.at[0], grads_ref.at[1], grads_ref.at[2]
    scale = head_size**-0.5
    zero = jnp.zeros((), jnp.bfloat16)
    length = query_ref.shape[0]
    units = []
    for index in range(together):
        head = pl.program_id(0) * together + index
        base, mask = head_window(head, head_size, width)
        window = (slice(None), pl.ds(base, 256))
        units += [(head, base, mask, window, start) for start in range(0, length, rows)]

    def products(unit):
        head, base, mask, window, start = unit
        block = (pl.ds(start, rows), pl.ds(base, 256))
        query = jnp.where(mask, query_ref[block], zero)
        grad = jnp.where(mask & (keep_ref[head] > 0), grad_ref[block], zero)
        scores = matmul(key_ref[window], query, ROWS_NT)
        return query, grad, scores, matmul(value_ref[window], grad, ROWS_NT)

    ready = products(units[0])
    for number, unit in enumerate(units):
        later = products(units[number + 1]) if number + 1 < len(units) else None
        head, base, mask, window, start = unit
        query, grad, scores, prob_grad = ready
        block = (pl.ds(start, rows), pl.ds(base, 256))
        if start == 0:
            keys_across = jnp.transpose(key_ref[window])
            key_grad = jnp.zeros((length, 256), jnp.float32)
            value_grad = jnp.zeros((length, 256), jnp.float32)
        row_dot = as_row(
            jnp.sum(
                grad.astype(jnp.float32) * out_ref[block].astype(jnp.float32), axis=-1, keepdims=True
            )
        )
        lse = lse_ref[pl.ds(head, 1), pl.ds(start, rows)]
        probs = jnp.exp2(scores * (scale * LOG2E) - lse)
        score_grad = (probs * (prob_grad - row_dot)).astype(jnp.bfloat16)
        value_grad = value_grad + matmul(probs.astype(jnp.bfloat16), grad, ROWS_NN)
        key_grad = key_grad + matmul(score_grad, query, ROWS_NN)
        query_grad = jnp.transpose(matmul(keys_across, score_grad, ROWS_NN)) * scale
        dquery_ref[block] = jnp.where(mask, query_grad.astype(jnp.bfloat16), dquery_ref[block])
        if start + rows == length:
            dkey_ref[window] = jnp.where(
                mask, (key_grad * scale).astype(jnp.bfloat16), dkey_ref[window]
            )
            dvalue_ref[window] = jnp.where(mask, value_grad.astype(jnp.bfloat16), dvalue_ref[window])
        ready = later


def whole(shape):
    return pl.BlockSpec(shape, lambda *_: (0,) * len(shape), pipeline_mode=pl.Buffered(1))


def one_of(index, length, width):
    return pl.BlockSpec(
        (1, length, width), lambda head: (index, 0, 0), pipeline_mode=pl.Buffered(1)
    )


def attend_forward(qkv, keep, rows=512, together=2):
    _, length, width = qkv.shape
    heads = keep.shape[0]
    cells = heads * length * length
    return pl.pallas_call(
        functools.partial(
            attend_forward_kernel,
            head_size=width // heads,
            width=width,
            rows=min(rows, length),
            together=together,
        ),
        grid=(heads // together,),
        in_specs=[pl.BlockSpec(memory_space=pltpu.SMEM)]
        + [one_of(i, length, width) for i in range(3)],
        out_specs=[
            pl.BlockSpec((length, width), lambda head: (0, 0)),
            pl.BlockSpec((heads, length), lambda head: (0, 0)),
        ],
        out_shape=[
            jax.ShapeDtypeStruct((length, width), jnp.bfloat16),
            jax.ShapeDtypeStruct((heads, length), jnp.float32),
        ],
        compiler_params=pltpu.CompilerParams(vmem_limit_bytes=48 << 20),
        cost_estimate=pl.CostEstimate(
            flops=cells * 1024, transcendentals=cells, bytes_accessed=length * width * 8
        ),
        name="attend_forward",
    )(keep, qkv, qkv, qkv)


def attend_backward(qkv, out, grad, lse, keep, rows=256, together=2):
    _, length, width = qkv.shape
    heads = keep.shape[0]
    cells = heads * length * length
    return pl.pallas_call(
        functools.partial(
            attend_backward_kernel,
            head_size=width // heads,
            width=width,
            rows=min(rows, length),
            together=together,
        ),
        grid=(heads // together,),
        in_specs=[pl.BlockSpec(memory_space=pltpu.SMEM)]
        + [one_of(i, length, width) for i in range(3)]
        + [whole((length, width))] * 2
        + [whole((heads, length))],
        out_specs=pl.BlockSpec((3, length, width), lambda head: (0, 0, 0)),
        out_shape=jax.ShapeDtypeStruct((3, length, width), jnp.bfloat16),
        compiler_params=pltpu.CompilerParams(vmem_limit_bytes=56 << 20),
        cost_estimate=pl.CostEstimate(
            flops=cells * 2560, transcendentals=cells, bytes_accessed=length * width * 16
        ),
        name="attend_backward",
    )(keep, qkv, qkv, qkv, out, grad, lse)


ROWS_TN = (((0,), (0,)), ((), ()))
ANY = pl.BlockSpec(memory_space=pl.ANY)


class Blocks(list):
    def __init__(self, arrays, order):
        super().__init__(arrays)
        self.order = order

    def block(self, r, x_r, z_r):
        y_r, core_r = r // 2, r % 2
        first_r, second_r = (x_r, y_r) if self.order == "xy" else (y_r, x_r)
        return self[2 * core_r + second_r].at[first_r, z_r]


def square_copies(place, sets, r, target, sem):
    part = jnp.bitwise_xor(place[2], r)
    if len(sets[0]) == 1:
        return [pltpu.make_async_copy(sets[0][0].at[part], target, sem)]
    copies, column = [], 0
    for refs in sets:
        rows, columns = refs[0].shape[2:]
        for x_r in range(2):
            for z_r in range(4):
                shard = (place[0] + z_r) % 4 * 2 + (place[1] + x_r) % 2
                block = (pl.ds(pl.multiple_of(shard * rows, 16), rows), pl.ds(column, columns))
                source = refs.block(r, x_r, z_r)
                copies.append(pltpu.make_async_copy(source, target.at[block], sem))
        column += columns
    return copies


def strip_copies(place, refs, chunk, target, sem):
    if len(refs) == 1:
        return [pltpu.make_async_copy(refs[0].at[chunk], target, sem)]
    rows = refs[0].shape[2]
    copies = []
    for core_r in range(2):
        for y in range(2):
            part = 2 * y + (place[2] + core_r) % 2
            for x in range(2):
                start = pl.multiple_of(x * (4 * rows) + part * rows, 16)
                source = refs[core_r].at[2 * chunk + x, y]
                copies.append(pltpu.make_async_copy(source, target.at[pl.ds(start, rows)], sem))
    return copies


def square_stores(place, outs, r, source, sem):
    part = jnp.bitwise_xor(place[2], r)
    if len(outs) == 1:
        return [pltpu.make_async_copy(source, outs[0].at[part], sem)]
    copies, column = [], 0
    for pair in range(0, len(outs), 2):
        out = outs[pair + r % 2]
        out = out if len(out.shape) == 4 else out.at[r // 2]
        rows, columns = out.shape[2:]
        for shard in range(8):
            x_r, z_r = (place[1] + shard % 2) % 2, (shard // 2 + 4 - place[0]) % 4
            block = source.at[pl.ds(shard * rows, rows), pl.ds(column, columns)]
            copies.append(pltpu.make_async_copy(block, out.at[x_r, z_r], sem))
        column += columns
    return copies


def strip_stores(place, outs, chunk, source, sem):
    if len(outs) == 1:
        return [pltpu.make_async_copy(source, outs[0].at[chunk], sem)]
    rows = outs[0].shape[3]
    z_r = (chunk + 4 - place[0]) % 4
    copies = []
    for r in range(4):
        part = jnp.bitwise_xor(place[2], r)
        for x in range(2):
            block = source.at[pl.ds(pl.multiple_of(x * (4 * rows) + part * rows, 16), rows)]
            x_r = (place[1] + x) % 2
            copies.append(pltpu.make_async_copy(block, outs[r % 2].at[r // 2, x_r, z_r], sem))
    return copies


def in_sets(refs, sets):
    refs, found = list(refs), []
    for entry in sets:
        found.append(Blocks(refs[: len(entry)], entry.order))
        refs = refs[len(entry) :]
    return found


def flat(sets):
    return [array for entry in sets for array in entry]


def start_all(copies):
    for copy in copies:
        copy.start()


def wait_all(copies):
    for copy in copies:
        copy.wait()


def for_each(step, action):
    for r in range(4):

        @pl.when(step == r)
        def _(r=r):
            action(r)


def fetch_squares(place, sets, step, count, held, sems):
    def at(step, action):
        slot = step % 2

        @pl.when(step < count)
        def _():
            for_each(
                jnp.bitwise_xor(place[2], step),
                lambda r: action(square_copies(place, sets, r, held.at[slot], sems.at[slot])),
            )

    @pl.when(step == 0)
    def _():
        at(step, start_all)

    at(step + 1, start_all)
    at(step, wait_all)


def tiles(length, rows=256):
    return [pl.ds(start, min(rows, length)) for start in range(0, length, min(rows, length))]


def prepare_kernel(
    tokens_ref, cotangent_ref, parts_ref, mod_ref, across_ref, grad_ref, sum_ref, rows_ref
):
    width = tokens_ref.shape[1]

    @pl.when(pl.program_id(0) == 0)
    def _():
        for row in range(parts_ref.shape[1] // width):
            part = parts_ref[:, row * width : (row + 1) * width]
            rows_ref[row : row + 1] = jnp.sum(part, axis=0, keepdims=True)
        sum_ref[...] = jnp.zeros_like(sum_ref)

    normed, _ = norm_forward(tokens_ref[...].astype(jnp.float32))
    mod = normed * (1.0 + row_of(rows_ref, SCALE_ATTN)) + row_of(rows_ref, SHIFT_ATTN)
    mod_ref[...] = mod.astype(jnp.bfloat16)
    across_ref[...] = jnp.transpose(mod).astype(jnp.bfloat16)
    grad = (cotangent_ref[...].astype(jnp.float32) * row_of(rows_ref, GATE_MLP)).astype(jnp.bfloat16)
    grad_ref[...] = grad
    sum_ref[0:1] += jnp.sum(grad.astype(jnp.float32), axis=0, keepdims=True)


def prepare(tokens, cotangent, parts, tile=256):
    length, width = tokens.shape
    tile = min(tile, length)
    by_rows = pl.BlockSpec((tile, width), lambda step: (step, 0))
    fixed = pl.BlockSpec((8, width), lambda step: (0, 0))
    table = (16, width)
    return pl.pallas_call(
        prepare_kernel,
        grid=(length // tile,),
        in_specs=[by_rows, by_rows, pl.BlockSpec(parts.shape, lambda step: (0, 0))],
        out_specs=[
            by_rows,
            pl.BlockSpec((width, tile), lambda step: (0, step)),
            by_rows,
            fixed,
            pl.BlockSpec(table, lambda step: (0, 0)),
        ],
        out_shape=[
            jax.ShapeDtypeStruct((length, width), jnp.bfloat16),
            jax.ShapeDtypeStruct((width, length), jnp.bfloat16),
            jax.ShapeDtypeStruct((length, width), jnp.bfloat16),
            jax.ShapeDtypeStruct((8, width), jnp.float32),
            jax.ShapeDtypeStruct(table, jnp.float32),
        ],
        compiler_params=vmem_params(),
        cost_estimate=cost(20 * length * width, 10 * length * width),
        name="prepare",
    )(tokens, cotangent, parts)


def project_kernel(place, mod_ref, rows_ref, *rest, sets):
    *refs, out_ref, held, sems = rest
    step = pl.program_id(0)
    fetch_squares(place, in_sets(refs, sets), step, 3, held, sems)
    weight = held.at[step % 2]
    bias = rows_ref[pl.ds(QUERY_BIAS + step // 2, 1)] * (step != 1).astype(jnp.float32)
    for tile in tiles(mod_ref.shape[0]):
        out_ref[0, tile] = (matmul(mod_ref[tile], weight[...], ROWS_NN) + bias).astype(jnp.bfloat16)


def vmem_params(mebibytes=56):
    return pltpu.CompilerParams(
        vmem_limit_bytes=mebibytes << 20, dimension_semantics=("arbitrary",)
    )


def cost(flops, moved):
    return pl.CostEstimate(flops=1, transcendentals=0, bytes_accessed=1)


def project(place, mod, rows, squares):
    length, width = mod.shape
    return pl.pallas_call(
        functools.partial(project_kernel, sets=squares),
        grid_spec=pltpu.PrefetchScalarGridSpec(
            num_scalar_prefetch=1,
            grid=(3,),
            in_specs=[
                pl.BlockSpec((length, width), lambda step, place: (0, 0)),
                pl.BlockSpec(rows.shape, lambda step, place: (0, 0)),
            ]
            + [ANY] * len(flat(squares)),
            out_specs=pl.BlockSpec(
                (1, length, width), lambda step, place: (step, 0, 0)
            ),
            scratch_shapes=[
                pltpu.VMEM((2, width, width), jnp.bfloat16),
                pltpu.SemaphoreType.DMA((2,)),
            ],
        ),
        out_shape=jax.ShapeDtypeStruct((3, length, width), jnp.bfloat16),
        compiler_params=vmem_params(),
        cost_estimate=cost(6 * length * width * width, 14 * length * width),
        name="project",
    )(place, mod, rows, *flat(squares))


def fetch_part(place, sets, wanted, target, sem):
    part = jnp.bitwise_xor(place[2], wanted)
    for_each(part, lambda r: start_all(square_copies(place, sets, r, target, sem)))
    for_each(part, lambda r: wait_all(square_copies(place, sets, r, target, sem)))


def row_of(rows_ref, index):
    return rows_ref[index : index + 1]


SHIFT_ATTN, SCALE_ATTN, GATE_ATTN, SHIFT_MLP, SCALE_MLP, GATE_MLP = range(6)
QUERY_BIAS, VALUE_BIAS, OUT_BIAS, UP_BIAS, DOWN_BIAS = 6, 7, 8, 9, 13


def after_attention_kernel(place, low_ref, tokens_ref, rows_ref, *rest, sets):
    *refs, branch_ref, middle_ref, mod_ref, across_ref, weight, sem = rest

    @pl.when(pl.program_id(0) == 0)
    def _():
        fetch_part(place, in_sets(refs, sets), 3, weight, sem)

    branch = matmul(low_ref[...], weight[...], ROWS_NN) + row_of(rows_ref, OUT_BIAS)
    middle = tokens_ref[...].astype(jnp.float32) + row_of(rows_ref, GATE_ATTN) * branch
    normed, _ = norm_forward(middle)
    mod = normed * (1.0 + row_of(rows_ref, SCALE_MLP)) + row_of(rows_ref, SHIFT_MLP)
    branch_ref[...] = branch
    middle_ref[...] = middle
    mod_ref[...] = mod.astype(jnp.bfloat16)
    across_ref[...] = jnp.transpose(mod).astype(jnp.bfloat16)


def after_attention(place, low, tokens, rows, squares, tile=256):
    length, width = low.shape
    tile = min(tile, length)
    by_rows = pl.BlockSpec((tile, width), lambda step, place: (step, 0))
    return pl.pallas_call(
        functools.partial(after_attention_kernel, sets=squares),
        grid_spec=pltpu.PrefetchScalarGridSpec(
            num_scalar_prefetch=1,
            grid=(length // tile,),
            in_specs=[by_rows, by_rows, pl.BlockSpec(rows.shape, lambda step, place: (0, 0))]
            + [ANY] * len(flat(squares)),
            out_specs=[by_rows] * 3 + [pl.BlockSpec((width, tile), lambda step, place: (0, step))],
            scratch_shapes=[pltpu.VMEM((width, width), jnp.bfloat16), pltpu.SemaphoreType.DMA],
        ),
        out_shape=[
            jax.ShapeDtypeStruct((length, width), jnp.float32),
            jax.ShapeDtypeStruct((length, width), jnp.float32),
            jax.ShapeDtypeStruct((length, width), jnp.bfloat16),
            jax.ShapeDtypeStruct((width, length), jnp.bfloat16),
        ],
        compiler_params=vmem_params(),
        cost_estimate=cost(2 * length * width * width, 18 * length * width),
        name="after_attention",
    )(place, low, tokens, rows, *flat(squares))


ROOT = 0.7978845608028654


def gelu_and_slope(values):
    square = values * values
    bend = jnp.tanh(values * (ROOT + (ROOT * 0.044715) * square))
    half = 0.5 + 0.5 * bend
    slope = half + (0.5 * values) * (1.0 - bend * bend) * (ROOT + (3 * 0.044715 * ROOT) * square)
    return values * half, slope


def mlp_kernel(place, rows_ref, keep_ref, *rest, ups, downs):
    inputs, rest = rest[:3], rest[3:]
    count = len(flat(ups)) + downs
    refs, rest = rest[:count], rest[count:]
    up_sets, down_refs = in_sets(refs, ups), refs[-downs:]
    branch_out, dmod_out, dbias_ref, *stores = rest[:-12]
    mod_ref, across_ref, grad_ref, branch_ref, dmod_ref, act, dpre, up_all, down_all = rest[-12:-3]
    in_sems, out_sem, sum_sem = rest[-3:]
    up_stores, down_stores = stores[: len(stores) // 2], stores[len(stores) // 2 :]
    length, width = mod_ref.shape

    def chunk_of(r):
        return jnp.bitwise_xor(place[2], r)

    first = place[2] % 2

    def spot(r):
        start = pl.multiple_of(jnp.bitwise_xor(first, r % 2) * width, 128)
        return pl.ds(start, width)

    halves = ((0, 1), (2, 3))
    loads = [
        [pltpu.make_async_copy(inputs[0], mod_ref, in_sems.at[0])],
        [pltpu.make_async_copy(inputs[2], grad_ref, in_sems.at[1])],
        [],
        [],
        [pltpu.make_async_copy(inputs[1], across_ref, in_sems.at[4])],
    ]
    for index, pair in enumerate(halves):
        for r in pair:
            target = up_all.at[index, :, spot(r)]
            loads[2 * index] += square_copies(place, up_sets, r, target, in_sems.at[2 * index])
            target = down_all.at[index, spot(r)]
            loads[2 * index + 1] += strip_copies(
                place, down_refs, chunk_of(r), target, in_sems.at[2 * index + 1]
            )
    for index in (0, 1, 4, 2, 3):
        start_all(loads[index])
    rows = min(512, length)
    columns = 768 if 2 * width % 768 == 0 else width
    leaving = []
    for index, pair in enumerate(halves):
        up, down = up_all.at[index], down_all.at[index]
        low_chunk = chunk_of(pair[0]) // 2 * 2

        def row_pair(ref, at):
            return jnp.concatenate([ref[pl.ds(at, 1)], ref[pl.ds(at + 1, 1)]], axis=1)

        bias = row_pair(rows_ref, UP_BIAS + low_chunk)
        keep = row_pair(keep_ref, low_chunk)
        wait_all(loads[2 * index])
        wait_all(loads[2 * index + 1])

        def row_tile(number, total):
            tile = pl.ds(pl.multiple_of(number * rows, rows), rows)
            sums = []
            for column in range(0, 2 * width, columns):
                part = slice(column, column + columns)
                gelu, slope = gelu_and_slope(
                    matmul(mod_ref[tile], up[:, part], ROWS_NN) + bias[:, part]
                )
                act[tile, part] = (gelu * keep[:, part]).astype(jnp.bfloat16)
                back = matmul(grad_ref[tile], down[part], ROWS_NT)
                low = (slope * keep[:, part] * back).astype(jnp.bfloat16)
                dpre[tile, part] = low
                sums.append(jnp.sum(low.astype(jnp.float32), axis=0, keepdims=True))
            branch = matmul(act[tile], down[...], ROWS_NN)
            dmod = matmul(dpre[tile], up[...], ROWS_NT)
            if index:
                branch_ref[tile] += branch
                dmod_ref[tile] += dmod
            else:
                branch_ref[tile] = branch
                dmod_ref[tile] = dmod
            return total + jnp.concatenate(sums, axis=1)

        total = lax.fori_loop(0, length // rows, row_tile, jnp.zeros_like(bias))
        dbias_ref[pl.ds(low_chunk, 1)] = total[:, :width]
        dbias_ref[pl.ds(low_chunk + 1, 1)] = total[:, width:]
        if index == 1:
            copies = [
                pltpu.make_async_copy(branch_ref, branch_out, sum_sem),
                pltpu.make_async_copy(dmod_ref, dmod_out, sum_sem),
            ]
            start_all(copies)
            leaving += copies
        else:
            wait_all(loads[4])

        for r in pair:
            up[:, spot(r)] = matmul(across_ref[...], dpre[:, spot(r)], ROWS_NN).astype(jnp.bfloat16)
            copies = square_stores(place, up_stores, r, up.at[:, spot(r)], out_sem)
            start_all(copies)
            leaving += copies
        for r in pair:
            down[spot(r)] = matmul(act[:, spot(r)], grad_ref[...], ROWS_TN).astype(jnp.bfloat16)
            copies = strip_stores(place, down_stores, chunk_of(r), down.at[spot(r)], out_sem)
            start_all(copies)
            leaving += copies
    wait_all(leaving)


def gradient_shapes(paired, rows, columns):
    if paired:
        return [
            jax.ShapeDtypeStruct((2, 2, 4, rows, count), jnp.bfloat16)
            for count in columns
            for _ in range(2)
        ]
    return [jax.ShapeDtypeStruct((4, sum(columns), sum(columns)), jnp.bfloat16)]


def mlp(place, mod, across, grad, rows, keep, ups, downs, block_rows):
    length, width = mod.shape
    stores = gradient_shapes(len(downs) > 1, block_rows, [width])
    count = len(flat(ups)) + len(downs)
    table = pl.BlockSpec((4, width), lambda step, place: (0, 0))
    return pl.pallas_call(
        functools.partial(mlp_kernel, ups=ups, downs=len(downs)),
        grid_spec=pltpu.PrefetchScalarGridSpec(
            num_scalar_prefetch=1,
            grid=(1,),
            in_specs=[pl.BlockSpec(rows.shape, lambda step, place: (0, 0)), table]
            + [ANY] * (3 + count),
            out_specs=[ANY, ANY, table] + [ANY] * (2 * len(stores)),
            scratch_shapes=[
                pltpu.VMEM((length, width), jnp.bfloat16),
                pltpu.VMEM((width, length), jnp.bfloat16),
                pltpu.VMEM((length, width), jnp.bfloat16),
                pltpu.VMEM((length, width), jnp.float32),
                pltpu.VMEM((length, width), jnp.float32),
                pltpu.VMEM((length, 2 * width), jnp.bfloat16),
                pltpu.VMEM((length, 2 * width), jnp.bfloat16),
                pltpu.VMEM((2, width, 2 * width), jnp.bfloat16),
                pltpu.VMEM((2, 2 * width, width), jnp.bfloat16),
                pltpu.SemaphoreType.DMA((5,)),
                pltpu.SemaphoreType.DMA,
                pltpu.SemaphoreType.DMA,
            ],
        ),
        out_shape=[jax.ShapeDtypeStruct((length, width), jnp.float32)] * 2
        + [jax.ShapeDtypeStruct((4, width), jnp.float32)]
        + stores
        + stores,
        compiler_params=vmem_params(62),
        cost_estimate=cost(48 * length * width * width, 32 * width * width),
        name="mlp",
    )(place, rows, keep, mod, across, grad, *flat(ups), *downs)


def after_mlp_kernel(
    place, dmod_ref, middle_ref, cotangent_ref, rows_ref, *rest, sets
):
    *refs, dmiddle_ref, dbranch_ref, dlow_ref, sums_ref, weight, sem = rest

    @pl.when(pl.program_id(0) == 0)
    def _():
        fetch_part(place, in_sets(refs, sets), 3, weight, sem)
        sums_ref[...] = jnp.zeros_like(sums_ref)

    normed, inverse = norm_forward(middle_ref[...])
    dmod = dmod_ref[...]
    dmiddle = cotangent_ref[...].astype(jnp.float32) + norm_backward(
        dmod * (1.0 + row_of(rows_ref, SCALE_MLP)), normed, inverse
    )
    dmiddle_ref[...] = dmiddle
    low = (dmiddle * row_of(rows_ref, GATE_ATTN)).astype(jnp.bfloat16)
    dbranch_ref[...] = low
    dlow_ref[...] = matmul(low, weight[...], ROWS_NT).astype(jnp.bfloat16)
    sums_ref[0:1] += jnp.sum(dmod * normed, axis=0, keepdims=True)
    sums_ref[1:2] += jnp.sum(dmod, axis=0, keepdims=True)
    sums_ref[2:3] += jnp.sum(low.astype(jnp.float32), axis=0, keepdims=True)


def after_mlp(place, dmod, middle, cotangent, rows, squares, tile=256):
    length, width = middle.shape
    tile = min(tile, length)
    by_rows = pl.BlockSpec((tile, width), lambda step, place: (step, 0))
    fixed = lambda shape: pl.BlockSpec(shape, lambda step, place: (0, 0))
    return pl.pallas_call(
        functools.partial(after_mlp_kernel, sets=squares),
        grid_spec=pltpu.PrefetchScalarGridSpec(
            num_scalar_prefetch=1,
            grid=(length // tile,),
            in_specs=[by_rows] * 3 + [fixed(rows.shape)] + [ANY] * len(flat(squares)),
            out_specs=[by_rows] * 3 + [fixed((8, width))],
            scratch_shapes=[pltpu.VMEM((width, width), jnp.bfloat16), pltpu.SemaphoreType.DMA],
        ),
        out_shape=[
            jax.ShapeDtypeStruct((length, width), jnp.float32),
            jax.ShapeDtypeStruct((length, width), jnp.bfloat16),
            jax.ShapeDtypeStruct((length, width), jnp.bfloat16),
            jax.ShapeDtypeStruct((8, width), jnp.float32),
        ],
        compiler_params=vmem_params(),
        cost_estimate=cost(2 * length * width * width, 20 * length * width),
        name="after_mlp",
    )(place, dmod, middle, cotangent, rows, *flat(squares))


def finish_kernel(
    mlp_ref, middle_ref, branch_ref, dmiddle_ref, cotangent_ref, rows_ref, out_ref, sums_ref
):
    @pl.when(pl.program_id(0) == 0)
    def _():
        sums_ref[...] = jnp.zeros_like(sums_ref)

    mlp_branch = mlp_ref[...] + row_of(rows_ref, DOWN_BIAS)
    out_ref[...] = (middle_ref[...] + row_of(rows_ref, GATE_MLP) * mlp_branch).astype(jnp.bfloat16)
    grad = cotangent_ref[...].astype(jnp.float32) * mlp_branch
    sums_ref[0:1] += jnp.sum(grad, axis=0, keepdims=True)
    sums_ref[1:2] += jnp.sum(dmiddle_ref[...] * branch_ref[...], axis=0, keepdims=True)


def finish(branch_mlp, middle, branch, dmiddle, cotangent, rows, tile=256):
    length, width = middle.shape
    tile = min(tile, length)
    by_rows = pl.BlockSpec((tile, width), lambda step: (step, 0))
    return pl.pallas_call(
        finish_kernel,
        grid=(length // tile,),
        in_specs=[by_rows] * 5 + [pl.BlockSpec(rows.shape, lambda step: (0, 0))],
        out_specs=[by_rows, pl.BlockSpec((8, width), lambda step: (0, 0))],
        out_shape=[
            jax.ShapeDtypeStruct((length, width), jnp.bfloat16),
            jax.ShapeDtypeStruct((8, width), jnp.float32),
        ],
        compiler_params=vmem_params(),
        cost_estimate=cost(8 * length * width, 20 * length * width),
        name="finish",
    )(branch_mlp, middle, branch, dmiddle, cotangent, rows)


def square_grads_kernel(place, across_ref, grads_ref, low_ref, dbranch_ref, *rest):
    *stores, staged, sems = rest
    step = pl.program_id(0)
    part = jnp.bitwise_xor(place[2], step)

    def leave(r):
        return square_stores(place, stores, r, staged.at[r % 2], sems.at[r % 2])

    for_each(step - 2, lambda r: wait_all(leave(r)))

    @pl.when(part < 3)
    def _():
        staged[step % 2] = matmul(across_ref[...], grads_ref[0], ROWS_NN).astype(jnp.bfloat16)

    @pl.when(part == 3)
    def _():
        staged[step % 2] = matmul(low_ref[...], dbranch_ref[...], ROWS_TN).astype(jnp.bfloat16)

    for_each(step, lambda r: start_all(leave(r)))

    @pl.when(step == 3)
    def _():
        wait_all(leave(2))
        wait_all(leave(3))


def square_grads(place, across, grads, low, dbranch, paired, block_rows, columns):
    width, length = across.shape
    stores = gradient_shapes(paired, block_rows, columns)
    held = pl.BlockSpec((length, width), lambda step, place: (0, 0), pipeline_mode=pl.Buffered(1))
    return pl.pallas_call(
        square_grads_kernel,
        grid_spec=pltpu.PrefetchScalarGridSpec(
            num_scalar_prefetch=1,
            grid=(4,),
            in_specs=[
                pl.BlockSpec((width, length), lambda step, place: (0, 0), pipeline_mode=pl.Buffered(1)),
                pl.BlockSpec(
                    (1, length, width),
                    lambda step, place: (jnp.minimum(jnp.bitwise_xor(place[2], step), 2), 0, 0),
                ),
                held,
                held,
            ],
            out_specs=[ANY] * len(stores),
            scratch_shapes=[
                pltpu.VMEM((2, width, width), jnp.bfloat16),
                pltpu.SemaphoreType.DMA((2,)),
            ],
        ),
        out_shape=stores,
        compiler_params=vmem_params(),
        cost_estimate=cost(8 * length * width * width, 20 * length * width),
        name="square_grads",
    )(place, across, grads, low, dbranch)


def tokens_back_kernel(place, grads_ref, tokens_ref, dmiddle_ref, rows_ref, *rest, sets):
    *refs, out_ref, sums_ref, dmod, held, sems = rest
    step = pl.program_id(0)
    fetch_squares(place, in_sets(refs, sets), step, 3, held, sems)
    length = tokens_ref.shape[0]

    @pl.when(step == 0)
    def _():
        dmod[...] = jnp.zeros_like(dmod)

    for tile in tiles(length):
        dmod[tile] += matmul(grads_ref[0, tile], held[step % 2], ROWS_NT)
    total = jnp.sum(grads_ref[0].astype(jnp.float32), axis=0, keepdims=True)
    sums_ref[pl.ds(2 + step, 1)] = total

    @pl.when(step == 2)
    def _():
        shift = jnp.zeros((1, dmod.shape[1]), jnp.float32)
        scale = shift
        for tile in tiles(length):
            back = dmod[tile]
            normed, inverse = norm_forward(tokens_ref[tile].astype(jnp.float32))
            scale = scale + jnp.sum(back * normed, axis=0, keepdims=True)
            shift = shift + jnp.sum(back, axis=0, keepdims=True)
            back = norm_backward(back * (1.0 + row_of(rows_ref, SCALE_ATTN)), normed, inverse)
            out_ref[tile] = (dmiddle_ref[tile] + back).astype(jnp.bfloat16)
        sums_ref[0:1] = shift
        sums_ref[1:2] = scale


def tokens_back(place, grads, tokens, dmiddle, rows, squares):
    length, width = tokens.shape
    held = pl.BlockSpec((length, width), lambda step, place: (0, 0), pipeline_mode=pl.Buffered(1))
    return pl.pallas_call(
        functools.partial(tokens_back_kernel, sets=squares),
        grid_spec=pltpu.PrefetchScalarGridSpec(
            num_scalar_prefetch=1,
            grid=(3,),
            in_specs=[
                pl.BlockSpec(
                    (1, length, width),
                    lambda step, place: (step, 0, 0),
                ),
                held,
                held,
                pl.BlockSpec(rows.shape, lambda step, place: (0, 0)),
            ]
            + [ANY] * len(flat(squares)),
            out_specs=[
                pl.BlockSpec((length, width), lambda step, place: (0, 0)),
                pl.BlockSpec((8, width), lambda step, place: (0, 0)),
            ],
            scratch_shapes=[
                pltpu.VMEM((length, width), jnp.float32),
                pltpu.VMEM((2, width, width), jnp.bfloat16),
                pltpu.SemaphoreType.DMA((2,)),
            ],
        ),
        out_shape=[
            jax.ShapeDtypeStruct((length, width), jnp.bfloat16),
            jax.ShapeDtypeStruct((8, width), jnp.float32),
        ],
        compiler_params=vmem_params(),
        cost_estimate=cost(6 * length * width * width, 20 * length * width),
        name="tokens_back",
    )(place, grads, tokens, dmiddle, rows, *flat(squares))


def gather_rows(rows, axis, size):
    place = lax.axis_index(axis)
    step = 1
    while step < size:
        other = lax.ppermute(rows, axis, [(i, i ^ step) for i in range(size)])
        high = (place // step) % 2 == 1
        rows = jnp.concatenate([jnp.where(high, other, rows), jnp.where(high, rows, other)], axis=0)
        step *= 2
    return rows


def swap(value, axis, size, step):
    return lax.ppermute(value, axis, [(i, i ^ step) for i in range(size)])


def both(value, axis, size, step, dim):
    other = swap(value, axis, size, step)
    first = lax.axis_index(axis) // step % 2 == 0
    return jnp.stack([jnp.where(first, value, other), jnp.where(first, other, value)], axis=dim)


def barrier(values):
    return lax.optimization_barrier(values)


def after(value, *others):
    return barrier((value, others))[0]


def add(*terms):
    return sum(term.astype(jnp.float32) for term in terms).astype(jnp.bfloat16)


class Pairwise:
    def __init__(self, shards, group):
        self.shards, self.group = shards, group

    def partner(self, value, kind):
        if kind == "x":
            return swap(value, "fsdp", self.shards, 1)
        return swap(value, "dp", self.group, 2 if kind == "y" else 1)

    def corners(self, block):
        size = self.shards * self.group
        x, y, far = [
            lax.ppermute(block, ("fsdp", "dp"), [(i, i ^ step) for i in range(size)])
            for step in (self.group, 2, self.group + 2)
        ]
        return jnp.stack([jnp.stack([block, x]), jnp.stack([y, far])])

    def ahead(self, value, count):
        pairs = [((target // 2 + count) % 4 * 2 + target % 2, target) for target in range(8)]
        return lax.ppermute(value, "fsdp", pairs)

    def along_z(self, block):
        return jnp.stack([block] + [self.ahead(block, count) for count in (1, 2, 3)])

    def pair(self, block, kind):
        return jnp.stack([block, self.partner(block, kind)])

    def first_sum(self, kept, other, kind):
        dim = 0 if kind == "y" else 1
        stay, go = [
            [lax.index_in_dim(half, i, dim, keepdims=False) for half in (kept, other)] for i in (0, 1)
        ]
        return add(*go), stay

    def second_sum(self, stay, back):
        return add(stay[0][1], stay[1][1], back[1]), add(stay[0][0], stay[1][0], back[0])

    def send_z(self, mine):
        return [self.ahead(mine[count], 4 - count) for count in (1, 2, 3)]

    def to_group(self, part):
        parts = both(both(part, "dp", self.group, 2, 0), "dp", self.group, 1, 1)
        return parts.reshape(4, *part.shape)


def reduce_all(grad):
    shard = lax.psum_scatter(grad, "fsdp", scatter_dimension=0, tiled=True)
    return lax.psum(shard, "dp").astype(jnp.float32)


def reduce_columns(parts):
    _, rows, width = parts.shape
    shard = reduce_all(parts.swapaxes(0, 1).reshape(rows, 4 * width))
    return [shard[:, i * width : (i + 1) * width] for i in range(4)]


def conditioning(times, labels, table, shard, width):
    class_count, columns = table.shape
    half = width // 2
    column = shard * columns + jnp.arange(columns, dtype=jnp.int32)
    frequency = jnp.exp(-math.log(10000.0) * (column % half).astype(jnp.float32) / half)
    angles = times.astype(jnp.float32)[:, None] * frequency[None, :]
    embed = jnp.where(column[None, :] < half, jnp.cos(angles), jnp.sin(angles))
    picked = labels[:, None] == jnp.arange(class_count, dtype=jnp.int32)[None, :]
    return embed + jnp.dot(
        picked.astype(jnp.bfloat16), table, preferred_element_type=jnp.float32
    )


def own_part(values, shard, size):
    return lax.dynamic_slice_in_dim(values, shard * size, size, axis=values.ndim - 1)


def body(
    shard_count,
    image_count,
    tokens,
    timesteps,
    labels,
    head_keep,
    chan_keep,
    cotangent,
    qkv_weight,
    qv_bias,
    out_weight,
    out_bias,
    up_weight,
    up_bias,
    down_weight,
    down_bias,
    ada_weight,
    ada_bias,
    class_table,
):
    _, length, width = tokens.shape
    hidden = chan_keep.shape[1]
    class_count = class_table.shape[0]
    columns = width // shard_count
    group_count = image_count // shard_count
    shard = lax.axis_index("fsdp")
    member = lax.axis_index("dp")
    bf16, f32 = jnp.bfloat16, jnp.float32

    place = jnp.stack([shard // 2, shard % 2, member]).astype(jnp.int32)
    paired = shard_count == 8 and group_count == 4 and columns % 16 == 0
    net = Pairwise(shard_count, group_count)
    splits = [width // 2 // 128 * 128]
    splits.append(width - splits[0])
    four = jnp.concatenate([qkv_weight, out_weight], axis=1)

    fact = jnp.stack([timesteps[0], labels[0]])
    if paired:
        near = net.pair(fact, "x")
        mine = lax.dynamic_slice_in_dim(four, member * width, width, axis=1)
        near = net.along_z(near)
        square = net.along_z(mine)
        facts = jnp.where(place[1] == 0, near, near[:, ::-1])
        facts = lax.dynamic_slice_in_dim(
            jnp.concatenate([facts, facts]), (4 - place[0]) % 4, 4, axis=0
        ).reshape(8, 2)
    else:
        facts = gather_rows(fact[None], "fsdp", shard_count)
    group_act = jax.nn.silu(
        conditioning(facts[:, 0], facts[:, 1], class_table, shard, width)
    ).astype(bf16)
    partial = jnp.dot(group_act, ada_weight, preferred_element_type=f32)

    def own_columns(values):
        values = values.astype(f32)
        full = jnp.zeros((values.shape[0] * shard_count,), f32)
        return lax.dynamic_update_slice_in_dim(full, values, shard * values.shape[0], axis=0)

    biases = jnp.concatenate(
        [own_columns(values) for values in (qv_bias[0], qv_bias[1], out_bias, up_bias, down_bias)]
    )
    sent = jnp.concatenate(
        [
            partial + own_columns(ada_bias),
            jnp.broadcast_to(biases, (shard_count, biases.shape[0])),
        ],
        axis=1,
    )
    if paired:
        square, sent, near = barrier((square, sent, near))
        parts = lax.all_to_all(sent, "fsdp", 0, 0, tiled=True)
        all_facts = near.swapaxes(0, 1)
        first = net.pair(square[:, :, : splits[0]], "x")
        second = net.pair(square[:, :, splits[0] :], "y")
        mine = lax.dynamic_slice_in_dim(up_weight, member * width, width, axis=1)
        down_mine = down_weight.reshape(2, 2, columns, width)
        down_mine = jnp.where(member % 2 == 0, down_mine[:, 0], down_mine[:, 1])
        mine, down_mine, first, second, parts = barrier((mine, down_mine, first, second, parts))
        first_y, second_x = net.partner(first, "y"), net.partner(second, "x")
        up = net.along_z(mine)
        prepared = prepare(tokens[0], cotangent[0], parts)
        first, second, first_y, second_x, up, prepared = barrier(
            (first, second, first_y, second_x, up, prepared)
        )
        squares = [
            Blocks([first, first_y, net.partner(first, "c"), net.partner(first_y, "c")], "xy"),
            Blocks([second, second_x, net.partner(second, "c"), net.partner(second_x, "c")], "yx"),
        ]
    else:
        parts = lax.all_to_all(sent, "fsdp", 0, 0, tiled=True)
        all_facts = gather_rows(facts, "dp", group_count)
        found = lax.all_gather(four, "fsdp", axis=0, tiled=True)
        squares = [Blocks([found.reshape(width, 4, width).swapaxes(0, 1)], "xy")]
        prepared = prepare(tokens[0], cotangent[0], parts)
    mod_one, mod_across, branch_grad, down_bias_g, rows = prepared
    if paired:
        up_x, up_y = net.partner(up, "x"), net.partner(up, "y")
        down = lax.all_gather(after(down_mine, squares[0][3]), "fsdp", axis=0)
    qkv = project(place, mod_one, rows, squares)
    if paired:
        qkv, up_x, up_y, all_facts = barrier((qkv, up_x, up_y, all_facts))
        up = jnp.stack([up, up_x])
        up_xy, up_c = net.partner(up_x, "y"), net.partner(up, "c")
        all_facts = net.pair(all_facts, "c").swapaxes(0, 1)
    attn_low, lse = attend_forward(qkv, head_keep[0])
    if paired:
        attn_low, up, up_xy, up_c, all_facts = barrier((attn_low, up, up_xy, up_c, all_facts))
        all_facts = net.pair(all_facts, "y").reshape(image_count, 2)
        up_y = jnp.stack([up_y, up_xy])
        up_y_c = net.partner(up_y, "c")
    attn_branch, middle, mod_two, mod_two_across = after_attention(
        place, attn_low, tokens[0], rows, squares
    )
    if paired:
        mod_two, down, up_y_c, all_facts = barrier((mod_two, down, up_y_c, all_facts))
        ups = [Blocks([up, up_y, up_c, up_y_c], "xy")]
        downs = [down, net.partner(down, "c")]
    else:
        found = lax.all_gather(up_weight, "fsdp", axis=0, tiled=True)
        ups = [Blocks([found.reshape(width, 4, width).swapaxes(0, 1)], "xy")]
        found = lax.all_gather(down_weight, "fsdp", axis=0, tiled=True)
        downs = [found.reshape(4, width, width)]
    branch_mlp, mod_two_grad, up_bias_g, *stores = mlp(
        place,
        mod_two,
        mod_two_across,
        branch_grad,
        rows,
        chan_keep.astype(f32).reshape(4, width),
        ups,
        downs,
        columns,
    )
    up_bias_g = up_bias_g.reshape(-1)
    if paired:
        up_kept, up_sent, down_kept, down_sent = stores
        up_other, down_other = net.partner(up_sent, "c"), net.partner(down_sent, "c")
    else:
        up_shard = jnp.concatenate(reduce_columns(stores[0]), axis=1)
        down_shard = reduce_all(stores[1].reshape(hidden, width))
    middle_grad, dbranch, low_grad, sums = after_mlp(
        place, mod_two_grad, middle, cotangent[0], rows, squares
    )
    scale_mlp_grad, shift_mlp_grad, out_bias_g = sums[0], sums[1], sums[2]
    if paired:
        low_grad, up_other, down_other = barrier((low_grad, up_other, down_other))
        up_go, up_stay = net.first_sum(up_kept, up_other, "x")
        down_go, down_stay = net.first_sum(down_kept, down_other, "y")
        low_grad, up_go, down_go = barrier((low_grad, up_go, down_go))
        up_back, down_back = net.partner(up_go, "x"), net.partner(down_go, "y")
    grads = attend_backward(qkv, attn_low, low_grad, lse, head_keep[0])
    if paired:
        grads, up_back, down_back = barrier((grads, up_back, down_back))
        up_go, up_stay = net.second_sum(up_stay, up_back)
        down_go, down_stay = net.second_sum(down_stay, down_back)
        grads, up_go, down_go = barrier((grads, up_go, down_go))
        up_back, down_back = net.partner(up_go, "y"), net.partner(down_go, "x")
    stores = square_grads(
        place, mod_across, grads, attn_low, dbranch, paired, columns, splits
    )
    block_out, gate_sums = finish(branch_mlp, middle, attn_branch, middle_grad, cotangent[0], rows)
    if paired:
        stores, grads, up_back, down_back, block_out, gate_sums = barrier(
            (stores, grads, up_back, down_back, block_out, gate_sums)
        )
        others = [net.partner(sent, "c") for sent in stores[1::2]]
        others = barrier(others)
        goes, stays = zip(
            *[net.first_sum(stores[2 * i], others[i], kind) for i, kind in enumerate("yx")]
        )
        up_mine = add(up_stay, up_back)
        goes, up_mine, grads = barrier((goes, up_mine, grads))
        backs = [net.partner(go, kind) for go, kind in zip(goes, "yx")]
        up_terms = net.send_z(up_mine)
    def small_grads(all_rows):
        cond = conditioning(all_facts[:, 0], all_facts[:, 1], class_table, shard, width)
        cond_act, silu_pull = jax.vjp(jax.nn.silu, cond)
        ada_grad = all_rows[:, : 6 * width]
        ada_weight_g = jnp.einsum(
            "sd,se->de", cond_act.astype(bf16), ada_grad, preferred_element_type=f32
        )
        cond_act_grad = jnp.einsum("se,de->sd", ada_grad, ada_weight, preferred_element_type=f32)
        cond_grad = silu_pull(cond_act_grad)[0]
        picked = all_facts[:, 1][:, None] == jnp.arange(class_count, dtype=jnp.int32)[None, :]
        table_g = jnp.einsum(
            "sc,sd->cd", picked.astype(f32), cond_grad, precision=lax.Precision.HIGHEST
        )
        sums = jnp.sum(all_rows.astype(f32), axis=0)
        ada_bias_g = own_part(sums[: 6 * width], shard, ada_bias.shape[0])
        qv_bias_g = own_part(sums[6 * width : 8 * width].reshape(2, width), shard, columns)
        out_bias_own = own_part(sums[8 * width : 9 * width], shard, columns)
        up_bias_own = own_part(sums[9 * width : 9 * width + hidden], shard, up_bias.shape[0])
        down_bias_own = own_part(sums[9 * width + hidden :], shard, columns)
        return qv_bias_g, out_bias_own, up_bias_own, down_bias_own, ada_weight_g, ada_bias_g, table_g

    tokens_grad, sums = tokens_back(place, grads, tokens[0], middle_grad, rows, squares)
    if paired:
        tokens_grad, sums, backs, up_terms = barrier((tokens_grad, sums, backs, up_terms))
    gate_mlp_grad, gate_attn_grad = gate_sums[0], gate_sums[1]
    row = jnp.concatenate(
        [
            sums[0],
            sums[1],
            gate_attn_grad,
            shift_mlp_grad,
            scale_mlp_grad,
            gate_mlp_grad,
            sums[2],
            sums[4],
            out_bias_g,
            up_bias_g,
            down_bias_g[0],
        ]
    ).astype(bf16)[None]
    if paired:
        down_mine = add(down_stay, down_back)
        goes, stays = zip(*[net.second_sum(stay, back) for stay, back in zip(stays, backs)])
        goes, row, down_mine = barrier((goes, row, down_mine))
        row = net.along_z(row)
        backs = [net.partner(go, kind) for go, kind in zip(goes, "xy")]
        down_terms = net.send_z(down_mine)
        backs, down_terms, row = barrier((backs, down_terms, row))
        mine = jnp.concatenate([add(stay, back) for stay, back in zip(stays, backs)], axis=2)
        part = jnp.stack([add(up_mine[0], *up_terms), add(down_mine[0], *down_terms)])
        mine, part, row = barrier((mine, part, row))
        terms = net.send_z(mine)
        row = net.corners(net.pair(row, "c"))
        mlp_parts = both(part, "dp", group_count, 2, 0)
        terms, row, mlp_parts = barrier((terms, row, mlp_parts))
        small = small_grads(row.reshape(image_count, -1))
        mlp_parts = both(mlp_parts, "dp", group_count, 1, 1).reshape(4, *part.shape)
        parts = net.to_group(add(mine[0], *terms)).astype(f32)
        up_shard = jnp.concatenate([mlp_parts[i, 0] for i in range(4)], axis=1).astype(f32)
        down_shard = mlp_parts[:, 1].reshape(down_weight.shape).astype(f32)
        query_g, key_g, value_g, out_shard = parts
    else:
        query_g, key_g, value_g, out_shard = reduce_columns(stores[0])
        all_rows = gather_rows(gather_rows(row, "fsdp", shard_count), "dp", group_count)
        small = small_grads(all_rows)
    qkv_shard = jnp.concatenate([query_g, key_g, value_g], axis=1)
    (
        qv_bias_g,
        out_bias_g,
        up_bias_g,
        down_bias_g,
        ada_weight_g,
        ada_bias_g,
        table_g,
    ) = small
    return (
        block_out[None],
        tokens_grad[None],
        qkv_shard,
        qv_bias_g,
        out_shard,
        out_bias_g,
        up_shard,
        up_bias_g,
        down_shard,
        down_bias_g,
        ada_weight_g,
        ada_bias_g,
        table_g,
    )


def solution(mesh):
    shard_count = mesh.shape["fsdp"]
    image_count = shard_count * mesh.shape["dp"]
    images = ("fsdp", "dp")
    return jax.shard_map(
        functools.partial(body, shard_count, image_count),
        mesh=mesh,
        in_specs=(
            P(images, None, None),
            P(images),
            P(images),
            P(images, None),
            P(images, None),
            P(images, None, None),
            P("fsdp", None),
            P(None, "fsdp"),
            P("fsdp", None),
            P("fsdp"),
            P("fsdp", None),
            P("fsdp"),
            P("fsdp", None),
            P("fsdp"),
            P("fsdp", None),
            P("fsdp"),
            P(None, "fsdp"),
        ),
        out_specs=(
            P(images, None, None),
            P(images, None, None),
            P("fsdp", None),
            P(None, "fsdp"),
            P("fsdp", None),
            P("fsdp"),
            P("fsdp", None),
            P("fsdp"),
            P("fsdp", None),
            P("fsdp"),
            P("fsdp", None),
            P("fsdp"),
            P(None, "fsdp"),
        ),
        check_vma=False,
    )
```

```python
import functools
import math

import jax
import jax.numpy as jnp
from jax import lax
from jax.experimental import pallas as pl
from jax.experimental.pallas import tpu as pltpu
from jax.sharding import PartitionSpec as P

LOG2E = 1.4426950408889634
ROWS_NT = (((1,), (1,)), ((), ()))
ROWS_NN = (((1,), (0,)), ((), ()))


def matmul(left, right, dims):
    return lax.dot_general(left, right, dims, preferred_element_type=jnp.float32)


def norm_forward(values):
    row_mean = jnp.mean(values, axis=-1, keepdims=True)
    centred = values - row_mean
    inverse = lax.rsqrt(jnp.mean(centred * centred, axis=-1, keepdims=True) + 1e-06)
    return (centred * inverse, inverse)


def norm_backward(gradient, normed, inverse):
    return inverse * (
        gradient
        - jnp.mean(gradient, axis=-1, keepdims=True)
        - normed * jnp.mean(gradient * normed, axis=-1, keepdims=True)
    )


def head_window(head, head_size, width):
    tile = jnp.minimum((head * head_size) // 128, width // 128 - 2)
    base = pl.multiple_of(tile * 128, 128)
    lane = lax.broadcasted_iota(jnp.int32, (1, 256), 1) + (base - head * head_size)
    return base, (lane >= 0) & (lane < head_size)


def as_row(column):
    return jnp.transpose(jnp.broadcast_to(column, (column.shape[0], 128)))[0:1]


def attend_forward_kernel(
    keep_ref, query_ref, key_ref, value_ref, out_ref, lse_ref, *, head_size, width, rows, together
):
    query_ref, key_ref, value_ref = query_ref.at[0], key_ref.at[0], value_ref.at[0]
    scale = head_size**-0.5 * LOG2E
    zero = jnp.zeros((), jnp.bfloat16)
    length = query_ref.shape[0]
    units = []
    for index in range(together):
        head = pl.program_id(0) * together + index
        base, mask = head_window(head, head_size, width)
        window = (slice(None), pl.ds(base, 256))
        units += [(head, base, mask, window, start) for start in range(0, length, rows)]

    def score(unit):
        head, base, mask, window, start = unit
        query = jnp.where(mask, query_ref[pl.ds(start, rows), pl.ds(base, 256)], zero)
        return matmul(query, key_ref[window], ROWS_NT)

    scores = score(units[0])
    for number, unit in enumerate(units):
        later = score(units[number + 1]) if number + 1 < len(units) else None
        head, base, mask, window, start = unit
        block = (pl.ds(start, rows), pl.ds(base, 256))
        top = jnp.max(scores, axis=-1, keepdims=True)
        probs = jnp.exp2((scores - top) * scale)
        total = jnp.sum(probs, axis=-1, keepdims=True)
        mixed = matmul(probs.astype(jnp.bfloat16), value_ref[window], ROWS_NN)
        mixed = (mixed * (keep_ref[head].astype(jnp.float32) / total)).astype(jnp.bfloat16)
        out_ref[block] = jnp.where(mask, mixed, out_ref[block])
        lse_ref[pl.ds(head, 1), pl.ds(start, rows)] = as_row(top * scale + jnp.log2(total))
        scores = later


def attend_backward_kernel(
    keep_ref,
    query_ref,
    key_ref,
    value_ref,
    out_ref,
    grad_ref,
    lse_ref,
    grads_ref,
    *,
    head_size,
    width,
    rows,
    together,
):
    query_ref, key_ref, value_ref = query_ref.at[0], key_ref.at[0], value_ref.at[0]
    dquery_ref, dkey_ref, dvalue_ref = grads_ref.at[0], grads_ref.at[1], grads_ref.at[2]
    scale = head_size**-0.5
    zero = jnp.zeros((), jnp.bfloat16)
    length = query_ref.shape[0]
    units = []
    for index in range(together):
        head = pl.program_id(0) * together + index
        base, mask = head_window(head, head_size, width)
        window = (slice(None), pl.ds(base, 256))
        units += [(head, base, mask, window, start) for start in range(0, length, rows)]

    def products(unit):
        head, base, mask, window, start = unit
        block = (pl.ds(start, rows), pl.ds(base, 256))
        query = jnp.where(mask, query_ref[block], zero)
        grad = jnp.where(mask & (keep_ref[head] > 0), grad_ref[block], zero)
        scores = matmul(key_ref[window], query, ROWS_NT)
        return query, grad, scores, matmul(value_ref[window], grad, ROWS_NT)

    ready = products(units[0])
    for number, unit in enumerate(units):
        later = products(units[number + 1]) if number + 1 < len(units) else None
        head, base, mask, window, start = unit
        query, grad, scores, prob_grad = ready
        block = (pl.ds(start, rows), pl.ds(base, 256))
        if start == 0:
            keys_across = jnp.transpose(key_ref[window])
            key_grad = jnp.zeros((length, 256), jnp.float32)
            value_grad = jnp.zeros((length, 256), jnp.float32)
        row_dot = as_row(
            jnp.sum(
                grad.astype(jnp.float32) * out_ref[block].astype(jnp.float32), axis=-1, keepdims=True
            )
        )
        lse = lse_ref[pl.ds(head, 1), pl.ds(start, rows)]
        probs = jnp.exp2(scores * (scale * LOG2E) - lse)
        score_grad = (probs * (prob_grad - row_dot)).astype(jnp.bfloat16)
        value_grad = value_grad + matmul(probs.astype(jnp.bfloat16), grad, ROWS_NN)
        key_grad = key_grad + matmul(score_grad, query, ROWS_NN)
        query_grad = jnp.transpose(matmul(keys_across, score_grad, ROWS_NN)) * scale
        dquery_ref[block] = jnp.where(mask, query_grad.astype(jnp.bfloat16), dquery_ref[block])
        if start + rows == length:
            dkey_ref[window] = jnp.where(
                mask, (key_grad * scale).astype(jnp.bfloat16), dkey_ref[window]
            )
            dvalue_ref[window] = jnp.where(mask, value_grad.astype(jnp.bfloat16), dvalue_ref[window])
        ready = later


def whole(shape):
    return pl.BlockSpec(shape, lambda *_: (0,) * len(shape), pipeline_mode=pl.Buffered(1))


def one_of(index, length, width):
    return pl.BlockSpec(
        (1, length, width), lambda head: (index, 0, 0), pipeline_mode=pl.Buffered(1)
    )


def attend_forward(qkv, keep, rows=512, together=2):
    _, length, width = qkv.shape
    heads = keep.shape[0]
    cells = heads * length * length
    return pl.pallas_call(
        functools.partial(
            attend_forward_kernel,
            head_size=width // heads,
            width=width,
            rows=min(rows, length),
            together=together,
        ),
        grid=(heads // together,),
        in_specs=[pl.BlockSpec(memory_space=pltpu.SMEM)]
        + [one_of(i, length, width) for i in range(3)],
        out_specs=[
            pl.BlockSpec((length, width), lambda head: (0, 0)),
            pl.BlockSpec((heads, length), lambda head: (0, 0)),
        ],
        out_shape=[
            jax.ShapeDtypeStruct((length, width), jnp.bfloat16),
            jax.ShapeDtypeStruct((heads, length), jnp.float32),
        ],
        compiler_params=pltpu.CompilerParams(vmem_limit_bytes=48 << 20),
        cost_estimate=pl.CostEstimate(
            flops=cells * 1024, transcendentals=cells, bytes_accessed=length * width * 8
        ),
        name="attend_forward",
    )(keep, qkv, qkv, qkv)


def attend_backward(qkv, out, grad, lse, keep, rows=256, together=2):
    _, length, width = qkv.shape
    heads = keep.shape[0]
    cells = heads * length * length
    return pl.pallas_call(
        functools.partial(
            attend_backward_kernel,
            head_size=width // heads,
            width=width,
            rows=min(rows, length),
            together=together,
        ),
        grid=(heads // together,),
        in_specs=[pl.BlockSpec(memory_space=pltpu.SMEM)]
        + [one_of(i, length, width) for i in range(3)]
        + [whole((length, width))] * 2
        + [whole((heads, length))],
        out_specs=pl.BlockSpec((3, length, width), lambda head: (0, 0, 0)),
        out_shape=jax.ShapeDtypeStruct((3, length, width), jnp.bfloat16),
        compiler_params=pltpu.CompilerParams(vmem_limit_bytes=56 << 20),
        cost_estimate=pl.CostEstimate(
            flops=cells * 2560, transcendentals=cells, bytes_accessed=length * width * 16
        ),
        name="attend_backward",
    )(keep, qkv, qkv, qkv, out, grad, lse)


ROWS_TN = (((0,), (0,)), ((), ()))
ANY = pl.BlockSpec(memory_space=pl.ANY)


class Blocks(list):
    def __init__(self, arrays, order):
        super().__init__(arrays)
        self.order = order

    def block(self, r, x_r, z_r):
        y_r, core_r = r // 2, r % 2
        first_r, second_r = (x_r, y_r) if self.order == "xy" else (y_r, x_r)
        if len(self) == 8:
            return self[4 * core_r + 2 * second_r + first_r].at[z_r]
        return self[2 * core_r + second_r].at[first_r, z_r]


def square_copies(place, sets, r, target, sem):
    part = jnp.bitwise_xor(place[2], r)
    if len(sets[0]) == 1:
        return [pltpu.make_async_copy(sets[0][0].at[part], target, sem)]
    copies, column = [], 0
    for refs in sets:
        rows, columns = refs[0].shape[-2:]
        for x_r in range(2):
            for z_r in range(4):
                shard = (place[0] + z_r) % 4 * 2 + (place[1] + x_r) % 2
                block = (pl.ds(pl.multiple_of(shard * rows, 16), rows), pl.ds(column, columns))
                source = refs.block(r, x_r, z_r)
                copies.append(pltpu.make_async_copy(source, target.at[block], sem))
        column += columns
    return copies


def strip_copies(place, refs, chunk, target, sem):
    if len(refs) == 1:
        return [pltpu.make_async_copy(refs[0].at[chunk], target, sem)]
    rows = refs[0].shape[2]
    copies = []
    for core_r in range(2):
        for y in range(2):
            part = 2 * y + (place[2] + core_r) % 2
            for x in range(2):
                start = pl.multiple_of(x * (4 * rows) + part * rows, 16)
                source = refs[core_r].at[2 * chunk + x, y]
                copies.append(pltpu.make_async_copy(source, target.at[pl.ds(start, rows)], sem))
    return copies


def square_stores(place, outs, r, source, sem):
    part = jnp.bitwise_xor(place[2], r)
    if len(outs) == 1:
        return [pltpu.make_async_copy(source, outs[0].at[part], sem)]
    copies, column = [], 0
    for pair in range(0, len(outs), 2):
        out = outs[pair + r % 2]
        out = out if len(out.shape) == 4 else out.at[r // 2]
        rows, columns = out.shape[2:]
        for shard in range(8):
            x_r, z_r = (place[1] + shard % 2) % 2, (shard // 2 + 4 - place[0]) % 4
            block = source.at[pl.ds(shard * rows, rows), pl.ds(column, columns)]
            copies.append(pltpu.make_async_copy(block, out.at[x_r, z_r], sem))
        column += columns
    return copies


def strip_stores(place, outs, chunk, source, sem):
    if len(outs) == 1:
        return [pltpu.make_async_copy(source, outs[0].at[chunk], sem)]
    rows = outs[0].shape[3]
    z_r = (chunk + 4 - place[0]) % 4
    copies = []
    for r in range(4):
        part = jnp.bitwise_xor(place[2], r)
        for x in range(2):
            block = source.at[pl.ds(pl.multiple_of(x * (4 * rows) + part * rows, 16), rows)]
            x_r = (place[1] + x) % 2
            copies.append(pltpu.make_async_copy(block, outs[r % 2].at[r // 2, x_r, z_r], sem))
    return copies


def in_sets(refs, sets):
    refs, found = list(refs), []
    for entry in sets:
        found.append(Blocks(refs[: len(entry)], entry.order))
        refs = refs[len(entry) :]
    return found


def flat(sets):
    return [array for entry in sets for array in entry]


def start_all(copies):
    for copy in copies:
        copy.start()


def wait_all(copies):
    for copy in copies:
        copy.wait()


def for_each(step, action):
    for r in range(4):

        @pl.when(step == r)
        def _(r=r):
            action(r)


def fetch_squares(place, sets, step, count, held, sems):
    def at(step, action):
        slot = step % 2

        @pl.when(step < count)
        def _():
            for_each(
                jnp.bitwise_xor(place[2], step),
                lambda r: action(square_copies(place, sets, r, held.at[slot], sems.at[slot])),
            )

    @pl.when(step == 0)
    def _():
        at(step, start_all)

    at(step + 1, start_all)
    at(step, wait_all)


def tiles(length, rows=256):
    return [pl.ds(start, min(rows, length)) for start in range(0, length, min(rows, length))]


def prepare_kernel(
    tokens_ref, cotangent_ref, parts_ref, mod_ref, across_ref, grad_ref, sum_ref, rows_ref
):
    width = tokens_ref.shape[1]

    @pl.when(pl.program_id(0) == 0)
    def _():
        for row in range(parts_ref.shape[1] // width):
            part = parts_ref[:, row * width : (row + 1) * width]
            rows_ref[row : row + 1] = jnp.sum(part, axis=0, keepdims=True)
        sum_ref[...] = jnp.zeros_like(sum_ref)

    normed, _ = norm_forward(tokens_ref[...].astype(jnp.float32))
    mod = normed * (1.0 + row_of(rows_ref, SCALE_ATTN)) + row_of(rows_ref, SHIFT_ATTN)
    mod_ref[...] = mod.astype(jnp.bfloat16)
    across_ref[...] = jnp.transpose(mod).astype(jnp.bfloat16)
    grad = (cotangent_ref[...].astype(jnp.float32) * row_of(rows_ref, GATE_MLP)).astype(jnp.bfloat16)
    grad_ref[...] = grad
    sum_ref[0:1] += jnp.sum(grad.astype(jnp.float32), axis=0, keepdims=True)


def prepare(tokens, cotangent, parts, tile=256):
    length, width = tokens.shape
    tile = min(tile, length)
    by_rows = pl.BlockSpec((tile, width), lambda step: (step, 0))
    fixed = pl.BlockSpec((8, width), lambda step: (0, 0))
    table = (16, width)
    return pl.pallas_call(
        prepare_kernel,
        grid=(length // tile,),
        in_specs=[by_rows, by_rows, pl.BlockSpec(parts.shape, lambda step: (0, 0))],
        out_specs=[
            by_rows,
            pl.BlockSpec((width, tile), lambda step: (0, step)),
            by_rows,
            fixed,
            pl.BlockSpec(table, lambda step: (0, 0)),
        ],
        out_shape=[
            jax.ShapeDtypeStruct((length, width), jnp.bfloat16),
            jax.ShapeDtypeStruct((width, length), jnp.bfloat16),
            jax.ShapeDtypeStruct((length, width), jnp.bfloat16),
            jax.ShapeDtypeStruct((8, width), jnp.float32),
            jax.ShapeDtypeStruct(table, jnp.float32),
        ],
        compiler_params=vmem_params(),
        cost_estimate=cost(20 * length * width, 10 * length * width),
        name="prepare",
    )(tokens, cotangent, parts)


def project_kernel(place, mod_ref, rows_ref, *rest, sets):
    *refs, out_ref, held, sems = rest
    step = pl.program_id(0)
    fetch_squares(place, in_sets(refs, sets), step, 3, held, sems)
    weight = held.at[step % 2]
    bias = rows_ref[pl.ds(QUERY_BIAS + step // 2, 1)] * (step != 1).astype(jnp.float32)
    for tile in tiles(mod_ref.shape[0]):
        out_ref[0, tile] = (matmul(mod_ref[tile], weight[...], ROWS_NN) + bias).astype(jnp.bfloat16)


def vmem_params(mebibytes=56):
    return pltpu.CompilerParams(
        vmem_limit_bytes=mebibytes << 20, dimension_semantics=("arbitrary",)
    )


def cost(flops, moved):
    return pl.CostEstimate(flops=1, transcendentals=0, bytes_accessed=1)


def project(place, mod, rows, squares):
    length, width = mod.shape
    return pl.pallas_call(
        functools.partial(project_kernel, sets=squares),
        grid_spec=pltpu.PrefetchScalarGridSpec(
            num_scalar_prefetch=1,
            grid=(3,),
            in_specs=[
                pl.BlockSpec((length, width), lambda step, place: (0, 0)),
                pl.BlockSpec(rows.shape, lambda step, place: (0, 0)),
            ]
            + [ANY] * len(flat(squares)),
            out_specs=pl.BlockSpec(
                (1, length, width), lambda step, place: (step, 0, 0)
            ),
            scratch_shapes=[
                pltpu.VMEM((2, width, width), jnp.bfloat16),
                pltpu.SemaphoreType.DMA((2,)),
            ],
        ),
        out_shape=jax.ShapeDtypeStruct((3, length, width), jnp.bfloat16),
        compiler_params=vmem_params(),
        cost_estimate=cost(6 * length * width * width, 14 * length * width),
        name="project",
    )(place, mod, rows, *flat(squares))


def fetch_part(place, sets, wanted, target, sem):
    part = jnp.bitwise_xor(place[2], wanted)
    for_each(part, lambda r: start_all(square_copies(place, sets, r, target, sem)))
    for_each(part, lambda r: wait_all(square_copies(place, sets, r, target, sem)))


def row_of(rows_ref, index):
    return rows_ref[index : index + 1]


SHIFT_ATTN, SCALE_ATTN, GATE_ATTN, SHIFT_MLP, SCALE_MLP, GATE_MLP = range(6)
QUERY_BIAS, VALUE_BIAS, OUT_BIAS, UP_BIAS, DOWN_BIAS = 6, 7, 8, 9, 13


def after_attention_kernel(place, low_ref, tokens_ref, rows_ref, *rest, sets):
    *refs, branch_ref, middle_ref, mod_ref, across_ref, weight, sem = rest

    @pl.when(pl.program_id(0) == 0)
    def _():
        fetch_part(place, in_sets(refs, sets), 3, weight, sem)

    branch = matmul(low_ref[...], weight[...], ROWS_NN) + row_of(rows_ref, OUT_BIAS)
    middle = tokens_ref[...].astype(jnp.float32) + row_of(rows_ref, GATE_ATTN) * branch
    normed, _ = norm_forward(middle)
    mod = normed * (1.0 + row_of(rows_ref, SCALE_MLP)) + row_of(rows_ref, SHIFT_MLP)
    branch_ref[...] = branch
    middle_ref[...] = middle
    mod_ref[...] = mod.astype(jnp.bfloat16)
    across_ref[...] = jnp.transpose(mod).astype(jnp.bfloat16)


def after_attention(place, low, tokens, rows, squares, tile=256):
    length, width = low.shape
    tile = min(tile, length)
    by_rows = pl.BlockSpec((tile, width), lambda step, place: (step, 0))
    return pl.pallas_call(
        functools.partial(after_attention_kernel, sets=squares),
        grid_spec=pltpu.PrefetchScalarGridSpec(
            num_scalar_prefetch=1,
            grid=(length // tile,),
            in_specs=[by_rows, by_rows, pl.BlockSpec(rows.shape, lambda step, place: (0, 0))]
            + [ANY] * len(flat(squares)),
            out_specs=[by_rows] * 3 + [pl.BlockSpec((width, tile), lambda step, place: (0, step))],
            scratch_shapes=[pltpu.VMEM((width, width), jnp.bfloat16), pltpu.SemaphoreType.DMA],
        ),
        out_shape=[
            jax.ShapeDtypeStruct((length, width), jnp.float32),
            jax.ShapeDtypeStruct((length, width), jnp.float32),
            jax.ShapeDtypeStruct((length, width), jnp.bfloat16),
            jax.ShapeDtypeStruct((width, length), jnp.bfloat16),
        ],
        compiler_params=vmem_params(),
        cost_estimate=cost(2 * length * width * width, 18 * length * width),
        name="after_attention",
    )(place, low, tokens, rows, *flat(squares))


ROOT = 0.7978845608028654


def gelu_and_slope(values):
    square = values * values
    bend = jnp.tanh(values * (ROOT + (ROOT * 0.044715) * square))
    half = 0.5 + 0.5 * bend
    slope = half + (0.5 * values) * (1.0 - bend * bend) * (ROOT + (3 * 0.044715 * ROOT) * square)
    return values * half, slope


def mlp_kernel(place, rows_ref, keep_ref, *rest, ups, downs):
    inputs, rest = rest[:3], rest[3:]
    count = len(flat(ups)) + downs
    refs, rest = rest[:count], rest[count:]
    up_sets, down_refs = in_sets(refs, ups), refs[-downs:]
    branch_out, dmod_out, dbias_ref, *stores = rest[:-12]
    mod_ref, across_ref, grad_ref, branch_ref, dmod_ref, act, dpre, up_all, down_all = rest[-12:-3]
    in_sems, out_sem, sum_sem = rest[-3:]
    up_stores, down_stores = stores[: len(stores) // 2], stores[len(stores) // 2 :]
    length, width = mod_ref.shape

    def chunk_of(r):
        return jnp.bitwise_xor(place[2], r)

    first = place[2] % 2

    def spot(r):
        start = pl.multiple_of(jnp.bitwise_xor(first, r % 2) * width, 128)
        return pl.ds(start, width)

    halves = ((0, 1), (2, 3))
    loads = [
        [pltpu.make_async_copy(inputs[0], mod_ref, in_sems.at[0])],
        [pltpu.make_async_copy(inputs[2], grad_ref, in_sems.at[1])],
        [],
        [],
        [pltpu.make_async_copy(inputs[1], across_ref, in_sems.at[4])],
    ]
    for index, pair in enumerate(halves):
        for r in pair:
            target = up_all.at[index, :, spot(r)]
            loads[2 * index] += square_copies(place, up_sets, r, target, in_sems.at[2 * index])
            target = down_all.at[index, spot(r)]
            loads[2 * index + 1] += strip_copies(
                place, down_refs, chunk_of(r), target, in_sems.at[2 * index + 1]
            )
    for index in (0, 1, 4, 2, 3):
        start_all(loads[index])
    rows = min(512, length)
    columns = 768 if 2 * width % 768 == 0 else width
    leaving = []
    for index, pair in enumerate(halves):
        up, down = up_all.at[index], down_all.at[index]
        low_chunk = chunk_of(pair[0]) // 2 * 2

        def row_pair(ref, at):
            return jnp.concatenate([ref[pl.ds(at, 1)], ref[pl.ds(at + 1, 1)]], axis=1)

        bias = row_pair(rows_ref, UP_BIAS + low_chunk)
        keep = row_pair(keep_ref, low_chunk)
        wait_all(loads[2 * index])
        wait_all(loads[2 * index + 1])

        def row_tile(number, total):
            tile = pl.ds(pl.multiple_of(number * rows, rows), rows)
            sums = []
            for column in range(0, 2 * width, columns):
                part = slice(column, column + columns)
                gelu, slope = gelu_and_slope(
                    matmul(mod_ref[tile], up[:, part], ROWS_NN) + bias[:, part]
                )
                act[tile, part] = (gelu * keep[:, part]).astype(jnp.bfloat16)
                back = matmul(grad_ref[tile], down[part], ROWS_NT)
                low = (slope * keep[:, part] * back).astype(jnp.bfloat16)
                dpre[tile, part] = low
                sums.append(jnp.sum(low.astype(jnp.float32), axis=0, keepdims=True))
            branch = matmul(act[tile], down[...], ROWS_NN)
            dmod = matmul(dpre[tile], up[...], ROWS_NT)
            if index:
                branch_ref[tile] += branch
                dmod_ref[tile] += dmod
            else:
                branch_ref[tile] = branch
                dmod_ref[tile] = dmod
            return total + jnp.concatenate(sums, axis=1)

        total = lax.fori_loop(0, length // rows, row_tile, jnp.zeros_like(bias))
        dbias_ref[pl.ds(low_chunk, 1)] = total[:, :width]
        dbias_ref[pl.ds(low_chunk + 1, 1)] = total[:, width:]
        if index == 1:
            copies = [
                pltpu.make_async_copy(branch_ref, branch_out, sum_sem),
                pltpu.make_async_copy(dmod_ref, dmod_out, sum_sem),
            ]
            start_all(copies)
            leaving += copies
        else:
            wait_all(loads[4])

        for r in pair:
            up[:, spot(r)] = matmul(across_ref[...], dpre[:, spot(r)], ROWS_NN).astype(jnp.bfloat16)
            copies = square_stores(place, up_stores, r, up.at[:, spot(r)], out_sem)
            start_all(copies)
            leaving += copies
        for r in pair:
            down[spot(r)] = matmul(act[:, spot(r)], grad_ref[...], ROWS_TN).astype(jnp.bfloat16)
            copies = strip_stores(place, down_stores, chunk_of(r), down.at[spot(r)], out_sem)
            start_all(copies)
            leaving += copies
    wait_all(leaving)


def gradient_shapes(paired, rows, columns):
    if paired:
        return [
            jax.ShapeDtypeStruct((2, 2, 4, rows, count), jnp.bfloat16)
            for count in columns
            for _ in range(2)
        ]
    return [jax.ShapeDtypeStruct((4, sum(columns), sum(columns)), jnp.bfloat16)]


def mlp(place, mod, across, grad, rows, keep, ups, downs, block_rows):
    length, width = mod.shape
    stores = gradient_shapes(len(downs) > 1, block_rows, [width])
    count = len(flat(ups)) + len(downs)
    table = pl.BlockSpec((4, width), lambda step, place: (0, 0))
    return pl.pallas_call(
        functools.partial(mlp_kernel, ups=ups, downs=len(downs)),
        grid_spec=pltpu.PrefetchScalarGridSpec(
            num_scalar_prefetch=1,
            grid=(1,),
            in_specs=[pl.BlockSpec(rows.shape, lambda step, place: (0, 0)), table]
            + [ANY] * (3 + count),
            out_specs=[ANY, ANY, table] + [ANY] * (2 * len(stores)),
            scratch_shapes=[
                pltpu.VMEM((length, width), jnp.bfloat16),
                pltpu.VMEM((width, length), jnp.bfloat16),
                pltpu.VMEM((length, width), jnp.bfloat16),
                pltpu.VMEM((length, width), jnp.float32),
                pltpu.VMEM((length, width), jnp.float32),
                pltpu.VMEM((length, 2 * width), jnp.bfloat16),
                pltpu.VMEM((length, 2 * width), jnp.bfloat16),
                pltpu.VMEM((2, width, 2 * width), jnp.bfloat16),
                pltpu.VMEM((2, 2 * width, width), jnp.bfloat16),
                pltpu.SemaphoreType.DMA((5,)),
                pltpu.SemaphoreType.DMA,
                pltpu.SemaphoreType.DMA,
            ],
        ),
        out_shape=[jax.ShapeDtypeStruct((length, width), jnp.float32)] * 2
        + [jax.ShapeDtypeStruct((4, width), jnp.float32)]
        + stores
        + stores,
        compiler_params=vmem_params(62),
        cost_estimate=cost(48 * length * width * width, 32 * width * width),
        name="mlp",
    )(place, rows, keep, mod, across, grad, *flat(ups), *downs)


def after_mlp_kernel(
    place, dmod_ref, middle_ref, cotangent_ref, rows_ref, *rest, sets
):
    *refs, dmiddle_ref, dbranch_ref, dlow_ref, sums_ref, weight, sem = rest

    @pl.when(pl.program_id(0) == 0)
    def _():
        fetch_part(place, in_sets(refs, sets), 3, weight, sem)
        sums_ref[...] = jnp.zeros_like(sums_ref)

    normed, inverse = norm_forward(middle_ref[...])
    dmod = dmod_ref[...]
    dmiddle = cotangent_ref[...].astype(jnp.float32) + norm_backward(
        dmod * (1.0 + row_of(rows_ref, SCALE_MLP)), normed, inverse
    )
    dmiddle_ref[...] = dmiddle
    low = (dmiddle * row_of(rows_ref, GATE_ATTN)).astype(jnp.bfloat16)
    dbranch_ref[...] = low
    dlow_ref[...] = matmul(low, weight[...], ROWS_NT).astype(jnp.bfloat16)
    sums_ref[0:1] += jnp.sum(dmod * normed, axis=0, keepdims=True)
    sums_ref[1:2] += jnp.sum(dmod, axis=0, keepdims=True)
    sums_ref[2:3] += jnp.sum(low.astype(jnp.float32), axis=0, keepdims=True)


def after_mlp(place, dmod, middle, cotangent, rows, squares, tile=256):
    length, width = middle.shape
    tile = min(tile, length)
    by_rows = pl.BlockSpec((tile, width), lambda step, place: (step, 0))
    fixed = lambda shape: pl.BlockSpec(shape, lambda step, place: (0, 0))
    return pl.pallas_call(
        functools.partial(after_mlp_kernel, sets=squares),
        grid_spec=pltpu.PrefetchScalarGridSpec(
            num_scalar_prefetch=1,
            grid=(length // tile,),
            in_specs=[by_rows] * 3 + [fixed(rows.shape)] + [ANY] * len(flat(squares)),
            out_specs=[by_rows] * 3 + [fixed((8, width))],
            scratch_shapes=[pltpu.VMEM((width, width), jnp.bfloat16), pltpu.SemaphoreType.DMA],
        ),
        out_shape=[
            jax.ShapeDtypeStruct((length, width), jnp.float32),
            jax.ShapeDtypeStruct((length, width), jnp.bfloat16),
            jax.ShapeDtypeStruct((length, width), jnp.bfloat16),
            jax.ShapeDtypeStruct((8, width), jnp.float32),
        ],
        compiler_params=vmem_params(),
        cost_estimate=cost(2 * length * width * width, 20 * length * width),
        name="after_mlp",
    )(place, dmod, middle, cotangent, rows, *flat(squares))


def finish_kernel(
    mlp_ref, middle_ref, branch_ref, dmiddle_ref, cotangent_ref, rows_ref, out_ref, sums_ref
):
    @pl.when(pl.program_id(0) == 0)
    def _():
        sums_ref[...] = jnp.zeros_like(sums_ref)

    mlp_branch = mlp_ref[...] + row_of(rows_ref, DOWN_BIAS)
    out_ref[...] = (middle_ref[...] + row_of(rows_ref, GATE_MLP) * mlp_branch).astype(jnp.bfloat16)
    grad = cotangent_ref[...].astype(jnp.float32) * mlp_branch
    sums_ref[0:1] += jnp.sum(grad, axis=0, keepdims=True)
    sums_ref[1:2] += jnp.sum(dmiddle_ref[...] * branch_ref[...], axis=0, keepdims=True)


def finish(branch_mlp, middle, branch, dmiddle, cotangent, rows, tile=256):
    length, width = middle.shape
    tile = min(tile, length)
    by_rows = pl.BlockSpec((tile, width), lambda step: (step, 0))
    return pl.pallas_call(
        finish_kernel,
        grid=(length // tile,),
        in_specs=[by_rows] * 5 + [pl.BlockSpec(rows.shape, lambda step: (0, 0))],
        out_specs=[by_rows, pl.BlockSpec((8, width), lambda step: (0, 0))],
        out_shape=[
            jax.ShapeDtypeStruct((length, width), jnp.bfloat16),
            jax.ShapeDtypeStruct((8, width), jnp.float32),
        ],
        compiler_params=vmem_params(),
        cost_estimate=cost(8 * length * width, 20 * length * width),
        name="finish",
    )(branch_mlp, middle, branch, dmiddle, cotangent, rows)


def square_grads_kernel(place, across_ref, grads_ref, low_ref, dbranch_ref, *rest):
    *stores, staged, sems = rest
    step = pl.program_id(0)
    part = jnp.bitwise_xor(place[2], step)

    def leave(r):
        return square_stores(place, stores, r, staged.at[r % 2], sems.at[r % 2])

    for_each(step - 2, lambda r: wait_all(leave(r)))

    @pl.when(part < 3)
    def _():
        staged[step % 2] = matmul(across_ref[...], grads_ref[0], ROWS_NN).astype(jnp.bfloat16)

    @pl.when(part == 3)
    def _():
        staged[step % 2] = matmul(low_ref[...], dbranch_ref[...], ROWS_TN).astype(jnp.bfloat16)

    for_each(step, lambda r: start_all(leave(r)))

    @pl.when(step == 3)
    def _():
        wait_all(leave(2))
        wait_all(leave(3))


def square_grads(place, across, grads, low, dbranch, paired, block_rows, columns):
    width, length = across.shape
    stores = gradient_shapes(paired, block_rows, columns)
    held = pl.BlockSpec((length, width), lambda step, place: (0, 0), pipeline_mode=pl.Buffered(1))
    return pl.pallas_call(
        square_grads_kernel,
        grid_spec=pltpu.PrefetchScalarGridSpec(
            num_scalar_prefetch=1,
            grid=(4,),
            in_specs=[
                pl.BlockSpec((width, length), lambda step, place: (0, 0), pipeline_mode=pl.Buffered(1)),
                pl.BlockSpec(
                    (1, length, width),
                    lambda step, place: (jnp.minimum(jnp.bitwise_xor(place[2], step), 2), 0, 0),
                ),
                held,
                held,
            ],
            out_specs=[ANY] * len(stores),
            scratch_shapes=[
                pltpu.VMEM((2, width, width), jnp.bfloat16),
                pltpu.SemaphoreType.DMA((2,)),
            ],
        ),
        out_shape=stores,
        compiler_params=vmem_params(),
        cost_estimate=cost(8 * length * width * width, 20 * length * width),
        name="square_grads",
    )(place, across, grads, low, dbranch)


def tokens_back_kernel(place, grads_ref, tokens_ref, dmiddle_ref, rows_ref, *rest, sets):
    *refs, out_ref, sums_ref, dmod, held, sems = rest
    step = pl.program_id(0)
    fetch_squares(place, in_sets(refs, sets), step, 3, held, sems)
    length = tokens_ref.shape[0]

    @pl.when(step == 0)
    def _():
        dmod[...] = jnp.zeros_like(dmod)

    for tile in tiles(length):
        dmod[tile] += matmul(grads_ref[0, tile], held[step % 2], ROWS_NT)
    total = jnp.sum(grads_ref[0].astype(jnp.float32), axis=0, keepdims=True)
    sums_ref[pl.ds(2 + step, 1)] = total

    @pl.when(step == 2)
    def _():
        shift = jnp.zeros((1, dmod.shape[1]), jnp.float32)
        scale = shift
        for tile in tiles(length):
            back = dmod[tile]
            normed, inverse = norm_forward(tokens_ref[tile].astype(jnp.float32))
            scale = scale + jnp.sum(back * normed, axis=0, keepdims=True)
            shift = shift + jnp.sum(back, axis=0, keepdims=True)
            back = norm_backward(back * (1.0 + row_of(rows_ref, SCALE_ATTN)), normed, inverse)
            out_ref[tile] = (dmiddle_ref[tile] + back).astype(jnp.bfloat16)
        sums_ref[0:1] = shift
        sums_ref[1:2] = scale


def tokens_back(place, grads, tokens, dmiddle, rows, squares):
    length, width = tokens.shape
    held = pl.BlockSpec((length, width), lambda step, place: (0, 0), pipeline_mode=pl.Buffered(1))
    return pl.pallas_call(
        functools.partial(tokens_back_kernel, sets=squares),
        grid_spec=pltpu.PrefetchScalarGridSpec(
            num_scalar_prefetch=1,
            grid=(3,),
            in_specs=[
                pl.BlockSpec(
                    (1, length, width),
                    lambda step, place: (step, 0, 0),
                ),
                held,
                held,
                pl.BlockSpec(rows.shape, lambda step, place: (0, 0)),
            ]
            + [ANY] * len(flat(squares)),
            out_specs=[
                pl.BlockSpec((length, width), lambda step, place: (0, 0)),
                pl.BlockSpec((8, width), lambda step, place: (0, 0)),
            ],
            scratch_shapes=[
                pltpu.VMEM((length, width), jnp.float32),
                pltpu.VMEM((2, width, width), jnp.bfloat16),
                pltpu.SemaphoreType.DMA((2,)),
            ],
        ),
        out_shape=[
            jax.ShapeDtypeStruct((length, width), jnp.bfloat16),
            jax.ShapeDtypeStruct((8, width), jnp.float32),
        ],
        compiler_params=vmem_params(),
        cost_estimate=cost(6 * length * width * width, 20 * length * width),
        name="tokens_back",
    )(place, grads, tokens, dmiddle, rows, *flat(squares))


def gather_rows(rows, axis, size):
    place = lax.axis_index(axis)
    step = 1
    while step < size:
        other = lax.ppermute(rows, axis, [(i, i ^ step) for i in range(size)])
        high = (place // step) % 2 == 1
        rows = jnp.concatenate([jnp.where(high, other, rows), jnp.where(high, rows, other)], axis=0)
        step *= 2
    return rows


def swap(value, axis, size, step):
    return lax.ppermute(value, axis, [(i, i ^ step) for i in range(size)])


def both(value, axis, size, step, dim):
    other = swap(value, axis, size, step)
    first = lax.axis_index(axis) // step % 2 == 0
    return jnp.stack([jnp.where(first, value, other), jnp.where(first, other, value)], axis=dim)


def barrier(values):
    return lax.optimization_barrier(values)


def after(value, *others):
    return barrier((value, others))[0]


def add(*terms):
    return sum(term.astype(jnp.float32) for term in terms).astype(jnp.bfloat16)


class Pairwise:
    def __init__(self, shards, group):
        self.shards, self.group = shards, group

    def partner(self, value, kind):
        if kind == "x":
            return swap(value, "fsdp", self.shards, 1)
        return swap(value, "dp", self.group, 2 if kind == "y" else 1)

    def corners(self, block):
        size = self.shards * self.group
        x, y, far = [
            lax.ppermute(block, ("fsdp", "dp"), [(i, i ^ step) for i in range(size)])
            for step in (self.group, 2, self.group + 2)
        ]
        return jnp.stack([jnp.stack([block, x]), jnp.stack([y, far])])

    def ahead(self, value, count):
        pairs = [((target // 2 + count) % 4 * 2 + target % 2, target) for target in range(8)]
        return lax.ppermute(value, "fsdp", pairs)

    def along_z(self, block):
        return jnp.stack([block] + [self.ahead(block, count) for count in (1, 2, 3)])

    def pair(self, block, kind):
        return jnp.stack([block, self.partner(block, kind)])

    def first_sum(self, kept, other, kind):
        dim = 0 if kind == "y" else 1
        stay, go = [
            [lax.index_in_dim(half, i, dim, keepdims=False) for half in (kept, other)] for i in (0, 1)
        ]
        return add(*go), stay

    def second_sum(self, stay, back):
        return add(stay[0][1], stay[1][1], back[1]), add(stay[0][0], stay[1][0], back[0])

    def send_z(self, mine):
        return [self.ahead(mine[count], 4 - count) for count in (1, 2, 3)]

    def to_group(self, part):
        parts = both(both(part, "dp", self.group, 2, 0), "dp", self.group, 1, 1)
        return parts.reshape(4, *part.shape)


def reduce_all(grad):
    shard = lax.psum_scatter(grad, "fsdp", scatter_dimension=0, tiled=True)
    return lax.psum(shard, "dp").astype(jnp.float32)


def reduce_columns(parts):
    _, rows, width = parts.shape
    shard = reduce_all(parts.swapaxes(0, 1).reshape(rows, 4 * width))
    return [shard[:, i * width : (i + 1) * width] for i in range(4)]


def conditioning(times, labels, table, shard, width):
    class_count, columns = table.shape
    half = width // 2
    column = shard * columns + jnp.arange(columns, dtype=jnp.int32)
    frequency = jnp.exp(-math.log(10000.0) * (column % half).astype(jnp.float32) / half)
    angles = times.astype(jnp.float32)[:, None] * frequency[None, :]
    embed = jnp.where(column[None, :] < half, jnp.cos(angles), jnp.sin(angles))
    picked = labels[:, None] == jnp.arange(class_count, dtype=jnp.int32)[None, :]
    return embed + jnp.dot(
        picked.astype(jnp.bfloat16), table, preferred_element_type=jnp.float32
    )


def own_part(values, shard, size):
    return lax.dynamic_slice_in_dim(values, shard * size, size, axis=values.ndim - 1)


def body(
    shard_count,
    image_count,
    tokens,
    timesteps,
    labels,
    head_keep,
    chan_keep,
    cotangent,
    qkv_weight,
    qv_bias,
    out_weight,
    out_bias,
    up_weight,
    up_bias,
    down_weight,
    down_bias,
    ada_weight,
    ada_bias,
    class_table,
):
    _, length, width = tokens.shape
    hidden = chan_keep.shape[1]
    class_count = class_table.shape[0]
    columns = width // shard_count
    group_count = image_count // shard_count
    shard = lax.axis_index("fsdp")
    member = lax.axis_index("dp")
    bf16, f32 = jnp.bfloat16, jnp.float32

    place = jnp.stack([shard // 2, shard % 2, member]).astype(jnp.int32)
    paired = shard_count == 8 and group_count == 4 and columns % 16 == 0
    net = Pairwise(shard_count, group_count)
    splits = [width // 2 // 128 * 128]
    splits.append(width - splits[0])
    four = jnp.concatenate([qkv_weight, out_weight], axis=1)

    fact = jnp.stack([timesteps[0], labels[0]])
    if paired:
        near = net.pair(fact, "x")
        mine = lax.dynamic_slice_in_dim(four, member * width, width, axis=1)
        near = net.along_z(near)
        square = net.along_z(mine)
        facts = jnp.where(place[1] == 0, near, near[:, ::-1])
        facts = lax.dynamic_slice_in_dim(
            jnp.concatenate([facts, facts]), (4 - place[0]) % 4, 4, axis=0
        ).reshape(8, 2)
    else:
        facts = gather_rows(fact[None], "fsdp", shard_count)
    group_act = jax.nn.silu(
        conditioning(facts[:, 0], facts[:, 1], class_table, shard, width)
    ).astype(bf16)
    partial = jnp.dot(group_act, ada_weight, preferred_element_type=f32)

    def own_columns(values):
        values = values.astype(f32)
        full = jnp.zeros((values.shape[0] * shard_count,), f32)
        return lax.dynamic_update_slice_in_dim(full, values, shard * values.shape[0], axis=0)

    biases = jnp.concatenate(
        [own_columns(values) for values in (qv_bias[0], qv_bias[1], out_bias, up_bias, down_bias)]
    )
    sent = jnp.concatenate(
        [
            partial + own_columns(ada_bias),
            jnp.broadcast_to(biases, (shard_count, biases.shape[0])),
        ],
        axis=1,
    )
    if paired:
        square, sent, near = barrier((square, sent, near))
        parts = lax.all_to_all(sent, "fsdp", 0, 0, tiled=True)
        all_facts = near.swapaxes(0, 1)
        first = net.pair(square[:, :, : splits[0]], "x")
        second = net.pair(square[:, :, splits[0] :], "y")
        mine = lax.dynamic_slice_in_dim(up_weight, member * width, width, axis=1)
        down_mine = down_weight.reshape(2, 2, columns, width)
        down_mine = jnp.where(member % 2 == 0, down_mine[:, 0], down_mine[:, 1])
        mine, down_mine, first, second, parts = barrier((mine, down_mine, first, second, parts))
        first_y, second_x = net.partner(first, "y"), net.partner(second, "x")
        up = net.along_z(mine)
        prepared = prepare(tokens[0], cotangent[0], parts)
        first, second, first_y, second_x, up, prepared = barrier(
            (first, second, first_y, second_x, up, prepared)
        )
        squares = [
            Blocks([first, first_y, net.partner(first, "c"), net.partner(first_y, "c")], "xy"),
            Blocks([second, second_x, net.partner(second, "c"), net.partner(second_x, "c")], "yx"),
        ]
    else:
        parts = lax.all_to_all(sent, "fsdp", 0, 0, tiled=True)
        all_facts = gather_rows(facts, "dp", group_count)
        found = lax.all_gather(four, "fsdp", axis=0, tiled=True)
        squares = [Blocks([found.reshape(width, 4, width).swapaxes(0, 1)], "xy")]
        prepared = prepare(tokens[0], cotangent[0], parts)
    mod_one, mod_across, branch_grad, down_bias_g, rows = prepared
    if paired:
        up_x, up_y = net.partner(up, "x"), net.partner(up, "y")
        down = lax.all_gather(after(down_mine, squares[0][3]), "fsdp", axis=0)
    qkv = project(place, mod_one, rows, squares)
    if paired:
        qkv, up_x, up_y, all_facts = barrier((qkv, up_x, up_y, all_facts))
        up_xy, up_c, up_x_c = net.partner(up_x, "y"), net.partner(up, "c"), net.partner(up_x, "c")
        all_facts = net.pair(all_facts, "c").swapaxes(0, 1)
    attn_low, lse = attend_forward(qkv, head_keep[0])
    if paired:
        attn_low, up_y, up_xy, up_c, up_x_c, all_facts = barrier(
            (attn_low, up_y, up_xy, up_c, up_x_c, all_facts)
        )
        all_facts = net.pair(all_facts, "y").reshape(image_count, 2)
        up_y_c, up_xy_c = net.partner(up_y, "c"), net.partner(up_xy, "c")
    attn_branch, middle, mod_two, mod_two_across = after_attention(
        place, attn_low, tokens[0], rows, squares
    )
    if paired:
        mod_two, down, up_y_c, up_xy_c, all_facts = barrier(
            (mod_two, down, up_y_c, up_xy_c, all_facts)
        )
        ups = [Blocks([up, up_x, up_y, up_xy, up_c, up_x_c, up_y_c, up_xy_c], "xy")]
        downs = [down, net.partner(down, "c")]
    else:
        found = lax.all_gather(up_weight, "fsdp", axis=0, tiled=True)
        ups = [Blocks([found.reshape(width, 4, width).swapaxes(0, 1)], "xy")]
        found = lax.all_gather(down_weight, "fsdp", axis=0, tiled=True)
        downs = [found.reshape(4, width, width)]
    branch_mlp, mod_two_grad, up_bias_g, *stores = mlp(
        place,
        mod_two,
        mod_two_across,
        branch_grad,
        rows,
        chan_keep.astype(f32).reshape(4, width),
        ups,
        downs,
        columns,
    )
    up_bias_g = up_bias_g.reshape(-1)
    if paired:
        up_kept, up_sent, down_kept, down_sent = stores
        up_other, down_other = net.partner(up_sent, "c"), net.partner(down_sent, "c")
    else:
        up_shard = jnp.concatenate(reduce_columns(stores[0]), axis=1)
        down_shard = reduce_all(stores[1].reshape(hidden, width))
    middle_grad, dbranch, low_grad, sums = after_mlp(
        place, mod_two_grad, middle, cotangent[0], rows, squares
    )
    scale_mlp_grad, shift_mlp_grad, out_bias_g = sums[0], sums[1], sums[2]
    if paired:
        low_grad, up_other, down_other = barrier((low_grad, up_other, down_other))
        up_go, up_stay = net.first_sum(up_kept, up_other, "x")
        down_go, down_stay = net.first_sum(down_kept, down_other, "y")
        low_grad, up_go, down_go = barrier((low_grad, up_go, down_go))
        up_back, down_back = net.partner(up_go, "x"), net.partner(down_go, "y")
    grads = attend_backward(qkv, attn_low, low_grad, lse, head_keep[0])
    if paired:
        grads, up_back, down_back = barrier((grads, up_back, down_back))
        up_go, up_stay = net.second_sum(up_stay, up_back)
        down_go, down_stay = net.second_sum(down_stay, down_back)
        grads, up_go, down_go = barrier((grads, up_go, down_go))
        up_back, down_back = net.partner(up_go, "y"), net.partner(down_go, "x")
    stores = square_grads(
        place, mod_across, grads, attn_low, dbranch, paired, columns, splits
    )
    block_out, gate_sums = finish(branch_mlp, middle, attn_branch, middle_grad, cotangent[0], rows)
    if paired:
        stores, grads, up_back, down_back, block_out, gate_sums = barrier(
            (stores, grads, up_back, down_back, block_out, gate_sums)
        )
        others = [net.partner(sent, "c") for sent in stores[1::2]]
        others = barrier(others)
        goes, stays = zip(
            *[net.first_sum(stores[2 * i], others[i], kind) for i, kind in enumerate("yx")]
        )
        up_mine = add(up_stay, up_back)
        goes, up_mine, grads = barrier((goes, up_mine, grads))
        backs = [net.partner(go, kind) for go, kind in zip(goes, "yx")]
        up_terms = net.send_z(up_mine)
    def small_grads(all_rows):
        cond = conditioning(all_facts[:, 0], all_facts[:, 1], class_table, shard, width)
        cond_act, silu_pull = jax.vjp(jax.nn.silu, cond)
        ada_grad = all_rows[:, : 6 * width]
        ada_weight_g = jnp.einsum(
            "sd,se->de", cond_act.astype(bf16), ada_grad, preferred_element_type=f32
        )
        cond_act_grad = jnp.einsum("se,de->sd", ada_grad, ada_weight, preferred_element_type=f32)
        cond_grad = silu_pull(cond_act_grad)[0]
        picked = all_facts[:, 1][:, None] == jnp.arange(class_count, dtype=jnp.int32)[None, :]
        table_g = jnp.einsum(
            "sc,sd->cd", picked.astype(f32), cond_grad, precision=lax.Precision.HIGHEST
        )
        sums = jnp.sum(all_rows.astype(f32), axis=0)
        ada_bias_g = own_part(sums[: 6 * width], shard, ada_bias.shape[0])
        qv_bias_g = own_part(sums[6 * width : 8 * width].reshape(2, width), shard, columns)
        out_bias_own = own_part(sums[8 * width : 9 * width], shard, columns)
        up_bias_own = own_part(sums[9 * width : 9 * width + hidden], shard, up_bias.shape[0])
        down_bias_own = own_part(sums[9 * width + hidden :], shard, columns)
        return qv_bias_g, out_bias_own, up_bias_own, down_bias_own, ada_weight_g, ada_bias_g, table_g

    tokens_grad, sums = tokens_back(place, grads, tokens[0], middle_grad, rows, squares)
    if paired:
        tokens_grad, sums, backs, up_terms = barrier((tokens_grad, sums, backs, up_terms))
    gate_mlp_grad, gate_attn_grad = gate_sums[0], gate_sums[1]
    row = jnp.concatenate(
        [
            sums[0],
            sums[1],
            gate_attn_grad,
            shift_mlp_grad,
            scale_mlp_grad,
            gate_mlp_grad,
            sums[2],
            sums[4],
            out_bias_g,
            up_bias_g,
            down_bias_g[0],
        ]
    ).astype(bf16)[None]
    if paired:
        down_mine = add(down_stay, down_back)
        goes, stays = zip(*[net.second_sum(stay, back) for stay, back in zip(stays, backs)])
        goes, row, down_mine = barrier((goes, row, down_mine))
        row = net.along_z(row)
        backs = [net.partner(go, kind) for go, kind in zip(goes, "xy")]
        down_terms = net.send_z(down_mine)
        backs, down_terms, row = barrier((backs, down_terms, row))
        mine = jnp.concatenate([add(stay, back) for stay, back in zip(stays, backs)], axis=2)
        part = jnp.stack([add(up_mine[0], *up_terms), add(down_mine[0], *down_terms)])
        mine, part, row = barrier((mine, part, row))
        terms = net.send_z(mine)
        row = net.corners(net.pair(row, "c"))
        mlp_parts = both(part, "dp", group_count, 2, 0)
        terms, row, mlp_parts = barrier((terms, row, mlp_parts))
        small = small_grads(row.reshape(image_count, -1))
        mlp_parts = both(mlp_parts, "dp", group_count, 1, 1).reshape(4, *part.shape)
        parts = net.to_group(add(mine[0], *terms)).astype(f32)
        up_shard = jnp.concatenate([mlp_parts[i, 0] for i in range(4)], axis=1).astype(f32)
        down_shard = mlp_parts[:, 1].reshape(down_weight.shape).astype(f32)
        query_g, key_g, value_g, out_shard = parts
    else:
        query_g, key_g, value_g, out_shard = reduce_columns(stores[0])
        all_rows = gather_rows(gather_rows(row, "fsdp", shard_count), "dp", group_count)
        small = small_grads(all_rows)
    qkv_shard = jnp.concatenate([query_g, key_g, value_g], axis=1)
    (
        qv_bias_g,
        out_bias_g,
        up_bias_g,
        down_bias_g,
        ada_weight_g,
        ada_bias_g,
        table_g,
    ) = small
    return (
        block_out[None],
        tokens_grad[None],
        qkv_shard,
        qv_bias_g,
        out_shard,
        out_bias_g,
        up_shard,
        up_bias_g,
        down_shard,
        down_bias_g,
        ada_weight_g,
        ada_bias_g,
        table_g,
    )


def solution(mesh):
    shard_count = mesh.shape["fsdp"]
    image_count = shard_count * mesh.shape["dp"]
    images = ("fsdp", "dp")
    return jax.shard_map(
        functools.partial(body, shard_count, image_count),
        mesh=mesh,
        in_specs=(
            P(images, None, None),
            P(images),
            P(images),
            P(images, None),
            P(images, None),
            P(images, None, None),
            P("fsdp", None),
            P(None, "fsdp"),
            P("fsdp", None),
            P("fsdp"),
            P("fsdp", None),
            P("fsdp"),
            P("fsdp", None),
            P("fsdp"),
            P("fsdp", None),
            P("fsdp"),
            P(None, "fsdp"),
        ),
        out_specs=(
            P(images, None, None),
            P(images, None, None),
            P("fsdp", None),
            P(None, "fsdp"),
            P("fsdp", None),
            P("fsdp"),
            P("fsdp", None),
            P("fsdp"),
            P("fsdp", None),
            P("fsdp"),
            P("fsdp", None),
            P("fsdp"),
            P(None, "fsdp"),
        ),
        check_vma=False,
    )
```
